128 devices in a mesh: chan: 32 (over z, x_lo, y), win: 4 (over x_hi, core).
Axes of the slice: x: 4 (x_hi: 2, x_lo: 2; x = x_hi * 2 + x_lo), y: 4, z: 4, core: 2. Of those that a mesh axis runs over, the one named last changes fastest.
Arguments:
- samples: int32 [6144, 8, 6144], P('chan', 'win'), may hold values from -2048 to 2046
- exponents: int32 [6144, 8, 24], P('chan', 'win'), may hold values from 0 to 4
- alive: int32 [6144], P('chan'), may hold values 0 or 1
- offsets: int32 [128], P('chan'), may hold values from 0 to 191
Outputs:
- stacks: float32 [128, 384, 2048], P('chan', 'win')
The draws below stay inside these ranges and needn't reach their ends.
All inputs are finite; a program needn't handle non-finite values. No bound on the sum of `alive` on one device may be relied on, other than what follows from the above.
Results may differ from the reference program's by a relative error of at most 0.0032.
Values may be sent and summed in bfloat16 or wider, within the bound.
No kernel may reach another device: no remote copies, remote signals or barrier semaphores. Data moves between devices by JAX's collectives and lax.ppermute only.
A program may use at most 256 MiB of HBM per device.

```python
import math
import jax
import jax.numpy as jnp
from jax import lax

CH_DEV = 192
SRC_DEV = 4
SEG = 1024
BAND = 192
TW = 6144
NBLK = 24
CHANNELS = 6144
NSRC = 128
WINDOWS = 8


def draw_samples(key, part):
    wave_key = jax.random.fold_in(key, 11)
    noise_key = jax.random.fold_in(key, 12)
    source_wave = jax.random.randint(wave_key, (WINDOWS, TW + CHANNELS), -1024, 1024, dtype=jnp.int32)
    positions = jnp.arange(CHANNELS, dtype=jnp.int32)[:, None] + jnp.arange(TW, dtype=jnp.int32)[None, :]
    moved = jnp.take(source_wave, positions, axis=1)
    noise_part = jax.random.randint(noise_key, (CHANNELS, WINDOWS, TW), -1024, 1024, dtype=jnp.int32)
    return jnp.transpose(moved, (1, 0, 2)) + noise_part


def plant(entries, key, least, top_value):
    spot = [jax.random.randint(jax.random.fold_in(key, axis), (), 0, length) for axis, length in enumerate(entries.shape)]
    main_axis = entries.shape.index(max(entries.shape))
    beside = spot[:main_axis] + [(spot[main_axis] + 1) % entries.shape[main_axis]] + spot[main_axis + 1:]
    return entries.at[tuple(spot)].set(least).at[tuple(beside)].set(top_value)


def setup_inputs(seed: int = 0) -> dict:
    keys = jax.random.split(jax.random.key(seed), 5)
    return {
        "samples": draw_samples(jax.random.fold_in(keys[4], 71), 0),
        "exponents": plant(jax.random.randint(keys[1], (CHANNELS, WINDOWS, NBLK), 0, 5), jax.random.fold_in(keys[1], 1), 0, 4).astype(jnp.int32),
        "alive": plant((jax.random.randint(keys[2], (CHANNELS,), 0, 10) < 9).astype(jnp.int32), jax.random.fold_in(keys[2], 1), 0, 1),
        "offsets": plant(jax.random.randint(keys[3], (NSRC,), 0, CH_DEV), jax.random.fold_in(keys[3], 1), 0, CH_DEV - 1).astype(jnp.int32),
    }


def block_scale(exponents):
    levels = jnp.arange(5, dtype=jnp.int32)
    powers = jnp.exp2(levels.astype(jnp.float32))
    return lax.optimization_barrier(jnp.sum(jnp.where(exponents[..., None] == levels, powers, 0.0), axis=-1))

def normalize(samples, exponents, alive):
    channels, windows, length = samples.shape
    block_count = exponents.shape[2]
    amplitude = samples.astype(jnp.float32).reshape(channels, windows, block_count, length // block_count)
    amplitude = amplitude * block_scale(exponents)[..., None]
    energy = lax.optimization_barrier(jnp.mean(amplitude * amplitude, axis=(2, 3), keepdims=True))
    factor = alive.astype(jnp.float32)[:, None, None, None] * lax.rsqrt(energy + 1e-06)
    return (amplitude * factor).reshape(channels, windows, length).astype(jnp.bfloat16)

def forward_basis(seg_len):
    full_len = 2 * seg_len
    sample_index = jnp.arange(seg_len, dtype=jnp.int32)
    phases = sample_index[:, None] * sample_index[None, :] % full_len
    angles = phases.astype(jnp.float32) * (2.0 * math.pi / full_len)
    return jnp.concatenate([jnp.cos(angles), -jnp.sin(angles)], axis=1).astype(jnp.bfloat16)

def transform(normed, seg_len):
    channels, windows, length = normed.shape
    seg_count = length // seg_len
    segments = normed.reshape(channels * windows * seg_count, seg_len)
    spectra = jnp.dot(segments, forward_basis(seg_len), preferred_element_type=jnp.float32).astype(jnp.bfloat16)
    return spectra.reshape(channels, windows * seg_count, 2 * seg_len)

def inverse_table(seg_len, windows, seg_count):
    full_len = 2 * seg_len
    bin_index = jnp.arange(seg_len, dtype=jnp.int32)
    lag_index = jnp.arange(full_len, dtype=jnp.int32) - full_len // 2
    phases = bin_index[:, None] * lag_index[None, :] % full_len
    angles = phases.astype(jnp.float32) * (2.0 * math.pi / full_len)
    weight = jnp.where(bin_index == 0, 1.0, 2.0).astype(jnp.float32) / float(full_len * windows * seg_count * seg_len)
    return jnp.concatenate([weight[:, None] * jnp.cos(angles), -weight[:, None] * jnp.sin(angles)], axis=0)

def cross_spectra(source, band_rows):
    bin_count = source.shape[1] // 2
    src_re = source[:, :bin_count]
    src_im = source[:, bin_count:]
    band_re = band_rows[..., :bin_count]
    band_im = band_rows[..., bin_count:]
    real_part = lax.optimization_barrier(jnp.sum(src_re * band_re + src_im * band_im, axis=1))
    imag_part = lax.optimization_barrier(jnp.sum(src_re * band_im - src_im * band_re, axis=1))
    return jnp.concatenate([real_part, imag_part], axis=-1)

def reference(samples, exponents, alive, offsets):
    channels, windows, length = samples.shape
    seg_count = length // SEG
    normed = normalize(samples, exponents, alive)
    blocks = normed.reshape(channels // CH_DEV, CH_DEV, windows, length)

    def block_spectra(block):
        return transform(block, SEG)
    spectra = lax.map(block_spectra, blocks).reshape(channels, windows * seg_count, 2 * SEG)
    padded = jnp.pad(spectra, ((BAND, BAND), (0, 0), (0, 0)))
    src_chan = jnp.arange(NSRC, dtype=jnp.int32) // SRC_DEV * CH_DEV + offsets.astype(jnp.int32)
    lag_table = inverse_table(SEG, windows, seg_count)

    def one_source(first_row):
        source = lax.dynamic_index_in_dim(padded, first_row + BAND, 0, keepdims=False).astype(jnp.float32)
        band_rows = lax.dynamic_slice_in_dim(padded, first_row, 2 * BAND, 0).astype(jnp.float32)
        terms = cross_spectra(source, band_rows)
        return jnp.dot(terms, lag_table, precision=lax.Precision.HIGHEST, preferred_element_type=jnp.float32)
    return lax.map(one_source, src_chan)
```

```python
import math

import jax
import jax.numpy as jnp
import numpy as np
from jax import lax
from jax.experimental import pallas as pl
from jax.experimental.pallas import tpu as pltpu
from jax.sharding import PartitionSpec as P

SEG = 1024
BAND = 192
HALF = 96
CHUNKS = 4
BINS = SEG // CHUNKS
WIDTH = 2 * BINS
FOLD = 32
TILE = 32
SUB = 16
LANES = 128


def small_tables():
    u = np.arange(BINS)
    k = CHUNKS * u[None, :] + np.arange(CHUNKS)[:, None]
    step = np.arange(FOLD)

    def waves(stride):
        phase = (stride * step[None, :, None] * k[:, None, :]) % (2 * SEG)
        angle = phase * (2.0 * math.pi / (2 * SEG))
        return np.concatenate([np.cos(angle), np.sin(angle)], axis=-1).astype(np.float32)

    return waves(FOLD), waves(1)


def table_kernel(coarse_ref, fine_ref, hi_ref, lo_ref):
    fine_cos = fine_ref[0, :, :BINS]
    fine_sin = fine_ref[0, :, BINS:]

    def row_block(a, carry):
        base_cos = coarse_ref[0, pl.ds(a, 1), :BINS]
        base_sin = coarse_ref[0, pl.ds(a, 1), BINS:]
        real = base_cos * fine_cos - base_sin * fine_sin
        imag = -(base_sin * fine_cos + base_cos * fine_sin)
        rows = pl.ds(pl.multiple_of(a * FOLD, FOLD), FOLD)
        for part, lo_lane in ((real, 0), (imag, BINS)):
            top = part.astype(jnp.bfloat16)
            hi_ref[0, rows, lo_lane:lo_lane + BINS] = top
            lo_ref[0, rows, lo_lane:lo_lane + BINS] = (part - top.astype(jnp.float32)).astype(jnp.bfloat16)
        return carry

    lax.fori_loop(0, FOLD, row_block, 0)


def make_tables():
    coarse, fine = small_tables()
    shape = jax.ShapeDtypeStruct((CHUNKS, SEG, WIDTH), jnp.bfloat16)
    small = pl.BlockSpec((1, FOLD, WIDTH), lambda p: (p, 0, 0))
    large = pl.BlockSpec((1, SEG, WIDTH), lambda p: (p, 0, 0))
    return pl.pallas_call(
        table_kernel,
        grid=(CHUNKS,),
        in_specs=[small, small],
        out_specs=[large, large],
        out_shape=[shape, shape],
        name="tables",
    )(jnp.asarray(coarse), jnp.asarray(fine))


def normalize_kernel(half_ref, samples_ref, scale_ref, alive_ref, out_ref, *, seg_count):
    rows_per_channel = samples_ref.shape[0] // TILE
    windows = out_ref.shape[0] // seg_count
    pieces = SEG // LANES
    blocks = scale_ref.shape[1] // windows
    length = seg_count * SEG

    def rows(w, n, piece):
        start = (n * pieces + piece) * windows + w
        return samples_ref[pl.ds(start, TILE, stride=rows_per_channel), :].astype(jnp.float32)

    scale = scale_ref[...]
    for w in range(windows):
        total = jnp.zeros((TILE, LANES), jnp.float32)
        for n in range(seg_count):
            for pair in range(pieces // 2):
                column = w * blocks + n * (pieces // 2) + pair
                first = rows(w, n, 2 * pair)
                second = rows(w, n, 2 * pair + 1)
                weight = scale[:, column:column + 1]
                total = total + (first * first + second * second) * (weight * weight)
        energy = jnp.sum(total, axis=1, keepdims=True) * (1.0 / length)
        factor = alive_ref[...] * lax.rsqrt(energy + 1e-06)
        for n in range(seg_count):
            for pair in range(pieces // 2):
                column = w * blocks + n * (pieces // 2) + pair
                weight = scale[:, column:column + 1] * factor
                for piece in (2 * pair, 2 * pair + 1):
                    value = rows(w, n, piece) * weight
                    out_ref[w * seg_count + n, :, piece * LANES:(piece + 1) * LANES] = value.astype(jnp.bfloat16)


def normalize_half(half, samples_rows, scales, alive, seg_count, windows):
    per_channel = seg_count * (SEG // LANES) * windows
    steps = HALF // TILE
    import functools
    return pl.pallas_call(
        functools.partial(normalize_kernel, seg_count=seg_count),
        grid_spec=pltpu.PrefetchScalarGridSpec(
            num_scalar_prefetch=1,
            grid=(steps,),
            in_specs=[
                pl.BlockSpec((TILE * per_channel, LANES), lambda i, h: (h[0] * steps + i, 0)),
                pl.BlockSpec((TILE, scales.shape[1]), lambda i, h: (h[0] * steps + i, 0)),
                pl.BlockSpec((TILE, 1), lambda i, h: (h[0] * steps + i, 0)),
            ],
            out_specs=pl.BlockSpec((windows * seg_count, TILE, SEG), lambda i, h: (0, i, 0)),
        ),
        out_shape=jax.ShapeDtypeStruct((windows * seg_count, HALF, SEG), jnp.bfloat16),
        name="normalize",
    )(half, samples_rows, scales, alive)


def cross_kernel(limits_ref, near_ref, far_ref, sources_ref, table_ref, own_ref, up_ref, down_ref,
                 band_ref, src_ref, plus_ref, minus_ref):
    step = pl.program_id(0)
    count = near_ref.shape[0]
    seg_total = 2 * count
    table = table_ref[0]

    @pl.when(step == 0)
    def _():
        spec = jnp.dot(sources_ref[...], table, preferred_element_type=jnp.float32)
        spec = spec.astype(jnp.bfloat16).astype(jnp.float32)
        for b in range(BINS // LANES):
            real = spec[:, b * LANES:(b + 1) * LANES]
            imag = spec[:, BINS + b * LANES:BINS + (b + 1) * LANES]
            src_ref[b] = real
            plus_ref[b] = real + imag
            minus_ref[b] = imag - real

    for part, ref in ((0, near_ref), (1, far_ref)):
        rows = ref[...].reshape(count * TILE, SEG)
        spec = jnp.dot(rows, table, preferred_element_type=jnp.float32)
        band_ref[pl.ds(part * count * TILE, count * TILE), :] = spec.astype(jnp.bfloat16).astype(jnp.float32)

    def group(which, out_ref, bank, row):
        lane = pl.multiple_of(bank * LANES, LANES)
        real_lanes = pl.ds(lane, LANES)
        imag_lanes = pl.ds(BINS + lane, LANES)
        zero = jnp.zeros((8, LANES), jnp.float32)
        acc = [[[zero, zero, zero] for _ in range(4)] for _ in range(SUB // 8)]
        for q in range(seg_total):
            band = []
            for t in range(SUB // 8):
                at = pl.ds(q * TILE + row + 8 * t, 8)
                g_re = band_ref[at, real_lanes]
                g_im = band_ref[at, imag_lanes]
                band.append((g_re, g_im, g_re + g_im))
            for j in range(4):
                at = pl.ds((which * 4 + j) * seg_total + q, 8, stride=0)
                s_re = src_ref[bank, at, :]
                s_plus = plus_ref[bank, at, :]
                s_minus = minus_ref[bank, at, :]
                for t in range(SUB // 8):
                    g_re, g_im, g_sum = band[t]
                    a = acc[t][j]
                    a[0] = a[0] + s_re * g_sum
                    a[1] = a[1] + s_minus * g_im
                    a[2] = a[2] + s_plus * g_re
        for j in range(4):
            real = jnp.concatenate([acc[t][j][0] + acc[t][j][1] for t in range(SUB // 8)], axis=0)
            imag = jnp.concatenate([acc[t][j][0] - acc[t][j][2] for t in range(SUB // 8)], axis=0)
            out_ref[j, pl.ds(row, SUB), real_lanes] = real.astype(out_ref.dtype)
            out_ref[j, pl.ds(row, SUB), imag_lanes] = imag.astype(out_ref.dtype)

    def tile(index, carry):
        bank = index % (BINS // LANES)
        row = pl.multiple_of((index // (BINS // LANES)) * SUB, SUB)
        channel = limits_ref[0] + step * TILE + row

        @pl.when(channel + SUB > limits_ref[1])
        def _():
            group(1, up_ref, bank, row)

        @pl.when(channel < limits_ref[2])
        def _():
            group(2, down_ref, bank, row)

        group(0, own_ref, bank, row)
        return carry

    lax.fori_loop(0, (TILE // SUB) * (BINS // LANES), tile, 0)


def cross_chunk(chunk, limits, near, far, sources, tables):
    count = near.shape[0]
    src_rows = sources.shape[0]
    block = pl.BlockSpec((count, TILE, SEG), lambda i, h: (0, i, 0))
    result = pl.BlockSpec((4, TILE, WIDTH), lambda i, h: (0, i, 0))
    return pl.pallas_call(
        cross_kernel,
        grid_spec=pltpu.PrefetchScalarGridSpec(
            num_scalar_prefetch=1,
            grid=(HALF // TILE,),
            in_specs=[
                block,
                block,
                pl.BlockSpec((src_rows, SEG), lambda i, h: (0, 0)),
                pl.BlockSpec((1, SEG, WIDTH), lambda i, h: (chunk, 0, 0)),
            ],
            out_specs=[result, result, result],
            scratch_shapes=[
                pltpu.VMEM((2 * count * TILE, WIDTH), jnp.float32),
                pltpu.VMEM((BINS // LANES, src_rows, LANES), jnp.float32),
                pltpu.VMEM((BINS // LANES, src_rows, LANES), jnp.float32),
                pltpu.VMEM((BINS // LANES, src_rows, LANES), jnp.float32),
            ],
        ),
        out_shape=[
            jax.ShapeDtypeStruct((4, HALF, WIDTH), jnp.float32),
            jax.ShapeDtypeStruct((4, HALF, WIDTH), jnp.bfloat16),
            jax.ShapeDtypeStruct((4, HALF, WIDTH), jnp.bfloat16),
        ],
        name="cross",
    )(limits, near, far, sources, tables)


def inverse_kernel(starts_ref, *refs, chunk):
    if chunk:
        mine_ref, mate_ref, weight_ref, hi_ref, lo_ref, prev_ref, out_ref, top_ref, rest_ref = refs
    else:
        mine_ref, mate_ref, weight_ref, hi_ref, lo_ref, out_ref, top_ref, rest_ref = refs
    source_row = lax.broadcasted_iota(jnp.int32, (HALF, 2 * HALF), 1)
    target_row = lax.broadcasted_iota(jnp.int32, (HALF, 2 * HALF), 0)
    for j in range(4):
        wanted = target_row + starts_ref[j]
        wanted = jnp.where(wanted >= 2 * HALF, wanted - 2 * HALF, wanted)
        turn = jnp.where(source_row == wanted, 1.0, 0.0).astype(jnp.bfloat16)
        rows = jnp.concatenate([mine_ref[j], mate_ref[j]], axis=0) * weight_ref[0]
        top = rows.astype(jnp.bfloat16)
        rest = (rows - top.astype(jnp.float32)).astype(jnp.bfloat16)
        at = pl.ds(j * HALF, HALF)
        top_ref[at, :] = jnp.dot(turn, top, preferred_element_type=jnp.float32).astype(jnp.bfloat16)
        rest_ref[at, :] = jnp.dot(turn, rest, preferred_element_type=jnp.float32).astype(jnp.bfloat16)

    def product(a, b):
        return lax.dot_general(a, b, (((1,), (1,)), ((), ())), preferred_element_type=jnp.float32)

    top = top_ref[...]
    hi = hi_ref[0]
    terms = product(top, hi) + (product(rest_ref[...], hi) + product(top, lo_ref[0]))
    terms = terms.reshape(4, HALF, SEG)
    before = terms if chunk % 2 == 0 else -terms
    if chunk:
        out_ref[:, :, :SEG] = prev_ref[:, :, :SEG] + before
        out_ref[:, :, SEG:] = prev_ref[:, :, SEG:] + terms
    else:
        out_ref[:, :, :SEG] = before
        out_ref[:, :, SEG:] = terms


def inverse_chunk(chunk, starts, mine, mate, weights, hi, lo, prev):
    import functools
    whole = pl.BlockSpec((4, HALF, WIDTH), lambda i, h: (0, 0, 0))
    table = pl.BlockSpec((1, SEG, WIDTH), lambda i, h: (chunk, 0, 0))
    stacks = pl.BlockSpec((4, HALF, 2 * SEG), lambda i, h: (0, 0, 0))
    operands = [starts, mine, mate, weights, hi, lo] + ([prev] if chunk else [])
    return pl.pallas_call(
        functools.partial(inverse_kernel, chunk=chunk),
        grid_spec=pltpu.PrefetchScalarGridSpec(
            num_scalar_prefetch=1,
            grid=(1,),
            in_specs=[whole, whole, pl.BlockSpec((1, 1, WIDTH), lambda i, h: (chunk, 0, 0)), table, table]
            + ([stacks] if chunk else []),
            out_specs=stacks,
            scratch_shapes=[
                pltpu.VMEM((4 * HALF, WIDTH), jnp.bfloat16),
                pltpu.VMEM((4 * HALF, WIDTH), jnp.bfloat16),
            ],
        ),
        out_shape=jax.ShapeDtypeStruct((4, HALF, 2 * SEG), jnp.float32),
        input_output_aliases={6: 0} if chunk else {},
        name="inverse",
    )(*operands)


def block_scale(exponents):
    levels = jnp.arange(5, dtype=jnp.int32)
    powers = jnp.exp2(levels.astype(jnp.float32))
    return jnp.sum(jnp.where(exponents[..., None] == levels, powers, 0.0), axis=-1)


def passed_along(block, axis, distance):
    devices = range(lax.axis_size(axis))
    route = [(i - distance, i) for i in devices if i - distance in devices]
    return lax.ppermute(block, axis, route)


def partner(block, bit):
    return lax.ppermute(block, "win", [(i, i ^ bit) for i in range(lax.axis_size("win"))])


def source_rows(samples_rows, scales, alive, offsets, windows, seg_count):
    pieces = SEG // LANES
    blocks = seg_count * pieces // 2
    per_channel = seg_count * pieces * windows
    values, factors, lives = [], [], []
    for j in range(4):
        values.append(lax.dynamic_slice_in_dim(samples_rows, offsets[j] * per_channel, per_channel, 0))
        factors.append(lax.dynamic_slice_in_dim(scales, offsets[j], 1, 0))
        lives.append(lax.dynamic_slice_in_dim(alive, offsets[j], 1, 0))
    raw = jnp.stack(values).astype(jnp.float32).reshape(4, blocks, 2, windows, LANES)
    scale = jnp.concatenate(factors).reshape(4, windows, blocks).transpose(0, 2, 1)
    amplitude = raw * scale[:, :, None, :, None]
    energy = jnp.mean(amplitude * amplitude, axis=(1, 2, 4), keepdims=True)
    factor = jnp.concatenate(lives).reshape(4, 1, 1, 1, 1) * lax.rsqrt(energy + 1e-06)
    normed = (amplitude * factor).astype(jnp.bfloat16)
    normed = normed.reshape(4, seg_count, pieces, windows, LANES).transpose(0, 3, 1, 2, 4)
    return normed.reshape(4, windows * seg_count, SEG)


def shards(samples, exponents, alive, offsets):
    channels, windows, length = samples.shape
    seg_count = length // SEG
    place = lax.axis_index("win")
    chan = lax.axis_index("chan")
    core = place % 2
    upper_half = place // 2
    last = lax.axis_size("chan") - 1

    samples_rows = samples.reshape(channels, windows, length // LANES, LANES)
    samples_rows = samples_rows.transpose(0, 2, 1, 3).reshape(channels * windows * (length // LANES), LANES)
    scales = block_scale(exponents).reshape(channels, -1)
    live = alive.astype(jnp.float32).reshape(channels, 1)

    own_src = source_rows(samples_rows, scales, live, offsets, windows, seg_count)
    own_src = jnp.concatenate([own_src, partner(own_src, 1)], axis=1)
    above_src = passed_along(own_src, "chan", -1)
    below_src = passed_along(own_src, "chan", 1)
    above_off = passed_along(offsets, "chan", -1)
    below_off = passed_along(offsets, "chan", 1)
    sources = jnp.concatenate([own_src, above_src, below_src], axis=0).reshape(-1, SEG)
    lowest = jnp.where(chan == last, channels, jnp.min(above_off))
    highest = jnp.where(chan == 0, 0, jnp.max(below_off))
    limits = jnp.stack([core * HALF, lowest, highest]).astype(jnp.int32)

    sent = normalize_half((1 - core).reshape(1), samples_rows, scales, live, seg_count, windows)
    far = partner(sent, 1)
    near = normalize_half(core.reshape(1), samples_rows, scales, live, seg_count, windows)
    hi, lo = make_tables()

    index = core * HALF + jnp.arange(HALF, dtype=jnp.int32)
    below_source = (index[None, :] < offsets[:, None])[:, :, None]
    keep_own = below_source == (upper_half == 0)
    k = CHUNKS * np.arange(BINS)[None, :] + np.arange(CHUNKS)[:, None]
    weights = np.where(k == 0, 1.0, 2.0) / float(2 * SEG * windows * 4 * seg_count * SEG)
    weights = jnp.asarray(np.concatenate([weights, weights], axis=1).astype(np.float32).reshape(CHUNKS, 1, WIDTH))

    stacks = None
    for chunk in range(CHUNKS):
        own, to_above, to_below = cross_chunk(chunk, limits, near, far, sources, hi)
        from_below = passed_along(to_above, "chan", 1)
        from_above = passed_along(to_below, "chan", -1)
        other = jnp.where(below_source, from_above, from_below).astype(jnp.float32)
        kept = jnp.where(keep_own, own, other)
        passed = jnp.where(keep_own, other, own).astype(jnp.bfloat16)
        total = kept + partner(passed, 2).astype(jnp.float32)
        mate = partner(total, 1)
        stacks = inverse_chunk(chunk, offsets, total, mate, weights, hi, lo, stacks)
    return stacks


def solution(mesh):
    placed = (P("chan", "win", None), P("chan", "win", None), P("chan"), P("chan"))
    return jax.shard_map(
        shards, mesh=mesh, in_specs=placed, out_specs=P("chan", "win", None), check_vma=False
    )
```

```python
import functools
import math

import jax
import jax.numpy as jnp
import numpy as np
from jax import lax
from jax.experimental import pallas as pl
from jax.experimental.pallas import tpu as pltpu
from jax.sharding import PartitionSpec as P

SEG = 1024
HALF = 96
LANES = 128
GROUPS = SEG // LANES
PAIR = 2 * LANES
CHUNKS = ((0, 3), (3, 3), (6, 2))
FOLD = 32
TILE = 32
SUB = 16
PITCH = 104
SOURCES = 4
SLOT = 16
COLS = 256


def small_tables():
    k = GROUPS * np.arange(LANES)[None, :] + np.arange(GROUPS)[:, None]
    step = np.arange(FOLD)

    def waves(stride):
        phase = (stride * step[None, :, None] * k[:, None, :]) % (2 * SEG)
        angle = phase * (2.0 * math.pi / (2 * SEG))
        return np.stack([np.cos(angle), np.sin(angle)], axis=1).astype(np.float32)

    return waves(FOLD), waves(1)


def table_kernel(coarse_ref, fine_ref, hi_ref, lo_ref):
    fine_cos = fine_ref[0, 0]
    fine_sin = fine_ref[0, 1]

    def row_block(a, carry):
        base_cos = jnp.concatenate([coarse_ref[0, 0, pl.ds(a, 8, stride=0), :]] * (FOLD // 8), axis=0)
        base_sin = jnp.concatenate([coarse_ref[0, 1, pl.ds(a, 8, stride=0), :]] * (FOLD // 8), axis=0)
        real = base_cos * fine_cos - base_sin * fine_sin
        imag = -(base_sin * fine_cos + base_cos * fine_sin)
        rows = pl.ds(pl.multiple_of(a * FOLD, FOLD), FOLD)
        for part, lane in ((real, 0), (imag, LANES)):
            top = part.astype(jnp.bfloat16)
            hi_ref[0, rows, lane:lane + LANES] = top
            lo_ref[0, rows, lane:lane + LANES] = (part - top.astype(jnp.float32)).astype(jnp.bfloat16)
        return carry

    lax.fori_loop(0, FOLD, row_block, 0)


def make_tables(first, count, coarse, fine):
    shape = jax.ShapeDtypeStruct((count, SEG, PAIR), jnp.bfloat16)
    small = pl.BlockSpec((1, 2, FOLD, LANES), lambda p: (first + p, 0, 0, 0))
    large = pl.BlockSpec((1, SEG, PAIR), lambda p: (p, 0, 0))
    return pl.pallas_call(
        table_kernel,
        grid=(count,),
        in_specs=[small, small],
        out_specs=[large, large],
        out_shape=[shape, shape],
        name="tables",
    )(coarse, fine)


def normalize_kernel(half_ref, samples_ref, scale_ref, out_ref, buffer_ref, sems, *, seg_count, windows):
    step = pl.program_id(0)
    steps = pl.num_programs(0)
    per_channel = samples_ref.shape[1]
    pieces = SEG // LANES
    pairs = pieces // 2
    blocks = seg_count * pairs
    slot = step % 2

    def copy(at, into):
        first = half_ref[0] * HALF + at * TILE
        return pltpu.make_async_copy(
            samples_ref.at[pl.ds(first, TILE)],
            buffer_ref.at[into, :, pl.ds(0, per_channel), :],
            sems.at[into],
        )

    @pl.when(step == 0)
    def _():
        copy(0, 0).start()

    @pl.when(step + 1 < steps)
    def _():
        copy(step + 1, 1 - slot).start()

    copy(step, slot).wait()
    flat = buffer_ref.reshape(2 * TILE * PITCH, LANES)
    base = slot * (TILE * PITCH)

    def rows(w, n, piece):
        start = base + (n * pieces + piece) * windows + w
        return flat[pl.ds(start, TILE, stride=PITCH), :].astype(jnp.float32)

    scale = scale_ref[...]
    live = scale[:, windows * blocks:windows * blocks + 1]
    for w in range(windows):
        total = jnp.zeros((TILE, LANES), jnp.float32)
        for n in range(seg_count):
            for pair in range(pairs):
                column = w * blocks + n * pairs + pair
                one = rows(w, n, 2 * pair)
                two = rows(w, n, 2 * pair + 1)
                weight = scale[:, column:column + 1]
                total = total + (one * one + two * two) * (weight * weight)
        energy = jnp.sum(total, axis=1, keepdims=True) * (1.0 / (seg_count * SEG))
        factor = live * lax.rsqrt(energy + 1e-06)
        for n in range(seg_count):
            for pair in range(pairs):
                column = w * blocks + n * pairs + pair
                weight = scale[:, column:column + 1] * factor
                for piece in (2 * pair, 2 * pair + 1):
                    value = rows(w, n, piece) * weight
                    out_ref[w * seg_count + n, :, piece * LANES:(piece + 1) * LANES] = value.astype(jnp.bfloat16)


def normalize_half(half, samples_rows, scales, seg_count, windows):
    steps = HALF // TILE
    return pl.pallas_call(
        functools.partial(normalize_kernel, seg_count=seg_count, windows=windows),
        grid_spec=pltpu.PrefetchScalarGridSpec(
            num_scalar_prefetch=1,
            grid=(steps,),
            in_specs=[
                pl.BlockSpec(memory_space=pl.ANY),
                pl.BlockSpec((TILE, scales.shape[1]), lambda i, h: (h[0] * steps + i, 0)),
            ],
            out_specs=pl.BlockSpec((windows * seg_count, TILE, SEG), lambda i, h: (0, i, 0)),
            scratch_shapes=[
                pltpu.VMEM((2, TILE, PITCH, LANES), jnp.int32),
                pltpu.SemaphoreType.DMA((2,)),
            ],
        ),
        out_shape=jax.ShapeDtypeStruct((windows * seg_count, HALF, SEG), jnp.bfloat16),
        name="normalize",
    )(half, samples_rows, scales)


def source_kernel(offsets_ref, samples_ref, scale_ref, out_ref, sorted_ref, buffer_ref, rows_ref, sems, *,
                  seg_count, windows):
    pieces = SEG // LANES
    pairs = pieces // 2
    blocks = seg_count * pairs
    channels = scale_ref.shape[0]
    per_channel = samples_ref.shape[1]
    given = [offsets_ref[j] for j in range(SOURCES)]
    ranks = []
    for j in range(SOURCES):
        rank = jnp.int32(0)
        for i in range(SOURCES):
            if i != j:
                ahead = given[i] <= given[j] if i < j else given[i] < given[j]
                rank = rank + jnp.where(ahead, 1, 0)
        ranks.append(rank)
    order = []
    for r in range(SOURCES):
        offset = jnp.int32(0)
        origin = jnp.int32(0)
        for j in range(SOURCES):
            hit = ranks[j] == r
            offset = jnp.where(hit, given[j], offset)
            origin = jnp.where(hit, j, origin)
        sorted_ref[r] = offset
        sorted_ref[SOURCES + r] = origin
        order.append(offset)
    copies = []
    for r in range(SOURCES):
        copy = pltpu.make_async_copy(
            samples_ref.at[order[r]], buffer_ref.at[r, pl.ds(0, per_channel), :], sems.at[r]
        )
        copy.start()
        copies.append(copy)
    channel = lax.broadcasted_iota(jnp.int32, scale_ref.shape, 0)
    lane = lax.broadcasted_iota(jnp.int32, (8, scale_ref.shape[1]), 1)
    segment = lax.broadcasted_iota(jnp.int32, (8, scale_ref.shape[1]), 0)
    valid = lax.broadcasted_iota(jnp.int32, (8, LANES), 0) < seg_count
    rows_ref[...] = jnp.zeros(rows_ref.shape, jnp.float32)
    for r in range(SOURCES):
        picked = jnp.sum(jnp.where(channel == order[r], scale_ref[...], 0.0), axis=0, keepdims=True)
        picked = jnp.broadcast_to(picked, (8, scale_ref.shape[1]))
        live = jnp.sum(jnp.where(lane == windows * blocks, picked, 0.0), axis=1, keepdims=True)
        copies[r].wait()
        for w in range(windows):
            parts = []
            total = jnp.zeros((8, LANES), jnp.float32)
            for pair in range(pairs):
                column = w * blocks + segment * pairs + pair
                weight = jnp.sum(jnp.where(lane == column, picked, 0.0), axis=1, keepdims=True)
                for piece in (2 * pair, 2 * pair + 1):
                    raw = buffer_ref[r, pl.ds(piece * windows + w, 8, stride=pieces * windows), :]
                    part = jnp.where(valid, raw.astype(jnp.float32), 0.0) * weight
                    total = total + part * part
                    parts.append(part)
            energy = jnp.sum(jnp.sum(total, axis=1, keepdims=True), axis=0, keepdims=True)
            factor = live * lax.rsqrt(energy * (1.0 / (seg_count * SEG)) + 1e-06)
            for piece in range(pieces):
                rows_ref[r, pl.ds(w * seg_count, seg_count), piece * LANES:(piece + 1) * LANES] = (
                    parts[piece] * factor
                )[:seg_count]
        rows_ref[r, pl.ds(windows * seg_count, 1), :] = jnp.full((1, SEG), 1, jnp.float32) * (
            order[r] + 1
        ).astype(jnp.float32)
        out_ref[r] = rows_ref[r].astype(jnp.bfloat16)


def source_rows(offsets, samples_rows, scales, seg_count, windows):
    return pl.pallas_call(
        functools.partial(source_kernel, seg_count=seg_count, windows=windows),
        grid_spec=pltpu.PrefetchScalarGridSpec(
            num_scalar_prefetch=1,
            grid=(1,),
            in_specs=[
                pl.BlockSpec(memory_space=pl.ANY),
                pl.BlockSpec(scales.shape, lambda i, h: (0, 0)),
            ],
            out_specs=[
                pl.BlockSpec((SOURCES, SLOT, SEG), lambda i, h: (0, 0, 0)),
                pl.BlockSpec(memory_space=pltpu.SMEM),
            ],
            scratch_shapes=[
                pltpu.VMEM((SOURCES, 128, LANES), jnp.int32),
                pltpu.VMEM((SOURCES, SLOT, SEG), jnp.float32),
                pltpu.SemaphoreType.DMA((SOURCES,)),
            ],
        ),
        out_shape=[
            jax.ShapeDtypeStruct((SOURCES, SLOT, SEG), jnp.bfloat16),
            jax.ShapeDtypeStruct((2 * SOURCES,), jnp.int32),
        ],
        name="sources",
    )(offsets, samples_rows, scales)


def cross_kernel(limits_ref, near_ref, far_ref, own_src_ref, above_src_ref, below_src_ref, table_ref,
                 own_ref, up_ref, down_ref, band_ref, src_ref, plus_ref, minus_ref):
    step = pl.program_id(0)
    count = near_ref.shape[0]
    groups = table_ref.shape[0]
    src_rows = 2 * SLOT

    @pl.when(step == 0)
    def _():
        for which, ref in enumerate((own_src_ref, above_src_ref, below_src_ref)):
            rows = ref[...].reshape(SOURCES * src_rows, SEG)
            at = pl.ds(which * SOURCES * src_rows, SOURCES * src_rows)
            for g in range(groups):
                spec = jnp.dot(rows, table_ref[g], preferred_element_type=jnp.float32)
                spec = spec.astype(jnp.bfloat16).astype(jnp.float32)
                real = spec[:, :LANES]
                imag = spec[:, LANES:]
                src_ref[g, at, :] = real
                plus_ref[g, at, :] = real + imag
                minus_ref[g, at, :] = imag - real

    for part, ref in ((0, near_ref), (1, far_ref)):
        rows = ref[...].reshape(count * TILE, SEG)
        at = pl.ds(part * count * TILE, count * TILE)
        for g in range(groups):
            spec = jnp.dot(rows, table_ref[g], preferred_element_type=jnp.float32)
            spec = spec.astype(jnp.bfloat16).astype(jnp.float32)
            band_ref[2 * g, at, :] = spec[:, :LANES]
            band_ref[2 * g + 1, at, :] = spec[:, LANES:]

    def products(which, members, out_ref, g, row):
        lane = pl.multiple_of(g * PAIR, PAIR)
        real_lanes = pl.ds(lane, LANES)
        imag_lanes = pl.ds(pl.multiple_of(lane + LANES, LANES), LANES)
        zero = jnp.zeros((8, LANES), jnp.float32)
        acc = {(t, j): [zero, zero, zero] for t in range(SUB // 8) for j in members}
        for q in range(2 * count):
            band = []
            for t in range(SUB // 8):
                at = pl.ds(q * TILE + row + 8 * t, 8)
                g_re = band_ref[2 * g, at, :]
                g_im = band_ref[2 * g + 1, at, :]
                band.append((g_re, g_im, g_re + g_im))
            spot = q if q < count else SLOT + q - count
            for j in members:
                at = pl.ds((which * SOURCES + j) * src_rows + spot, 8, stride=0)
                s_re = src_ref[g, at, :]
                s_plus = plus_ref[g, at, :]
                s_minus = minus_ref[g, at, :]
                for t in range(SUB // 8):
                    g_re, g_im, g_sum = band[t]
                    a = acc[t, j]
                    a[0] = a[0] + s_re * g_sum
                    a[1] = a[1] + s_minus * g_im
                    a[2] = a[2] + s_plus * g_re
        for j in members:
            real = jnp.concatenate([acc[t, j][0] + acc[t, j][1] for t in range(SUB // 8)], axis=0)
            imag = jnp.concatenate([acc[t, j][0] - acc[t, j][2] for t in range(SUB // 8)], axis=0)
            out_ref[j, pl.ds(row, SUB), real_lanes] = real.astype(out_ref.dtype)
            out_ref[j, pl.ds(row, SUB), imag_lanes] = imag.astype(out_ref.dtype)

    def tile(index, carry):
        g = index // (TILE // SUB)
        row = pl.multiple_of((index % (TILE // SUB)) * SUB, SUB)
        channel = limits_ref[0] + step * TILE + row
        for first in (0, 2):
            pair = (first, first + 1)

            @pl.when(channel + SUB > limits_ref[1 + first])
            def _():
                products(1, pair, up_ref, g, row)

            @pl.when(channel < limits_ref[1 + SOURCES + first + 1])
            def _():
                products(2, pair, down_ref, g, row)

        products(0, (0, 1, 2, 3), own_ref, g, row)
        return carry

    lax.fori_loop(0, groups * (TILE // SUB), tile, 0)


def cross_chunk(limits, near, far, own_src, above_src, below_src, table):
    count = near.shape[0]
    groups = table.shape[0]
    width = groups * PAIR
    src_rows = 3 * SOURCES * 2 * SLOT
    block = pl.BlockSpec((count, TILE, SEG), lambda i, h: (0, i, 0))
    src = pl.BlockSpec((SOURCES, 2 * SLOT, SEG), lambda i, h: (0, 0, 0))
    result = pl.BlockSpec((SOURCES, TILE, width), lambda i, h: (0, i, 0))
    return pl.pallas_call(
        cross_kernel,
        grid_spec=pltpu.PrefetchScalarGridSpec(
            num_scalar_prefetch=1,
            grid=(HALF // TILE,),
            in_specs=[block, block, src, src, src, pl.BlockSpec((groups, SEG, PAIR), lambda i, h: (0, 0, 0))],
            out_specs=[result, result, result],
            scratch_shapes=[
                pltpu.VMEM((2 * groups, 2 * count * TILE, LANES), jnp.float32),
                pltpu.VMEM((groups, src_rows, LANES), jnp.float32),
                pltpu.VMEM((groups, src_rows, LANES), jnp.float32),
                pltpu.VMEM((groups, src_rows, LANES), jnp.float32),
            ],
        ),
        out_shape=[
            jax.ShapeDtypeStruct((SOURCES, HALF, width), jnp.float32),
            jax.ShapeDtypeStruct((SOURCES, HALF, width), jnp.bfloat16),
            jax.ShapeDtypeStruct((SOURCES, HALF, width), jnp.bfloat16),
        ],
        name="cross",
    )(limits, near, far, own_src, above_src, below_src, table)


def select_kernel(sorted_ref, place_ref, own_ref, below_ref, above_ref, kept_ref, passed_ref):
    base = place_ref[0]
    lower = place_ref[1] == 0
    index = base + lax.broadcasted_iota(jnp.int32, (HALF, LANES), 0)
    for j in range(SOURCES):
        below_source = index < sorted_ref[j]
        first = jnp.where(below_source, 1, 0)
        keep = first == jnp.where(lower, 1, 0)
        for lane in range(0, own_ref.shape[2], LANES):
            at = (j, slice(None), slice(lane, lane + LANES))
            own = own_ref[at]
            other = jnp.where(below_source, above_ref[at].astype(jnp.float32), below_ref[at].astype(jnp.float32))
            kept_ref[at] = jnp.where(keep, own, other)
            passed_ref[at] = jnp.where(keep, other, own).astype(jnp.bfloat16)


def select_rows(ordered, place, own, from_below, from_above):
    whole = pl.BlockSpec(memory_space=pltpu.VMEM)
    return pl.pallas_call(
        select_kernel,
        in_specs=[pl.BlockSpec(memory_space=pltpu.SMEM), pl.BlockSpec(memory_space=pltpu.SMEM), whole, whole, whole],
        out_specs=[whole, whole],
        out_shape=[jax.ShapeDtypeStruct(own.shape, jnp.float32), jax.ShapeDtypeStruct(own.shape, jnp.bfloat16)],
        name="select",
    )(ordered, place, own, from_below, from_above)


def turned(ordered_ref, mine_ref, mate_ref, top_ref, halve):
    source_row = lax.broadcasted_iota(jnp.int32, (HALF, 2 * HALF), 1)
    target_row = lax.broadcasted_iota(jnp.int32, (HALF, 2 * HALF), 0)
    for j in range(SOURCES):
        wanted = target_row + ordered_ref[j]
        wanted = jnp.where(wanted >= 2 * HALF, wanted - 2 * HALF, wanted)
        turn = jnp.where(source_row == wanted, 1.0, 0.0).astype(jnp.bfloat16)
        rows = jnp.concatenate([mine_ref[j], mate_ref[j]], axis=0)
        top_ref[pl.ds(j * HALF, HALF), :] = jnp.dot(turn, rows, preferred_element_type=jnp.float32).astype(
            jnp.bfloat16
        )
    if halve:
        lane = lax.broadcasted_iota(jnp.int32, (SOURCES * HALF, LANES), 1)
        first = top_ref[:, :LANES].astype(jnp.float32)
        top_ref[:, :LANES] = jnp.where(lane == 0, 0.5 * first, first).astype(jnp.bfloat16)


def folded(top_ref, hi_ref, lo_ref, first, sums):
    for g in range(hi_ref.shape[0]):
        rows = top_ref[:, g * PAIR:(g + 1) * PAIR]
        for table in (hi_ref[g], lo_ref[g]):
            part = lax.dot_general(rows, table, (((1,), (1,)), ((), ())), preferred_element_type=jnp.float32)
            parity = (first + g) % 2
            sums[parity] = part if sums[parity] is None else sums[parity] + part


def early_kernel(ordered_ref, *refs, firsts):
    count = len(firsts)
    tops = refs[4 * count + 2:]
    even_ref, odd_ref = refs[4 * count:4 * count + 2]
    for c, first in enumerate(firsts):
        @pl.when(pl.program_id(0) == 0)
        def _():
            turned(ordered_ref, refs[4 * c], refs[4 * c + 1], tops[c], first == 0)
    sums = [None, None]
    for c, first in enumerate(firsts):
        folded(tops[c], refs[4 * c + 2], refs[4 * c + 3], first, sums)
    even_ref[...] = sums[0]
    odd_ref[...] = sums[1]


def chunk_specs(groups):
    rows = pl.BlockSpec((SOURCES, HALF, groups * PAIR), lambda m, h: (0, 0, 0))
    table = pl.BlockSpec((groups, COLS, PAIR), lambda m, h: (0, m, 0))
    return [rows, rows, table, table]


def early_inverse(ordered, parts, firsts):
    specs, operands, tops = [], [], []
    for part in parts:
        groups = part[2].shape[0]
        specs += chunk_specs(groups)
        operands += list(part)
        tops.append(pltpu.VMEM((SOURCES * HALF, groups * PAIR), jnp.bfloat16))
    block = pl.BlockSpec((SOURCES * HALF, COLS), lambda m, h: (0, m))
    shape = jax.ShapeDtypeStruct((SOURCES * HALF, SEG), jnp.float32)
    return pl.pallas_call(
        functools.partial(early_kernel, firsts=firsts),
        grid_spec=pltpu.PrefetchScalarGridSpec(
            num_scalar_prefetch=1,
            grid=(SEG // COLS,),
            in_specs=specs,
            out_specs=[block, block],
            scratch_shapes=tops,
        ),
        out_shape=[shape, shape],
        name="early",
    )(ordered, *operands)


def last_kernel(ordered_ref, mine_ref, mate_ref, hi_ref, lo_ref, even_ref, odd_ref, out_ref, top_ref, stage_ref, sem,
                *, first, scale):
    m = pl.program_id(0)

    @pl.when(m == 0)
    def _():
        turned(ordered_ref, mine_ref, mate_ref, top_ref, first == 0)

    sums = [even_ref[...], odd_ref[...]]
    folded(top_ref, hi_ref, lo_ref, first, sums)
    stage_ref[m, 0] = (sums[0] - sums[1]) * scale
    stage_ref[m, 1] = (sums[0] + sums[1]) * scale

    def copy(step, side, j):
        lane = pl.multiple_of(side * SEG + step * COLS, COLS)
        return pltpu.make_async_copy(
            stage_ref.at[step, side, pl.ds(j * HALF, HALF), :],
            out_ref.at[ordered_ref[SOURCES + j], :, pl.ds(lane, COLS)],
            sem.at[step, side, j],
        )

    for side in range(2):
        for j in range(SOURCES):
            copy(m, side, j).start()

    @pl.when(m == pl.num_programs(0) - 1)
    def _():
        for step in range(SEG // COLS):
            for side in range(2):
                for j in range(SOURCES):
                    copy(step, side, j).wait()


def last_inverse(ordered, part, even, odd, first, scale):
    groups = part[2].shape[0]
    block = pl.BlockSpec((SOURCES * HALF, COLS), lambda m, h: (0, m))
    return pl.pallas_call(
        functools.partial(last_kernel, first=first, scale=scale),
        grid_spec=pltpu.PrefetchScalarGridSpec(
            num_scalar_prefetch=1,
            grid=(SEG // COLS,),
            in_specs=chunk_specs(groups) + [block, block],
            out_specs=pl.BlockSpec(memory_space=pl.ANY),
            scratch_shapes=[
                pltpu.VMEM((SOURCES * HALF, groups * PAIR), jnp.bfloat16),
                pltpu.VMEM((SEG // COLS, 2, SOURCES * HALF, COLS), jnp.float32),
                pltpu.SemaphoreType.DMA((SEG // COLS, 2, SOURCES)),
            ],
        ),
        out_shape=jax.ShapeDtypeStruct((SOURCES, HALF, 2 * SEG), jnp.float32),
        name="last",
    )(ordered, *part, even, odd)


def block_scale(exponents):
    levels = jnp.arange(5, dtype=jnp.int32)
    powers = jnp.exp2(levels.astype(jnp.float32))
    return jnp.sum(jnp.where(exponents[..., None] == levels, powers, 0.0), axis=-1)


def passed_along(block, axis, distance):
    devices = range(lax.axis_size(axis))
    route = [(i - distance, i) for i in devices if i - distance in devices]
    return lax.ppermute(block, axis, route)


def partner(block, bit):
    return lax.ppermute(block, "win", [(i, i ^ bit) for i in range(lax.axis_size("win"))])


def after(value, *others):
    return lax.optimization_barrier((value,) + others)[0]


def shards(samples, exponents, alive, offsets):
    channels, windows, length = samples.shape
    seg_count = length // SEG
    place = lax.axis_index("win")
    core = place & 1
    upper_half = place >> 1

    samples_rows = samples.reshape(channels, windows, length // LANES, LANES)
    samples_rows = samples_rows.transpose(0, 2, 1, 3).reshape(channels, windows * (length // LANES), LANES)
    scales = block_scale(exponents).reshape(channels, -1)
    scales = jnp.concatenate([scales, alive.astype(jnp.float32).reshape(channels, 1)], axis=1)

    own_src, ordered = source_rows(offsets, samples_rows, scales, seg_count, windows)
    own_src = jnp.concatenate([own_src, partner(own_src, 1)], axis=1)
    above_src = passed_along(own_src, "chan", -1)
    below_src = passed_along(own_src, "chan", 1)

    sent = normalize_half((1 - core).reshape(1), samples_rows, scales, seg_count, windows)
    far = partner(sent, 1)
    near = normalize_half(core.reshape(1), samples_rows, scales, seg_count, windows)
    coarse, fine = (jnp.asarray(t) for t in small_tables())

    flag = windows * seg_count
    above_off = above_src[:, flag, 0].astype(jnp.int32)
    below_off = below_src[:, flag, 0].astype(jnp.int32)
    limits = jnp.concatenate(
        [(core * HALF).reshape(1), jnp.where(above_off == 0, channels, above_off - 1), below_off - 1]
    ).astype(jnp.int32)
    where_am_i = jnp.stack([core * HALF, upper_half]).astype(jnp.int32)
    scale = 2.0 / float(2 * SEG * windows * lax.axis_size("win") * seg_count * SEG)

    tables = [make_tables(first, count, coarse, fine) for first, count in CHUNKS]
    total_chunks = len(CHUNKS)
    crossed, returned, selected, parts = [], [], [], []

    def finish(c):
        kept, moved = selected[c]
        total = (kept + moved.astype(jnp.float32)).astype(jnp.bfloat16)
        parts.append((total, partner(total, 1)) + tuple(tables[c]))

    for c in range(total_chunks):
        gate = limits
        if c >= 2:
            gate = after(limits, selected[c - 2][0])
        own, to_above, to_below = cross_chunk(gate, near, far, own_src, above_src, below_src, tables[c][0])
        crossed.append(own)
        returned.append((passed_along(to_above, "chan", 1), passed_along(to_below, "chan", -1)))
        if c >= 1:
            kept, moved = select_rows(after(ordered, own), where_am_i, crossed[c - 1], *returned[c - 1])
            selected.append((kept, partner(moved, 2)))
    c = total_chunks - 1
    kept, moved = select_rows(ordered, where_am_i, crossed[c], *returned[c])
    selected.append((kept, partner(moved, 2)))
    for c in range(total_chunks):
        finish(c)
    firsts = tuple(first for first, _ in CHUNKS)
    even, odd = early_inverse(ordered, parts[:-1], firsts[:-1])
    return last_inverse(ordered, parts[-1], even, odd, firsts[-1], scale)


def solution(mesh):
    placed = (P("chan", "win", None), P("chan", "win", None), P("chan"), P("chan"))
    return jax.shard_map(
        shards, mesh=mesh, in_specs=placed, out_specs=P("chan", "win", None), check_vma=False
    )
```

```python
import functools
import math

import jax
import jax.numpy as jnp
import numpy as np
from jax import lax
from jax.experimental import pallas as pl
from jax.experimental.pallas import tpu as pltpu
from jax.sharding import PartitionSpec as P


SEG = 1024
HALF = 96
LANES = 128
GROUPS = SEG // LANES
PAIR = 2 * LANES
CHUNKS = ((0, 3), (3, 3), (6, 2))
FOLD = 32
UNROLL = 4
TILE = 32
SUB = 16
PITCH = 104
SOURCES = 4
SLOT = 16
COLS = 256


def small_tables():
    k = GROUPS * np.arange(LANES)[None, :] + np.arange(GROUPS)[:, None]
    step = np.arange(FOLD)

    def waves(stride):
        phase = (stride * step[None, :, None] * k[:, None, :]) % (2 * SEG)
        angle = phase * (2.0 * math.pi / (2 * SEG))
        return np.stack([np.cos(angle), np.sin(angle)], axis=1).astype(np.float32)

    return waves(FOLD), waves(1)


def table_kernel(coarse_ref, fine_ref, hi_ref, lo_ref):
    fine_cos = fine_ref[0, 0]
    fine_sin = fine_ref[0, 1]

    def row_block(step, carry):
        for inner in range(UNROLL):
            a = step * UNROLL + inner
            base_cos = coarse_ref[0, 0, pl.ds(a, 8, stride=0), :]
            base_sin = coarse_ref[0, 1, pl.ds(a, 8, stride=0), :]
            base_cos = jnp.concatenate([base_cos] * (FOLD // 8), axis=0)
            base_sin = jnp.concatenate([base_sin] * (FOLD // 8), axis=0)
            real = base_cos * fine_cos - base_sin * fine_sin
            imag = -(base_sin * fine_cos + base_cos * fine_sin)
            rows = pl.ds(pl.multiple_of(a * FOLD, FOLD), FOLD)
            for part, lane in ((real, 0), (imag, LANES)):
                top = part.astype(jnp.bfloat16)
                hi_ref[0, rows, lane:lane + LANES] = top
                lo_ref[0, rows, lane:lane + LANES] = (part - top.astype(jnp.float32)).astype(jnp.bfloat16)
        return carry

    lax.fori_loop(0, FOLD // UNROLL, row_block, 0)


def make_tables(first, count, coarse, fine):
    shape = jax.ShapeDtypeStruct((count, SEG, PAIR), jnp.bfloat16)
    small = pl.BlockSpec((1, 2, FOLD, LANES), lambda p: (first + p, 0, 0, 0))
    large = pl.BlockSpec((1, SEG, PAIR), lambda p: (p, 0, 0))
    return pl.pallas_call(
        table_kernel,
        grid=(count,),
        in_specs=[small, small],
        out_specs=[large, large],
        out_shape=[shape, shape],
        name="tables",
    )(coarse, fine)


def normalize_kernel(half_ref, samples_ref, scale_ref, out_ref, buffer_ref, spread_ref, wide_ref, sems, *,
                     seg_count, windows):
    step = pl.program_id(0)
    steps = pl.num_programs(0)
    per_channel = samples_ref.shape[1]
    pieces = SEG // LANES
    pairs = pieces // 2
    blocks = seg_count * pairs
    slot = step % 2

    def copy(at, into):
        first = half_ref[0] * HALF + at * TILE
        return pltpu.make_async_copy(
            samples_ref.at[pl.ds(first, TILE)],
            buffer_ref.at[into, :, pl.ds(0, per_channel), :],
            sems.at[into],
        )

    @pl.when(step == 0)
    def _():
        copy(0, 0).start()

    @pl.when(step + 1 < steps)
    def _():
        copy(step + 1, 1 - slot).start()

    columns = wide_ref.shape[0]

    @pl.when(step == 0)
    def _():
        for column in range(columns):
            row = lax.broadcasted_iota(jnp.int32, (columns, LANES), 0)
            spread_ref[:, column * LANES:(column + 1) * LANES] = jnp.where(row == column, 1.0, 0.0).astype(jnp.bfloat16)

    scale = scale_ref[...]
    narrow = scale[:, :columns].astype(jnp.bfloat16)
    for column in range(0, columns, 2):
        both = jnp.dot(
            narrow, spread_ref[:, column * LANES:(column + 2) * LANES], preferred_element_type=jnp.float32
        )
        wide_ref[column] = both[:, :LANES]
        wide_ref[column + 1] = both[:, LANES:]

    copy(step, slot).wait()
    flat = buffer_ref.reshape(2 * TILE * PITCH, LANES)
    base = slot * (TILE * PITCH)

    def rows(w, n, piece):
        start = base + (n * pieces + piece) * windows + w
        return flat[pl.ds(start, TILE, stride=PITCH), :].astype(jnp.float32)

    live = scale[:, windows * blocks:windows * blocks + 1]
    for w in range(windows):
        total = jnp.zeros((TILE, LANES), jnp.float32)
        for n in range(seg_count):
            for pair in range(pairs):
                column = w * blocks + n * pairs + pair
                one = rows(w, n, 2 * pair)
                two = rows(w, n, 2 * pair + 1)
                weight = wide_ref[column]
                total = total + (one * one + two * two) * (weight * weight)
        energy = jnp.sum(total, axis=1, keepdims=True) * (1.0 / (seg_count * SEG))
        factor = jnp.broadcast_to(live * lax.rsqrt(energy + 1e-06), (TILE, LANES))
        for n in range(seg_count):
            for pair in range(pairs):
                column = w * blocks + n * pairs + pair
                weight = wide_ref[column] * factor
                for piece in (2 * pair, 2 * pair + 1):
                    value = rows(w, n, piece) * weight
                    out_ref[w * seg_count + n, :, piece * LANES:(piece + 1) * LANES] = value.astype(jnp.bfloat16)


def normalize_half(half, samples_rows, scales, seg_count, windows):
    steps = HALF // TILE
    return pl.pallas_call(
        functools.partial(normalize_kernel, seg_count=seg_count, windows=windows),
        grid_spec=pltpu.PrefetchScalarGridSpec(
            num_scalar_prefetch=1,
            grid=(steps,),
            in_specs=[
                pl.BlockSpec(memory_space=pl.ANY),
                pl.BlockSpec((TILE, scales.shape[1]), lambda i, h: (h[0] * steps + i, 0)),
            ],
            out_specs=pl.BlockSpec((windows * seg_count, TILE, SEG), lambda i, h: (0, i, 0)),
            scratch_shapes=[
                pltpu.VMEM((2, TILE, PITCH, LANES), jnp.int32),
                pltpu.VMEM((scales.shape[1] - 1, (scales.shape[1] - 1) * LANES), jnp.bfloat16),
                pltpu.VMEM((scales.shape[1] - 1, TILE, LANES), jnp.float32),
                pltpu.SemaphoreType.DMA((2,)),
            ],
        ),
        out_shape=jax.ShapeDtypeStruct((windows * seg_count, HALF, SEG), jnp.bfloat16),
        name="normalize",
    )(half, samples_rows, scales)


def source_kernel(offsets_ref, samples_ref, scale_ref, out_ref, sorted_ref, buffer_ref, rows_ref, sems, *,
                  seg_count, windows):
    pieces = SEG // LANES
    pairs = pieces // 2
    blocks = seg_count * pairs
    per_channel = samples_ref.shape[1]
    given = [offsets_ref[j] for j in range(SOURCES)]
    ranks = []
    for j in range(SOURCES):
        rank = jnp.int32(0)
        for i in range(SOURCES):
            if i != j:
                ahead = given[i] <= given[j] if i < j else given[i] < given[j]
                rank = rank + jnp.where(ahead, 1, 0)
        ranks.append(rank)
    order = []
    for r in range(SOURCES):
        offset = jnp.int32(0)
        origin = jnp.int32(0)
        for j in range(SOURCES):
            hit = ranks[j] == r
            offset = jnp.where(hit, given[j], offset)
            origin = jnp.where(hit, j, origin)
        sorted_ref[r] = offset
        sorted_ref[SOURCES + r] = origin
        order.append(offset)
    copies = []
    for r in range(SOURCES):
        copy = pltpu.make_async_copy(
            samples_ref.at[order[r]], buffer_ref.at[r, pl.ds(0, per_channel), :], sems.at[r]
        )
        copy.start()
        copies.append(copy)
    channel = lax.broadcasted_iota(jnp.int32, scale_ref.shape, 0)
    lane = lax.broadcasted_iota(jnp.int32, (8, scale_ref.shape[1]), 1)
    segment = lax.broadcasted_iota(jnp.int32, (8, scale_ref.shape[1]), 0)
    valid = lax.broadcasted_iota(jnp.int32, (8, LANES), 0) < seg_count
    rows_ref[...] = jnp.zeros(rows_ref.shape, jnp.float32)
    for r in range(SOURCES):
        picked = jnp.sum(jnp.where(channel == order[r], scale_ref[...], 0.0), axis=0, keepdims=True)
        picked = jnp.broadcast_to(picked, (8, scale_ref.shape[1]))
        live = jnp.sum(jnp.where(lane == windows * blocks, picked, 0.0), axis=1, keepdims=True)
        copies[r].wait()
        for w in range(windows):
            parts = []
            total = jnp.zeros((8, LANES), jnp.float32)
            for pair in range(pairs):
                column = w * blocks + segment * pairs + pair
                weight = jnp.sum(jnp.where(lane == column, picked, 0.0), axis=1, keepdims=True)
                for piece in (2 * pair, 2 * pair + 1):
                    raw = buffer_ref[r, pl.ds(piece * windows + w, 8, stride=pieces * windows), :]
                    part = jnp.where(valid, raw.astype(jnp.float32), 0.0) * weight
                    total = total + part * part
                    parts.append(part)
            energy = jnp.sum(jnp.sum(total, axis=1, keepdims=True), axis=0, keepdims=True)
            factor = live * lax.rsqrt(energy * (1.0 / (seg_count * SEG)) + 1e-06)
            for piece in range(pieces):
                rows_ref[r, pl.ds(w * seg_count, seg_count), piece * LANES:(piece + 1) * LANES] = (
                    parts[piece] * factor
                )[:seg_count]
        rows_ref[r, pl.ds(windows * seg_count, 1), :] = jnp.full((1, SEG), 1, jnp.float32) * (
            order[r] + 1
        ).astype(jnp.float32)
        out_ref[r] = rows_ref[r].astype(jnp.bfloat16)


def source_rows(offsets, samples_rows, scales, seg_count, windows):
    return pl.pallas_call(
        functools.partial(source_kernel, seg_count=seg_count, windows=windows),
        grid_spec=pltpu.PrefetchScalarGridSpec(
            num_scalar_prefetch=1,
            grid=(1,),
            in_specs=[
                pl.BlockSpec(memory_space=pl.ANY),
                pl.BlockSpec(scales.shape, lambda i, h: (0, 0)),
            ],
            out_specs=[
                pl.BlockSpec((SOURCES, SLOT, SEG), lambda i, h: (0, 0, 0)),
                pl.BlockSpec(memory_space=pltpu.SMEM),
            ],
            scratch_shapes=[
                pltpu.VMEM((SOURCES, 128, LANES), jnp.int32),
                pltpu.VMEM((SOURCES, SLOT, SEG), jnp.float32),
                pltpu.SemaphoreType.DMA((SOURCES,)),
            ],
        ),
        out_shape=[
            jax.ShapeDtypeStruct((SOURCES, SLOT, SEG), jnp.bfloat16),
            jax.ShapeDtypeStruct((2 * SOURCES,), jnp.int32),
        ],
        name="sources",
    )(offsets, samples_rows, scales)


def cross_kernel(limits_ref, near_ref, far_ref, own_src_ref, above_src_ref, below_src_ref, table_ref,
                 own_ref, up_ref, down_ref, band_ref, src_ref, plus_ref, minus_ref):
    step = pl.program_id(0)
    count = near_ref.shape[0]
    groups = table_ref.shape[0]
    src_rows = 2 * SLOT

    @pl.when(step == 0)
    def _():
        for which, ref in enumerate((own_src_ref, above_src_ref, below_src_ref)):
            rows = ref[...].reshape(SOURCES * src_rows, SEG)
            at = pl.ds(which * SOURCES * src_rows, SOURCES * src_rows)
            for g in range(groups):
                spec = jnp.dot(rows, table_ref[g], preferred_element_type=jnp.float32)
                spec = spec.astype(jnp.bfloat16).astype(jnp.float32)
                real = spec[:, :LANES]
                imag = spec[:, LANES:]
                src_ref[g, at, :] = real
                plus_ref[g, at, :] = real + imag
                minus_ref[g, at, :] = imag - real

    for part, ref in ((0, near_ref), (1, far_ref)):
        rows = ref[...].reshape(count * TILE, SEG)
        at = pl.ds(part * count * TILE, count * TILE)
        for g in range(groups):
            spec = jnp.dot(rows, table_ref[g], preferred_element_type=jnp.float32)
            spec = spec.astype(jnp.bfloat16).astype(jnp.float32)
            band_ref[2 * g, at, :] = spec[:, :LANES]
            band_ref[2 * g + 1, at, :] = spec[:, LANES:]

    def products(which, members, out_ref, g, row):
        lane = pl.multiple_of(g * PAIR, PAIR)
        real_lanes = pl.ds(lane, LANES)
        imag_lanes = pl.ds(pl.multiple_of(lane + LANES, LANES), LANES)
        zero = jnp.zeros((8, LANES), jnp.float32)
        acc = {(t, j): [zero, zero, zero] for t in range(SUB // 8) for j in members}
        for q in range(2 * count):
            band = []
            for t in range(SUB // 8):
                at = pl.ds(q * TILE + row + 8 * t, 8)
                g_re = band_ref[2 * g, at, :]
                g_im = band_ref[2 * g + 1, at, :]
                band.append((g_re, g_im, g_re + g_im))
            spot = q if q < count else SLOT + q - count
            for j in members:
                at = pl.ds((which * SOURCES + j) * src_rows + spot, 8, stride=0)
                s_re = src_ref[g, at, :]
                s_plus = plus_ref[g, at, :]
                s_minus = minus_ref[g, at, :]
                for t in range(SUB // 8):
                    g_re, g_im, g_sum = band[t]
                    a = acc[t, j]
                    a[0] = a[0] + s_re * g_sum
                    a[1] = a[1] + s_minus * g_im
                    a[2] = a[2] + s_plus * g_re
        for j in members:
            real = jnp.concatenate([acc[t, j][0] + acc[t, j][1] for t in range(SUB // 8)], axis=0)
            imag = jnp.concatenate([acc[t, j][0] - acc[t, j][2] for t in range(SUB // 8)], axis=0)
            out_ref[j, pl.ds(row, SUB), real_lanes] = real.astype(out_ref.dtype)
            out_ref[j, pl.ds(row, SUB), imag_lanes] = imag.astype(out_ref.dtype)

    def tile(index, carry):
        g = index // (TILE // SUB)
        row = pl.multiple_of((index % (TILE // SUB)) * SUB, SUB)
        channel = limits_ref[0] + step * TILE + row
        for first in (0, 2):
            pair = (first, first + 1)

            @pl.when(channel + SUB > limits_ref[1 + first])
            def _():
                products(1, pair, up_ref, g, row)

            @pl.when(channel < limits_ref[1 + SOURCES + first + 1])
            def _():
                products(2, pair, down_ref, g, row)

        products(0, (0, 1, 2, 3), own_ref, g, row)
        return carry

    lax.fori_loop(0, groups * (TILE // SUB), tile, 0)


def cross_chunk(limits, near, far, own_src, above_src, below_src, table):
    count = near.shape[0]
    groups = table.shape[0]
    width = groups * PAIR
    src_rows = 3 * SOURCES * 2 * SLOT
    block = pl.BlockSpec((count, TILE, SEG), lambda i, h: (0, i, 0))
    src = pl.BlockSpec((SOURCES, 2 * SLOT, SEG), lambda i, h: (0, 0, 0))
    result = pl.BlockSpec((SOURCES, TILE, width), lambda i, h: (0, i, 0))
    return pl.pallas_call(
        cross_kernel,
        grid_spec=pltpu.PrefetchScalarGridSpec(
            num_scalar_prefetch=1,
            grid=(HALF // TILE,),
            in_specs=[block, block, src, src, src, pl.BlockSpec((groups, SEG, PAIR), lambda i, h: (0, 0, 0))],
            out_specs=[result, result, result],
            scratch_shapes=[
                pltpu.VMEM((2 * groups, 2 * count * TILE, LANES), jnp.float32),
                pltpu.VMEM((groups, src_rows, LANES), jnp.float32),
                pltpu.VMEM((groups, src_rows, LANES), jnp.float32),
                pltpu.VMEM((groups, src_rows, LANES), jnp.float32),
            ],
        ),
        out_shape=[
            jax.ShapeDtypeStruct((SOURCES, HALF, width), jnp.float32),
            jax.ShapeDtypeStruct((SOURCES, HALF, width), jnp.bfloat16),
            jax.ShapeDtypeStruct((SOURCES, HALF, width), jnp.bfloat16),
        ],
        name="cross",
    )(limits, near, far, own_src, above_src, below_src, table)


def select_rows(below_source, keep, own, from_below, from_above):
    other = jnp.where(below_source, from_above, from_below)
    kept = jnp.where(keep, own, other.astype(jnp.float32))
    return kept, jnp.where(keep, other, own.astype(jnp.bfloat16))


def turned(ordered_ref, mine_ref, mate_ref, top_ref, halve):
    source_row = lax.broadcasted_iota(jnp.int32, (HALF, 2 * HALF), 1)
    target_row = lax.broadcasted_iota(jnp.int32, (HALF, 2 * HALF), 0)
    for j in range(SOURCES):
        wanted = target_row + ordered_ref[j]
        wanted = jnp.where(wanted >= 2 * HALF, wanted - 2 * HALF, wanted)
        turn = jnp.where(source_row == wanted, 1.0, 0.0).astype(jnp.bfloat16)
        rows = jnp.concatenate([mine_ref[j], mate_ref[j]], axis=0)
        top_ref[pl.ds(j * HALF, HALF), :] = jnp.dot(turn, rows, preferred_element_type=jnp.float32).astype(
            jnp.bfloat16
        )
    if halve:
        lane = lax.broadcasted_iota(jnp.int32, (SOURCES * HALF, LANES), 1)
        first = top_ref[:, :LANES].astype(jnp.float32)
        top_ref[:, :LANES] = jnp.where(lane == 0, 0.5 * first, first).astype(jnp.bfloat16)


def folded(top_ref, hi_ref, lo_ref, first, sums):
    for g in range(hi_ref.shape[0]):
        rows = top_ref[:, g * PAIR:(g + 1) * PAIR]
        for table in (hi_ref[g], lo_ref[g]):
            part = lax.dot_general(rows, table, (((1,), (1,)), ((), ())), preferred_element_type=jnp.float32)
            parity = (first + g) % 2
            sums[parity] = part if sums[parity] is None else sums[parity] + part


def early_kernel(ordered_ref, *refs, firsts):
    count = len(firsts)
    even_ref, odd_ref = refs[4 * count:4 * count + 2]
    tops = refs[4 * count + 2:]

    @pl.when(pl.program_id(0) == 0)
    def _():
        for c, first in enumerate(firsts):
            turned(ordered_ref, refs[4 * c], refs[4 * c + 1], tops[c], first == 0)

    sums = [None, None]
    for c, first in enumerate(firsts):
        folded(tops[c], refs[4 * c + 2], refs[4 * c + 3], first, sums)
    even_ref[...] = sums[0]
    odd_ref[...] = sums[1]


def chunk_specs(groups):
    rows = pl.BlockSpec((SOURCES, HALF, groups * PAIR), lambda m, h: (0, 0, 0))
    table = pl.BlockSpec((groups, COLS, PAIR), lambda m, h: (0, m, 0))
    return [rows, rows, table, table]


def early_inverse(ordered, parts, firsts):
    specs, operands, tops = [], [], []
    for part in parts:
        groups = part[2].shape[0]
        specs += chunk_specs(groups)
        operands += list(part)
        tops.append(pltpu.VMEM((SOURCES * HALF, groups * PAIR), jnp.bfloat16))
    block = pl.BlockSpec((SOURCES * HALF, COLS), lambda m, h: (0, m))
    shape = jax.ShapeDtypeStruct((SOURCES * HALF, SEG), jnp.float32)
    return pl.pallas_call(
        functools.partial(early_kernel, firsts=firsts),
        grid_spec=pltpu.PrefetchScalarGridSpec(
            num_scalar_prefetch=1,
            grid=(SEG // COLS,),
            in_specs=specs,
            out_specs=[block, block],
            scratch_shapes=tops,
        ),
        out_shape=[shape, shape],
        name="early",
    )(ordered, *operands)


def last_kernel(ordered_ref, mine_ref, mate_ref, hi_ref, lo_ref, even_ref, odd_ref, out_ref, top_ref, stage_ref, sem,
                *, first, scale):
    m = pl.program_id(0)

    @pl.when(m == 0)
    def _():
        turned(ordered_ref, mine_ref, mate_ref, top_ref, first == 0)

    sums = [even_ref[...], odd_ref[...]]
    folded(top_ref, hi_ref, lo_ref, first, sums)
    stage_ref[m, 0] = (sums[0] - sums[1]) * scale
    stage_ref[m, 1] = (sums[0] + sums[1]) * scale

    def copy(step, side, j):
        lane = pl.multiple_of(side * SEG + step * COLS, COLS)
        return pltpu.make_async_copy(
            stage_ref.at[step, side, pl.ds(j * HALF, HALF), :],
            out_ref.at[ordered_ref[SOURCES + j], :, pl.ds(lane, COLS)],
            sem.at[step, side, j],
        )

    for side in range(2):
        for j in range(SOURCES):
            copy(m, side, j).start()

    @pl.when(m == pl.num_programs(0) - 1)
    def _():
        for step in range(SEG // COLS):
            for side in range(2):
                for j in range(SOURCES):
                    copy(step, side, j).wait()


def last_inverse(ordered, part, even, odd, first, scale):
    groups = part[2].shape[0]
    block = pl.BlockSpec((SOURCES * HALF, COLS), lambda m, h: (0, m))
    return pl.pallas_call(
        functools.partial(last_kernel, first=first, scale=scale),
        grid_spec=pltpu.PrefetchScalarGridSpec(
            num_scalar_prefetch=1,
            grid=(SEG // COLS,),
            in_specs=chunk_specs(groups) + [block, block],
            out_specs=pl.BlockSpec(memory_space=pl.ANY),
            scratch_shapes=[
                pltpu.VMEM((SOURCES * HALF, groups * PAIR), jnp.bfloat16),
                pltpu.VMEM((SEG // COLS, 2, SOURCES * HALF, COLS), jnp.float32),
                pltpu.SemaphoreType.DMA((SEG // COLS, 2, SOURCES)),
            ],
        ),
        out_shape=jax.ShapeDtypeStruct((SOURCES, HALF, 2 * SEG), jnp.float32),
        name="last",
    )(ordered, *part, even, odd)


def block_scale(exponents):
    levels = jnp.arange(5, dtype=jnp.int32)
    powers = jnp.exp2(levels.astype(jnp.float32))
    return jnp.sum(jnp.where(exponents[..., None] == levels, powers, 0.0), axis=-1)


def passed_along(block, axis, distance):
    devices = range(lax.axis_size(axis))
    route = [(i - distance, i) for i in devices if i - distance in devices]
    return lax.ppermute(block, axis, route)


def partner(block, bit):
    return lax.ppermute(block, "win", [(i, i ^ bit) for i in range(lax.axis_size("win"))])


def pipeline(samples, exponents, alive, offsets):
    channels, windows, length = samples.shape
    seg_count = length // SEG
    place = lax.axis_index("win")
    core = place & 1
    upper_half = place >> 1

    samples_rows = samples.reshape(channels, windows, length // LANES, LANES)
    samples_rows = samples_rows.transpose(0, 2, 1, 3).reshape(channels, windows * (length // LANES), LANES)
    scales = block_scale(exponents).reshape(channels, -1)
    scales = jnp.concatenate([scales, alive.astype(jnp.float32).reshape(channels, 1)], axis=1)

    own_src, ordered = source_rows(offsets, samples_rows, scales, seg_count, windows)
    mate_src = partner(own_src, 1)
    own_src = jnp.concatenate([own_src, mate_src], axis=1)
    above_src = passed_along(own_src, "chan", -1)
    below_src = passed_along(own_src, "chan", 1)

    sent = normalize_half((1 - core).reshape(1), samples_rows, scales, seg_count, windows)
    far = partner(sent, 1)
    near = normalize_half(core.reshape(1), samples_rows, scales, seg_count, windows)
    coarse, fine = (jnp.asarray(t) for t in small_tables())

    flag = windows * seg_count
    above_off = above_src[:, flag, 0].astype(jnp.int32)
    below_off = below_src[:, flag, 0].astype(jnp.int32)
    limits = jnp.concatenate(
        [(core * HALF).reshape(1), jnp.where(above_off == 0, channels, above_off - 1), below_off - 1]
    ).astype(jnp.int32)
    index = core * HALF + jnp.arange(HALF, dtype=jnp.int32)
    below_source = (index[None, :] < ordered[:SOURCES, None])[:, :, None]
    keep = below_source == (upper_half == 0)
    scale = 2.0 / float(2 * SEG * windows * lax.axis_size("win") * seg_count * SEG)

    tables = []
    for first, count in CHUNKS:
        tables.append(make_tables(first, count, coarse, fine))
    crossed, returned, selected = [], [], []

    def select(c):
        pieces = (crossed[c],) + returned[c]
        if c:
            pieces = lax.optimization_barrier(pieces + (selected[c - 1][0],))[:3]
        kept, moved = select_rows(below_source, keep, *pieces)
        selected.append((kept, partner(moved, 2)))

    for c in range(len(CHUNKS)):
        own, to_above, to_below = cross_chunk(limits, near, far, own_src, above_src, below_src, tables[c][0])
        crossed.append(own)
        from_below = passed_along(to_above, "chan", 1)
        from_above = passed_along(to_below, "chan", -1)
        returned.append((from_below, from_above))
    for c in range(len(CHUNKS)):
        select(c)
    parts = []
    for c in range(len(CHUNKS)):
        kept, moved = selected[c]
        if c:
            kept = lax.optimization_barrier((kept, parts[c - 1][0]))[0]
        total = (kept + moved.astype(jnp.float32)).astype(jnp.bfloat16)
        mate = partner(total, 1)
        parts.append((total, mate) + tuple(tables[c]))
    firsts = tuple(first for first, _ in CHUNKS)
    even, odd = early_inverse(ordered, parts[:-1], firsts[:-1])
    return last_inverse(ordered, parts[-1], even, odd, firsts[-1], scale)


def solution(mesh):
    placed = (P("chan", "win", None), P("chan", "win", None), P("chan"), P("chan"))
    return jax.shard_map(pipeline, mesh=mesh, in_specs=placed, out_specs=P("chan", "win", None), check_vma=False)
```

```python
import functools
import math

import jax
import jax.numpy as jnp
import numpy as np
from jax import lax
from jax.experimental import pallas as pl
from jax.experimental.pallas import tpu as pltpu
from jax.sharding import PartitionSpec as P


SEG = 1024
HALF = 96
LANES = 128
GROUPS = SEG // LANES
PAIR = 2 * LANES
CHUNKS = ((0, 4), (4, 4))
FOLD = 32
UNROLL = 4
TILE = 32
SUB = 16
PITCH = 104
SOURCES = 4
SLOT = 16
SEGMENTS = 12
COLS = 256


def small_tables():
    k = GROUPS * np.arange(LANES)[None, :] + np.arange(GROUPS)[:, None]
    step = np.arange(FOLD)

    def waves(stride):
        phase = (stride * step[None, :, None] * k[:, None, :]) % (2 * SEG)
        angle = phase * (2.0 * math.pi / (2 * SEG))
        return np.stack([np.cos(angle), np.sin(angle)], axis=1).astype(np.float32)

    return waves(FOLD), waves(1)


def table_kernel(coarse_ref, fine_ref, out_ref, *, rest):
    fine_cos = fine_ref[0, 0]
    fine_sin = fine_ref[0, 1]

    def row_block(step, carry):
        for inner in range(UNROLL):
            a = step * UNROLL + inner
            base_cos = coarse_ref[0, 0, pl.ds(a, 8, stride=0), :]
            base_sin = coarse_ref[0, 1, pl.ds(a, 8, stride=0), :]
            base_cos = jnp.concatenate([base_cos] * (FOLD // 8), axis=0)
            base_sin = jnp.concatenate([base_sin] * (FOLD // 8), axis=0)
            real = base_cos * fine_cos - base_sin * fine_sin
            imag = -(base_sin * fine_cos + base_cos * fine_sin)
            rows = pl.ds(pl.multiple_of(a * FOLD, FOLD), FOLD)
            for part, lane in ((real, 0), (imag, LANES)):
                top = part.astype(jnp.bfloat16)
                if rest:
                    top = (part - top.astype(jnp.float32)).astype(jnp.bfloat16)
                out_ref[0, rows, lane:lane + LANES] = top
        return carry

    lax.fori_loop(0, FOLD // UNROLL, row_block, 0)


def make_tables(first, count, coarse, fine, rest=False):
    shape = jax.ShapeDtypeStruct((count, SEG, PAIR), jnp.bfloat16)
    small = pl.BlockSpec((1, 2, FOLD, LANES), lambda p: (first + p, 0, 0, 0))
    large = pl.BlockSpec((1, SEG, PAIR), lambda p: (p, 0, 0))
    return pl.pallas_call(
        functools.partial(table_kernel, rest=rest),
        grid=(count,),
        in_specs=[small, small],
        out_specs=large,
        out_shape=shape,
        name="tables",
    )(coarse, fine)


def normalize_kernel(half_ref, samples_ref, scale_ref, out_ref, buffer_ref, spread_ref, wide_ref, sems, *,
                     seg_count, windows):
    step = pl.program_id(0)
    steps = pl.num_programs(0)
    per_channel = samples_ref.shape[1]
    pieces = SEG // LANES
    pairs = pieces // 2
    blocks = seg_count * pairs
    slot = step % 2

    def copy(at, into):
        first = half_ref[0] * HALF + at * TILE
        return pltpu.make_async_copy(
            samples_ref.at[pl.ds(first, TILE)],
            buffer_ref.at[into, :, pl.ds(0, per_channel), :],
            sems.at[into],
        )

    @pl.when(step == 0)
    def _():
        copy(0, 0).start()

    @pl.when(step + 1 < steps)
    def _():
        copy(step + 1, 1 - slot).start()

    columns = wide_ref.shape[0]

    @pl.when(step == 0)
    def _():
        for column in range(columns):
            row = lax.broadcasted_iota(jnp.int32, (columns, LANES), 0)
            spread_ref[:, column * LANES:(column + 1) * LANES] = jnp.where(row == column, 1.0, 0.0).astype(jnp.bfloat16)

    scale = scale_ref[...]
    narrow = scale[:, :columns].astype(jnp.bfloat16)
    for column in range(0, columns, 2):
        both = jnp.dot(
            narrow, spread_ref[:, column * LANES:(column + 2) * LANES], preferred_element_type=jnp.float32
        )
        wide_ref[column] = both[:, :LANES]
        wide_ref[column + 1] = both[:, LANES:]

    copy(step, slot).wait()
    flat = buffer_ref.reshape(2 * TILE * PITCH, LANES)
    base = slot * (TILE * PITCH)

    def rows(w, n, piece):
        start = base + (n * pieces + piece) * windows + w
        return flat[pl.ds(start, TILE, stride=PITCH), :].astype(jnp.float32)

    live = scale[:, windows * blocks:windows * blocks + 1]
    for w in range(windows):
        total = jnp.zeros((TILE, LANES), jnp.float32)
        for n in range(seg_count):
            for pair in range(pairs):
                column = w * blocks + n * pairs + pair
                one = rows(w, n, 2 * pair)
                two = rows(w, n, 2 * pair + 1)
                weight = wide_ref[column]
                total = total + (one * one + two * two) * (weight * weight)
        energy = jnp.sum(total, axis=1, keepdims=True) * (1.0 / (seg_count * SEG))
        factor = jnp.broadcast_to(live * lax.rsqrt(energy + 1e-06), (TILE, LANES))
        for n in range(seg_count):
            for pair in range(pairs):
                column = w * blocks + n * pairs + pair
                weight = wide_ref[column] * factor
                for piece in (2 * pair, 2 * pair + 1):
                    value = rows(w, n, piece) * weight
                    out_ref[w * seg_count + n, :, piece * LANES:(piece + 1) * LANES] = value.astype(jnp.bfloat16)


def normalize_half(half, samples_rows, scales, seg_count, windows):
    steps = HALF // TILE
    return pl.pallas_call(
        functools.partial(normalize_kernel, seg_count=seg_count, windows=windows),
        grid_spec=pltpu.PrefetchScalarGridSpec(
            num_scalar_prefetch=1,
            grid=(steps,),
            in_specs=[
                pl.BlockSpec(memory_space=pl.ANY),
                pl.BlockSpec((TILE, scales.shape[1]), lambda i, h: (h[0] * steps + i, 0)),
            ],
            out_specs=pl.BlockSpec((windows * seg_count, TILE, SEG), lambda i, h: (0, i, 0)),
            scratch_shapes=[
                pltpu.VMEM((2, TILE, PITCH, LANES), jnp.int32),
                pltpu.VMEM((scales.shape[1] - 1, (scales.shape[1] - 1) * LANES), jnp.bfloat16),
                pltpu.VMEM((scales.shape[1] - 1, TILE, LANES), jnp.float32),
                pltpu.SemaphoreType.DMA((2,)),
            ],
        ),
        out_shape=jax.ShapeDtypeStruct((windows * seg_count, HALF, SEG), jnp.bfloat16),
        name="normalize",
    )(half, samples_rows, scales)


def source_kernel(offsets_ref, samples_ref, scale_ref, out_ref, sorted_ref, buffer_ref, rows_ref, sems, *,
                  seg_count, windows):
    pieces = SEG // LANES
    pairs = pieces // 2
    blocks = seg_count * pairs
    per_channel = samples_ref.shape[1]
    given = [offsets_ref[j] for j in range(SOURCES)]
    ranks = []
    for j in range(SOURCES):
        rank = jnp.int32(0)
        for i in range(SOURCES):
            if i != j:
                ahead = given[i] <= given[j] if i < j else given[i] < given[j]
                rank = rank + jnp.where(ahead, 1, 0)
        ranks.append(rank)
    order = []
    for r in range(SOURCES):
        offset = jnp.int32(0)
        origin = jnp.int32(0)
        for j in range(SOURCES):
            hit = ranks[j] == r
            offset = jnp.where(hit, given[j], offset)
            origin = jnp.where(hit, j, origin)
        sorted_ref[r] = offset
        sorted_ref[SOURCES + r] = origin
        order.append(offset)
    copies = []
    for r in range(SOURCES):
        copy = pltpu.make_async_copy(
            samples_ref.at[order[r]], buffer_ref.at[r, pl.ds(0, per_channel), :], sems.at[r]
        )
        copy.start()
        copies.append(copy)
    channel = lax.broadcasted_iota(jnp.int32, scale_ref.shape, 0)
    lane = lax.broadcasted_iota(jnp.int32, (8, scale_ref.shape[1]), 1)
    segment = lax.broadcasted_iota(jnp.int32, (8, scale_ref.shape[1]), 0)
    valid = lax.broadcasted_iota(jnp.int32, (8, LANES), 0) < seg_count
    rows_ref[...] = jnp.zeros(rows_ref.shape, jnp.float32)
    for r in range(SOURCES):
        picked = jnp.sum(jnp.where(channel == order[r], scale_ref[...], 0.0), axis=0, keepdims=True)
        picked = jnp.broadcast_to(picked, (8, scale_ref.shape[1]))
        live = jnp.sum(jnp.where(lane == windows * blocks, picked, 0.0), axis=1, keepdims=True)
        copies[r].wait()
        for w in range(windows):
            parts = []
            total = jnp.zeros((8, LANES), jnp.float32)
            for pair in range(pairs):
                column = w * blocks + segment * pairs + pair
                weight = jnp.sum(jnp.where(lane == column, picked, 0.0), axis=1, keepdims=True)
                for piece in (2 * pair, 2 * pair + 1):
                    raw = buffer_ref[r, pl.ds(piece * windows + w, 8, stride=pieces * windows), :]
                    part = jnp.where(valid, raw.astype(jnp.float32), 0.0) * weight
                    total = total + part * part
                    parts.append(part)
            energy = jnp.sum(jnp.sum(total, axis=1, keepdims=True), axis=0, keepdims=True)
            factor = live * lax.rsqrt(energy * (1.0 / (seg_count * SEG)) + 1e-06)
            for piece in range(pieces):
                rows_ref[r, pl.ds(w * seg_count, seg_count), piece * LANES:(piece + 1) * LANES] = (
                    parts[piece] * factor
                )[:seg_count]
        rows_ref[r, pl.ds(windows * seg_count, 1), :] = jnp.full((1, SEG), 1, jnp.float32) * (
            order[r] + 1
        ).astype(jnp.float32)
        out_ref[r] = rows_ref[r].astype(jnp.bfloat16)


def source_rows(offsets, samples_rows, scales, seg_count, windows):
    return pl.pallas_call(
        functools.partial(source_kernel, seg_count=seg_count, windows=windows),
        grid_spec=pltpu.PrefetchScalarGridSpec(
            num_scalar_prefetch=1,
            grid=(1,),
            in_specs=[
                pl.BlockSpec(memory_space=pl.ANY),
                pl.BlockSpec(scales.shape, lambda i, h: (0, 0)),
            ],
            out_specs=[
                pl.BlockSpec((SOURCES, SLOT, SEG), lambda i, h: (0, 0, 0)),
                pl.BlockSpec(memory_space=pltpu.SMEM),
            ],
            scratch_shapes=[
                pltpu.VMEM((SOURCES, 128, LANES), jnp.int32),
                pltpu.VMEM((SOURCES, SLOT, SEG), jnp.float32),
                pltpu.SemaphoreType.DMA((SOURCES,)),
            ],
        ),
        out_shape=[
            jax.ShapeDtypeStruct((SOURCES, SLOT, SEG), jnp.bfloat16),
            jax.ShapeDtypeStruct((2 * SOURCES,), jnp.int32),
        ],
        name="sources",
    )(offsets, samples_rows, scales)


def products(band_ref, sources, base, members, out_ref, g, row):
    src_ref, plus_ref, minus_ref = sources
    count = SEGMENTS
    lane = pl.multiple_of(g * PAIR, PAIR)
    real_lanes = pl.ds(lane, LANES)
    imag_lanes = pl.ds(pl.multiple_of(lane + LANES, LANES), LANES)
    zero = jnp.zeros((8, LANES), jnp.float32)
    acc = {(t, j): [zero, zero, zero] for t in range(SUB // 8) for j in members}
    for q in range(2 * count):
        band = []
        for t in range(SUB // 8):
            at = pl.ds(q * TILE + row + 8 * t, 8)
            g_re = band_ref[2 * g, at, :]
            g_im = band_ref[2 * g + 1, at, :]
            band.append((g_re, g_im, g_re + g_im))
        spot = q if q < count else SLOT + q - count
        for j in members:
            at = pl.ds(base + j * 2 * SLOT + spot, 8, stride=0)
            s_re = src_ref[g, at, :]
            s_plus = plus_ref[g, at, :]
            s_minus = minus_ref[g, at, :]
            for t in range(SUB // 8):
                g_re, g_im, g_sum = band[t]
                a = acc[t, j]
                a[0] = a[0] + s_re * g_sum
                a[1] = a[1] + s_minus * g_im
                a[2] = a[2] + s_plus * g_re
    for j in members:
        real = jnp.concatenate([acc[t, j][0] + acc[t, j][1] for t in range(SUB // 8)], axis=0)
        imag = jnp.concatenate([acc[t, j][0] - acc[t, j][2] for t in range(SUB // 8)], axis=0)
        out_ref[j, pl.ds(row, SUB), real_lanes] = real.astype(out_ref.dtype)
        out_ref[j, pl.ds(row, SUB), imag_lanes] = imag.astype(out_ref.dtype)


def outer_kernel(limits_ref, near_ref, far_ref, own_src_ref, above_src_ref, below_src_ref, table_ref,
                 up_ref, down_ref, band_ref, own_re_ref, own_plus_ref, own_minus_ref, src_ref, plus_ref, minus_ref):
    step = pl.program_id(0)
    count = near_ref.shape[0]
    groups = table_ref.shape[0]
    src_rows = 2 * SLOT
    per_side = SOURCES * src_rows

    @pl.when(step == 0)
    def _():
        scratch = (src_ref, plus_ref, minus_ref)
        for ref, base, into in (
            (own_src_ref, 0, (own_re_ref, own_plus_ref, own_minus_ref)),
            (above_src_ref, 0, scratch),
            (below_src_ref, per_side, scratch),
        ):
            rows = ref[...].reshape(per_side, SEG)
            at = pl.ds(base, per_side)
            for g in range(groups):
                spec = jnp.dot(rows, table_ref[g], preferred_element_type=jnp.float32)
                spec = spec.astype(jnp.bfloat16).astype(jnp.float32)
                real = spec[:, :LANES]
                imag = spec[:, LANES:]
                into[0][g, at, :] = real
                into[1][g, at, :] = real + imag
                into[2][g, at, :] = imag - real

    for part, ref in ((0, near_ref), (1, far_ref)):
        rows = ref[...].reshape(count * TILE, SEG)
        at = pl.ds(part * count * TILE, count * TILE)
        for g in range(groups):
            spec = jnp.dot(rows, table_ref[g], preferred_element_type=jnp.float32)
            spec = spec.astype(jnp.bfloat16).astype(jnp.float32)
            band_ref[2 * g, at, :] = spec[:, :LANES]
            band_ref[2 * g + 1, at, :] = spec[:, LANES:]

    def tile(index, carry):
        g = index // (TILE // SUB)
        row = pl.multiple_of((index % (TILE // SUB)) * SUB, SUB)
        channel = limits_ref[0] + step * TILE + row
        sources = (src_ref, plus_ref, minus_ref)
        for first in (0, 2):
            pair = (first, first + 1)

            @pl.when(channel + SUB > limits_ref[1 + first])
            def _():
                products(band_ref, sources, 0, pair, up_ref, g, row)

            @pl.when(channel < limits_ref[1 + SOURCES + first + 1])
            def _():
                products(band_ref, sources, per_side, pair, down_ref, g, row)

        return carry

    lax.fori_loop(0, groups * (TILE // SUB), tile, 0)


def own_kernel(band_ref, src_ref, plus_ref, minus_ref, out_ref):
    groups = src_ref.shape[0]

    def tile(index, carry):
        g = index // (TILE // SUB)
        row = pl.multiple_of((index % (TILE // SUB)) * SUB, SUB)
        for first in (0, 2):
            products(band_ref, (src_ref, plus_ref, minus_ref), 0, (first, first + 1), out_ref, g, row)
        return carry

    lax.fori_loop(0, groups * (TILE // SUB), tile, 0)


def outer_chunk(limits, near, far, own_src, above_src, below_src, table):
    count = near.shape[0]
    groups = table.shape[0]
    width = groups * PAIR
    per_side = SOURCES * 2 * SLOT
    steps = HALF // TILE
    band_rows = 2 * count * TILE
    block = pl.BlockSpec((count, TILE, SEG), lambda i, h: (0, i, 0))
    src = pl.BlockSpec((SOURCES, 2 * SLOT, SEG), lambda i, h: (0, 0, 0))
    result = pl.BlockSpec((SOURCES, TILE, width), lambda i, h: (0, i, 0))
    spectra = pl.BlockSpec((groups, per_side, LANES), lambda i, h: (0, 0, 0))
    returned = jax.ShapeDtypeStruct((SOURCES, HALF, width), jnp.bfloat16)
    own = jax.ShapeDtypeStruct((groups, per_side, LANES), jnp.float32)
    return pl.pallas_call(
        outer_kernel,
        grid_spec=pltpu.PrefetchScalarGridSpec(
            num_scalar_prefetch=1,
            grid=(steps,),
            in_specs=[block, block, src, src, src, pl.BlockSpec((groups, SEG, PAIR), lambda i, h: (0, 0, 0))],
            out_specs=[
                result,
                result,
                pl.BlockSpec((2 * groups, band_rows, LANES), lambda i, h: (0, i, 0)),
                spectra,
                spectra,
                spectra,
            ],
            scratch_shapes=[pltpu.VMEM((groups, 2 * per_side, LANES), jnp.float32)] * 3,
        ),
        out_shape=[
            returned,
            returned,
            jax.ShapeDtypeStruct((2 * groups, steps * band_rows, LANES), jnp.float32),
            own,
            own,
            own,
        ],
        name="outer",
    )(limits, near, far, own_src, above_src, below_src, table)


def own_chunk(band, src, plus, minus):
    groups, per_side, _ = src.shape
    steps = HALF // TILE
    width = groups * PAIR
    spectra = pl.BlockSpec((groups, per_side, LANES), lambda i: (0, 0, 0))
    return pl.pallas_call(
        own_kernel,
        grid=(steps,),
        in_specs=[pl.BlockSpec((2 * groups, band.shape[1] // steps, LANES), lambda i: (0, i, 0)), spectra, spectra, spectra],
        out_specs=pl.BlockSpec((SOURCES, TILE, width), lambda i: (0, i, 0)),
        out_shape=jax.ShapeDtypeStruct((SOURCES, HALF, width), jnp.float32),
        name="own",
    )(band, src, plus, minus)


def select_rows(below_source, keep, own, from_below, from_above):
    other = jnp.where(below_source, from_above, from_below)
    kept = jnp.where(keep, own, other.astype(jnp.float32))
    return kept, jnp.where(keep, other, own.astype(jnp.bfloat16))


def turned(ordered_ref, mine_ref, mate_ref, top_ref, halve):
    source_row = lax.broadcasted_iota(jnp.int32, (HALF, 2 * HALF), 1)
    target_row = lax.broadcasted_iota(jnp.int32, (HALF, 2 * HALF), 0)
    for j in range(SOURCES):
        wanted = target_row + ordered_ref[j]
        wanted = jnp.where(wanted >= 2 * HALF, wanted - 2 * HALF, wanted)
        turn = jnp.where(source_row == wanted, 1.0, 0.0).astype(jnp.bfloat16)
        rows = jnp.concatenate([mine_ref[j], mate_ref[j]], axis=0)
        top_ref[pl.ds(j * HALF, HALF), :] = jnp.dot(turn, rows, preferred_element_type=jnp.float32).astype(
            jnp.bfloat16
        )
    if halve:
        lane = lax.broadcasted_iota(jnp.int32, (SOURCES * HALF, LANES), 1)
        first = top_ref[:, :LANES].astype(jnp.float32)
        top_ref[:, :LANES] = jnp.where(lane == 0, 0.5 * first, first).astype(jnp.bfloat16)


def folded(top_ref, hi_ref, lo_ref, first, sums):
    for g in range(hi_ref.shape[0]):
        rows = top_ref[:, g * PAIR:(g + 1) * PAIR]
        for table in (hi_ref[g], lo_ref[g]):
            part = lax.dot_general(rows, table, (((1,), (1,)), ((), ())), preferred_element_type=jnp.float32)
            parity = (first + g) % 2
            sums[parity] = part if sums[parity] is None else sums[parity] + part


def early_kernel(ordered_ref, *refs, firsts):
    count = len(firsts)
    even_ref, odd_ref = refs[4 * count:4 * count + 2]
    tops = refs[4 * count + 2:]

    @pl.when(pl.program_id(0) == 0)
    def _():
        for c, first in enumerate(firsts):
            turned(ordered_ref, refs[4 * c], refs[4 * c + 1], tops[c], first == 0)

    sums = [None, None]
    for c, first in enumerate(firsts):
        folded(tops[c], refs[4 * c + 2], refs[4 * c + 3], first, sums)
    even_ref[...] = sums[0]
    odd_ref[...] = sums[1]


def chunk_specs(groups, first):
    assert first % groups == 0
    rows = pl.BlockSpec((SOURCES, HALF, groups * PAIR), lambda m, h: (0, 0, 0))
    table = pl.BlockSpec((groups, COLS, PAIR), lambda m, h: (0, m, 0))
    rest = pl.BlockSpec((groups, COLS, PAIR), lambda m, h: (first // groups, m, 0))
    return [rows, rows, table, rest]


def early_inverse(ordered, parts, firsts):
    specs, operands, tops = [], [], []
    for part, first in zip(parts, firsts):
        groups = part[2].shape[0]
        specs += chunk_specs(groups, first)
        operands += list(part)
        tops.append(pltpu.VMEM((SOURCES * HALF, groups * PAIR), jnp.bfloat16))
    block = pl.BlockSpec((SOURCES * HALF, COLS), lambda m, h: (0, m))
    shape = jax.ShapeDtypeStruct((SOURCES * HALF, SEG), jnp.float32)
    return pl.pallas_call(
        functools.partial(early_kernel, firsts=firsts),
        grid_spec=pltpu.PrefetchScalarGridSpec(
            num_scalar_prefetch=1,
            grid=(SEG // COLS,),
            in_specs=specs,
            out_specs=[block, block],
            scratch_shapes=tops,
        ),
        out_shape=[shape, shape],
        name="early",
    )(ordered, *operands)


def last_kernel(ordered_ref, mine_ref, mate_ref, hi_ref, lo_ref, even_ref, odd_ref, out_ref, top_ref, stage_ref, sem,
                *, first, scale):
    m = pl.program_id(0)

    @pl.when(m == 0)
    def _():
        turned(ordered_ref, mine_ref, mate_ref, top_ref, first == 0)

    sums = [even_ref[...], odd_ref[...]]
    folded(top_ref, hi_ref, lo_ref, first, sums)
    stage_ref[m, 0] = (sums[0] - sums[1]) * scale
    stage_ref[m, 1] = (sums[0] + sums[1]) * scale

    def copy(step, side, j):
        lane = pl.multiple_of(side * SEG + step * COLS, COLS)
        return pltpu.make_async_copy(
            stage_ref.at[step, side, pl.ds(j * HALF, HALF), :],
            out_ref.at[ordered_ref[SOURCES + j], :, pl.ds(lane, COLS)],
            sem.at[step, side, j],
        )

    for side in range(2):
        for j in range(SOURCES):
            copy(m, side, j).start()

    @pl.when(m == pl.num_programs(0) - 1)
    def _():
        for step in range(SEG // COLS):
            for side in range(2):
                for j in range(SOURCES):
                    copy(step, side, j).wait()


def last_inverse(ordered, part, even, odd, first, scale):
    groups = part[2].shape[0]
    block = pl.BlockSpec((SOURCES * HALF, COLS), lambda m, h: (0, m))
    return pl.pallas_call(
        functools.partial(last_kernel, first=first, scale=scale),
        grid_spec=pltpu.PrefetchScalarGridSpec(
            num_scalar_prefetch=1,
            grid=(SEG // COLS,),
            in_specs=chunk_specs(groups, first) + [block, block],
            out_specs=pl.BlockSpec(memory_space=pl.ANY),
            scratch_shapes=[
                pltpu.VMEM((SOURCES * HALF, groups * PAIR), jnp.bfloat16),
                pltpu.VMEM((SEG // COLS, 2, SOURCES * HALF, COLS), jnp.float32),
                pltpu.SemaphoreType.DMA((SEG // COLS, 2, SOURCES)),
            ],
        ),
        out_shape=jax.ShapeDtypeStruct((SOURCES, HALF, 2 * SEG), jnp.float32),
        name="last",
    )(ordered, *part, even, odd)


def block_scale(exponents):
    levels = jnp.arange(5, dtype=jnp.int32)
    powers = jnp.exp2(levels.astype(jnp.float32))
    return jnp.sum(jnp.where(exponents[..., None] == levels, powers, 0.0), axis=-1)


def passed_along(block, axis, distance):
    devices = range(lax.axis_size(axis))
    route = [(i - distance, i) for i in devices if i - distance in devices]
    return lax.ppermute(block, axis, route)


def partner(block, bit):
    return lax.ppermute(block, "win", [(i, i ^ bit) for i in range(lax.axis_size("win"))])


def pipeline(samples, exponents, alive, offsets):
    channels, windows, length = samples.shape
    seg_count = length // SEG
    place = lax.axis_index("win")
    core = place & 1
    upper_half = place >> 1

    samples_rows = samples.reshape(channels, windows, length // LANES, LANES)
    samples_rows = samples_rows.transpose(0, 2, 1, 3).reshape(channels, windows * (length // LANES), LANES)
    scales = block_scale(exponents).reshape(channels, -1)
    scales = jnp.concatenate([scales, alive.astype(jnp.float32).reshape(channels, 1)], axis=1)

    own_src, ordered = source_rows(offsets, samples_rows, scales, seg_count, windows)
    mate_src = partner(own_src, 1)
    own_src = jnp.concatenate([own_src, mate_src], axis=1)
    above_src = passed_along(own_src, "chan", -1)
    below_src = passed_along(own_src, "chan", 1)

    sent = normalize_half((1 - core).reshape(1), samples_rows, scales, seg_count, windows)
    far = partner(sent, 1)
    near = normalize_half(core.reshape(1), samples_rows, scales, seg_count, windows)
    coarse, fine = (jnp.asarray(t) for t in small_tables())

    flag = windows * seg_count
    above_off = above_src[:, flag, 0].astype(jnp.int32)
    below_off = below_src[:, flag, 0].astype(jnp.int32)
    limits = jnp.concatenate(
        [(core * HALF).reshape(1), jnp.where(above_off == 0, channels, above_off - 1), below_off - 1]
    ).astype(jnp.int32)
    index = core * HALF + jnp.arange(HALF, dtype=jnp.int32)
    below_source = (index[None, :] < ordered[:SOURCES, None])[:, :, None]
    keep = below_source == (upper_half == 0)
    scale = 2.0 / float(2 * SEG * windows * lax.axis_size("win") * seg_count * SEG)

    tables = []
    for first, count in CHUNKS:
        tables.append(make_tables(first, count, coarse, fine))
    crossed, returned, selected = [], [], []

    def select(c):
        pieces = (crossed[c],) + returned[c]
        if c:
            pieces = lax.optimization_barrier(pieces + (selected[c - 1][2],))[:3]
        kept, moved = select_rows(below_source, keep, *pieces)
        selected.append((kept, partner(moved, 2), moved))

    kept_spectra = []
    for c in range(len(CHUNKS)):
        to_above, to_below, *spectra = outer_chunk(limits, near, far, own_src, above_src, below_src, tables[c])
        kept_spectra.append(spectra)
        from_below = passed_along(to_above, "chan", 1)
        from_above = passed_along(to_below, "chan", -1)
        returned.append((from_below, from_above))
    for c in range(len(CHUNKS)):
        crossed.append(own_chunk(*kept_spectra[c]))
        select(c)
    rest = make_tables(0, GROUPS, coarse, lax.optimization_barrier((fine, selected[0][2]))[0], True)
    parts = []
    for c in range(len(CHUNKS)):
        kept, moved, _ = selected[c]
        if c:
            kept = lax.optimization_barrier((kept, parts[c - 1][0]))[0]
        total = (kept + moved.astype(jnp.float32)).astype(jnp.bfloat16)
        mate = partner(total, 1)
        parts.append((total, mate, tables[c], rest))
    firsts = tuple(first for first, _ in CHUNKS)
    even, odd = early_inverse(ordered, parts[:-1], firsts[:-1])
    return last_inverse(ordered, parts[-1], even, odd, firsts[-1], scale)


def solution(mesh):
    placed = (P("chan", "win", None), P("chan", "win", None), P("chan"), P("chan"))
    return jax.shard_map(pipeline, mesh=mesh, in_specs=placed, out_specs=P("chan", "win", None), check_vma=False)
```

```python
import functools
import math

import jax
import jax.numpy as jnp
import numpy as np
from jax import lax
from jax.experimental import pallas as pl
from jax.experimental.pallas import tpu as pltpu
from jax.sharding import PartitionSpec as P


SEG = 1024
HALF = 96
LANES = 128
GROUPS = SEG // LANES
PAIR = 2 * LANES
CHUNKS = ((0, 4), (4, 4))
FOLD = 32
UNROLL = 4
TILE = 32
SUB = 16
PITCH = 104
SOURCES = 4
SLOT = 16
SEGMENTS = 12
COLS = 256


def small_tables():
    k = GROUPS * np.arange(LANES)[None, :] + np.arange(GROUPS)[:, None]
    step = np.arange(FOLD)

    def waves(stride):
        phase = (stride * step[None, :, None] * k[:, None, :]) % (2 * SEG)
        angle = phase * (2.0 * math.pi / (2 * SEG))
        return np.stack([np.cos(angle), np.sin(angle)], axis=1).astype(np.float32)

    return waves(FOLD), waves(1)


def table_kernel(coarse_ref, fine_ref, hi_ref, lo_ref):
    fine_cos = fine_ref[0, 0]
    fine_sin = fine_ref[0, 1]

    def row_block(step, carry):
        for inner in range(UNROLL):
            a = step * UNROLL + inner
            base_cos = coarse_ref[0, 0, pl.ds(a, 8, stride=0), :]
            base_sin = coarse_ref[0, 1, pl.ds(a, 8, stride=0), :]
            base_cos = jnp.concatenate([base_cos] * (FOLD // 8), axis=0)
            base_sin = jnp.concatenate([base_sin] * (FOLD // 8), axis=0)
            real = base_cos * fine_cos - base_sin * fine_sin
            imag = -(base_sin * fine_cos + base_cos * fine_sin)
            rows = pl.ds(pl.multiple_of(a * FOLD, FOLD), FOLD)
            for part, lane in ((real, 0), (imag, LANES)):
                top = part.astype(jnp.bfloat16)
                hi_ref[0, rows, lane:lane + LANES] = top
                lo_ref[0, rows, lane:lane + LANES] = (part - top.astype(jnp.float32)).astype(jnp.bfloat16)
        return carry

    lax.fori_loop(0, FOLD // UNROLL, row_block, 0)


def make_tables(first, count, coarse, fine):
    shape = jax.ShapeDtypeStruct((count, SEG, PAIR), jnp.bfloat16)
    small = pl.BlockSpec((1, 2, FOLD, LANES), lambda p: (first + p, 0, 0, 0))
    large = pl.BlockSpec((1, SEG, PAIR), lambda p: (p, 0, 0))
    return pl.pallas_call(
        table_kernel,
        grid=(count,),
        in_specs=[small, small],
        out_specs=[large, large],
        out_shape=[shape, shape],
        name="tables",
    )(coarse, fine)


def normalize_kernel(half_ref, samples_ref, scale_ref, out_ref, buffer_ref, spread_ref, wide_ref, sems, *,
                     seg_count, windows):
    step = pl.program_id(0)
    steps = pl.num_programs(0)
    per_channel = samples_ref.shape[1]
    pieces = SEG // LANES
    pairs = pieces // 2
    blocks = seg_count * pairs
    slot = step % 2

    def copy(at, into):
        first = half_ref[0] * HALF + at * TILE
        return pltpu.make_async_copy(
            samples_ref.at[pl.ds(first, TILE)],
            buffer_ref.at[into, :, pl.ds(0, per_channel), :],
            sems.at[into],
        )

    @pl.when(step == 0)
    def _():
        copy(0, 0).start()

    @pl.when(step + 1 < steps)
    def _():
        copy(step + 1, 1 - slot).start()

    columns = wide_ref.shape[0]

    @pl.when(step == 0)
    def _():
        for column in range(columns):
            row = lax.broadcasted_iota(jnp.int32, (columns, LANES), 0)
            spread_ref[:, column * LANES:(column + 1) * LANES] = jnp.where(row == column, 1.0, 0.0).astype(jnp.bfloat16)

    scale = scale_ref[...]
    narrow = scale[:, :columns].astype(jnp.bfloat16)
    for column in range(0, columns, 2):
        both = jnp.dot(
            narrow, spread_ref[:, column * LANES:(column + 2) * LANES], preferred_element_type=jnp.float32
        )
        wide_ref[column] = both[:, :LANES]
        wide_ref[column + 1] = both[:, LANES:]

    copy(step, slot).wait()
    flat = buffer_ref.reshape(2 * TILE * PITCH, LANES)
    base = slot * (TILE * PITCH)

    def rows(w, n, piece):
        start = base + (n * pieces + piece) * windows + w
        return flat[pl.ds(start, TILE, stride=PITCH), :].astype(jnp.float32)

    live = scale[:, windows * blocks:windows * blocks + 1]
    for w in range(windows):
        total = jnp.zeros((TILE, LANES), jnp.float32)
        for n in range(seg_count):
            for pair in range(pairs):
                column = w * blocks + n * pairs + pair
                one = rows(w, n, 2 * pair)
                two = rows(w, n, 2 * pair + 1)
                weight = wide_ref[column]
                total = total + (one * one + two * two) * (weight * weight)
        energy = jnp.sum(total, axis=1, keepdims=True) * (1.0 / (seg_count * SEG))
        factor = jnp.broadcast_to(live * lax.rsqrt(energy + 1e-06), (TILE, LANES))
        for n in range(seg_count):
            for pair in range(pairs):
                column = w * blocks + n * pairs + pair
                weight = wide_ref[column] * factor
                for piece in (2 * pair, 2 * pair + 1):
                    value = rows(w, n, piece) * weight
                    out_ref[w * seg_count + n, :, piece * LANES:(piece + 1) * LANES] = value.astype(jnp.bfloat16)


def normalize_half(half, samples_rows, scales, seg_count, windows):
    steps = HALF // TILE
    return pl.pallas_call(
        functools.partial(normalize_kernel, seg_count=seg_count, windows=windows),
        grid_spec=pltpu.PrefetchScalarGridSpec(
            num_scalar_prefetch=1,
            grid=(steps,),
            in_specs=[
                pl.BlockSpec(memory_space=pl.ANY),
                pl.BlockSpec((TILE, scales.shape[1]), lambda i, h: (h[0] * steps + i, 0)),
            ],
            out_specs=pl.BlockSpec((windows * seg_count, TILE, SEG), lambda i, h: (0, i, 0)),
            scratch_shapes=[
                pltpu.VMEM((2, TILE, PITCH, LANES), jnp.int32),
                pltpu.VMEM((scales.shape[1] - 1, (scales.shape[1] - 1) * LANES), jnp.bfloat16),
                pltpu.VMEM((scales.shape[1] - 1, TILE, LANES), jnp.float32),
                pltpu.SemaphoreType.DMA((2,)),
            ],
        ),
        out_shape=jax.ShapeDtypeStruct((windows * seg_count, HALF, SEG), jnp.bfloat16),
        name="normalize",
    )(half, samples_rows, scales)


def source_kernel(offsets_ref, samples_ref, scale_ref, out_ref, sorted_ref, buffer_ref, rows_ref, sems, *,
                  seg_count, windows):
    pieces = SEG // LANES
    pairs = pieces // 2
    blocks = seg_count * pairs
    per_channel = samples_ref.shape[1]
    given = [offsets_ref[j] for j in range(SOURCES)]
    ranks = []
    for j in range(SOURCES):
        rank = jnp.int32(0)
        for i in range(SOURCES):
            if i != j:
                ahead = given[i] <= given[j] if i < j else given[i] < given[j]
                rank = rank + jnp.where(ahead, 1, 0)
        ranks.append(rank)
    order = []
    for r in range(SOURCES):
        offset = jnp.int32(0)
        origin = jnp.int32(0)
        for j in range(SOURCES):
            hit = ranks[j] == r
            offset = jnp.where(hit, given[j], offset)
            origin = jnp.where(hit, j, origin)
        sorted_ref[r] = offset
        sorted_ref[SOURCES + r] = origin
        order.append(offset)
    copies = []
    for r in range(SOURCES):
        copy = pltpu.make_async_copy(
            samples_ref.at[order[r]], buffer_ref.at[r, pl.ds(0, per_channel), :], sems.at[r]
        )
        copy.start()
        copies.append(copy)
    channel = lax.broadcasted_iota(jnp.int32, scale_ref.shape, 0)
    lane = lax.broadcasted_iota(jnp.int32, (8, scale_ref.shape[1]), 1)
    segment = lax.broadcasted_iota(jnp.int32, (8, scale_ref.shape[1]), 0)
    valid = lax.broadcasted_iota(jnp.int32, (8, LANES), 0) < seg_count
    rows_ref[...] = jnp.zeros(rows_ref.shape, jnp.float32)
    for r in range(SOURCES):
        picked = jnp.sum(jnp.where(channel == order[r], scale_ref[...], 0.0), axis=0, keepdims=True)
        picked = jnp.broadcast_to(picked, (8, scale_ref.shape[1]))
        live = jnp.sum(jnp.where(lane == windows * blocks, picked, 0.0), axis=1, keepdims=True)
        copies[r].wait()
        for w in range(windows):
            parts = []
            total = jnp.zeros((8, LANES), jnp.float32)
            for pair in range(pairs):
                column = w * blocks + segment * pairs + pair
                weight = jnp.sum(jnp.where(lane == column, picked, 0.0), axis=1, keepdims=True)
                for piece in (2 * pair, 2 * pair + 1):
                    raw = buffer_ref[r, pl.ds(piece * windows + w, 8, stride=pieces * windows), :]
                    part = jnp.where(valid, raw.astype(jnp.float32), 0.0) * weight
                    total = total + part * part
                    parts.append(part)
            energy = jnp.sum(jnp.sum(total, axis=1, keepdims=True), axis=0, keepdims=True)
            factor = live * lax.rsqrt(energy * (1.0 / (seg_count * SEG)) + 1e-06)
            for piece in range(pieces):
                rows_ref[r, pl.ds(w * seg_count, seg_count), piece * LANES:(piece + 1) * LANES] = (
                    parts[piece] * factor
                )[:seg_count]
        rows_ref[r, pl.ds(windows * seg_count, 1), :] = jnp.full((1, SEG), 1, jnp.float32) * (
            order[r] + 1
        ).astype(jnp.float32)
        out_ref[r] = rows_ref[r].astype(jnp.bfloat16)


def source_rows(offsets, samples_rows, scales, seg_count, windows):
    return pl.pallas_call(
        functools.partial(source_kernel, seg_count=seg_count, windows=windows),
        grid_spec=pltpu.PrefetchScalarGridSpec(
            num_scalar_prefetch=1,
            grid=(1,),
            in_specs=[
                pl.BlockSpec(memory_space=pl.ANY),
                pl.BlockSpec(scales.shape, lambda i, h: (0, 0)),
            ],
            out_specs=[
                pl.BlockSpec((SOURCES, SLOT, SEG), lambda i, h: (0, 0, 0)),
                pl.BlockSpec(memory_space=pltpu.SMEM),
            ],
            scratch_shapes=[
                pltpu.VMEM((SOURCES, 128, LANES), jnp.int32),
                pltpu.VMEM((SOURCES, SLOT, SEG), jnp.float32),
                pltpu.SemaphoreType.DMA((SOURCES,)),
            ],
        ),
        out_shape=[
            jax.ShapeDtypeStruct((SOURCES, SLOT, SEG), jnp.bfloat16),
            jax.ShapeDtypeStruct((2 * SOURCES,), jnp.int32),
        ],
        name="sources",
    )(offsets, samples_rows, scales)


def products(band_ref, sources, base, members, emit, g, row):
    src_ref, plus_ref, minus_ref = sources
    count = SEGMENTS
    lane = pl.multiple_of(g * PAIR, PAIR)
    real_lanes = pl.ds(lane, LANES)
    imag_lanes = pl.ds(pl.multiple_of(lane + LANES, LANES), LANES)
    zero = jnp.zeros((8, LANES), jnp.float32)
    acc = {(t, j): [zero, zero, zero] for t in range(SUB // 8) for j in members}
    for q in range(2 * count):
        band = []
        for t in range(SUB // 8):
            at = pl.ds(q * TILE + row + 8 * t, 8)
            g_re = band_ref[2 * g, at, :]
            g_im = band_ref[2 * g + 1, at, :]
            band.append((g_re, g_im, g_re + g_im))
        spot = q if q < count else SLOT + q - count
        for j in members:
            at = pl.ds(base + j * 2 * SLOT + spot, 8, stride=0)
            s_re = src_ref[g, at, :]
            s_plus = plus_ref[g, at, :]
            s_minus = minus_ref[g, at, :]
            for t in range(SUB // 8):
                g_re, g_im, g_sum = band[t]
                a = acc[t, j]
                a[0] = a[0] + s_re * g_sum
                a[1] = a[1] + s_minus * g_im
                a[2] = a[2] + s_plus * g_re
    for j in members:
        real = jnp.concatenate([acc[t, j][0] + acc[t, j][1] for t in range(SUB // 8)], axis=0)
        imag = jnp.concatenate([acc[t, j][0] - acc[t, j][2] for t in range(SUB // 8)], axis=0)
        emit(j, pl.ds(row, SUB), real_lanes, real)
        emit(j, pl.ds(row, SUB), imag_lanes, imag)


def outer_kernel(limits_ref, near_ref, far_ref, own_src_ref, above_src_ref, below_src_ref, table_ref,
                 up_ref, down_ref, band_ref, own_re_ref, own_plus_ref, own_minus_ref, src_ref, plus_ref, minus_ref):
    step = pl.program_id(0)
    count = near_ref.shape[0]
    groups = table_ref.shape[0]
    src_rows = 2 * SLOT
    per_side = SOURCES * src_rows

    @pl.when(step == 0)
    def _():
        scratch = (src_ref, plus_ref, minus_ref)
        for ref, base, into in (
            (own_src_ref, 0, (own_re_ref, own_plus_ref, own_minus_ref)),
            (above_src_ref, 0, scratch),
            (below_src_ref, per_side, scratch),
        ):
            rows = ref[...].reshape(per_side, SEG)
            at = pl.ds(base, per_side)
            for g in range(groups):
                spec = jnp.dot(rows, table_ref[g], preferred_element_type=jnp.float32)
                spec = spec.astype(jnp.bfloat16).astype(jnp.float32)
                real = spec[:, :LANES]
                imag = spec[:, LANES:]
                into[0][g, at, :] = real
                into[1][g, at, :] = real + imag
                into[2][g, at, :] = imag - real

    for part, ref in ((0, near_ref), (1, far_ref)):
        rows = ref[...].reshape(count * TILE, SEG)
        at = pl.ds(part * count * TILE, count * TILE)
        for g in range(groups):
            spec = jnp.dot(rows, table_ref[g], preferred_element_type=jnp.float32)
            spec = spec.astype(jnp.bfloat16).astype(jnp.float32)
            band_ref[2 * g, at, :] = spec[:, :LANES]
            band_ref[2 * g + 1, at, :] = spec[:, LANES:]

    def to_up(j, rows, lanes, value):
        up_ref[j, rows, lanes] = value.astype(up_ref.dtype)

    def to_down(j, rows, lanes, value):
        down_ref[j, rows, lanes] = value.astype(down_ref.dtype)

    def tile(index, carry):
        g = index // (TILE // SUB)
        row = pl.multiple_of((index % (TILE // SUB)) * SUB, SUB)
        channel = limits_ref[0] + step * TILE + row
        sources = (src_ref, plus_ref, minus_ref)
        for first in (0, 2):
            pair = (first, first + 1)

            @pl.when(channel + SUB > limits_ref[1 + first])
            def _():
                products(band_ref, sources, 0, pair, to_up, g, row)

            @pl.when(channel < limits_ref[1 + SOURCES + first + 1])
            def _():
                products(band_ref, sources, per_side, pair, to_down, g, row)

        return carry

    lax.fori_loop(0, groups * (TILE // SUB), tile, 0)


def own_kernel(ordered_ref, place_ref, band_ref, src_ref, plus_ref, minus_ref, below_ref, above_ref,
               kept_ref, passed_ref):
    groups = src_ref.shape[0]
    lower = place_ref[1] == 0
    base = place_ref[0] + pl.program_id(0) * TILE

    def tile(index, carry):
        g = index // (TILE // SUB)
        row = pl.multiple_of((index % (TILE // SUB)) * SUB, SUB)
        channel = base + row + lax.broadcasted_iota(jnp.int32, (SUB, LANES), 0)

        def emit(j, rows, lanes, value):
            below_source = channel < ordered_ref[j]
            above = above_ref[j, rows, lanes].astype(jnp.float32)
            other = jnp.where(below_source, above, below_ref[j, rows, lanes].astype(jnp.float32))
            keep = jnp.where(below_source, 1, 0) == jnp.where(lower, 1, 0)
            kept_ref[j, rows, lanes] = jnp.where(keep, value, other)
            passed_ref[j, rows, lanes] = jnp.where(keep, other, value).astype(jnp.bfloat16)

        for first in (0, 2):
            products(band_ref, (src_ref, plus_ref, minus_ref), 0, (first, first + 1), emit, g, row)
        return carry

    lax.fori_loop(0, groups * (TILE // SUB), tile, 0)


def outer_chunk(limits, near, far, own_src, above_src, below_src, table):
    count = near.shape[0]
    groups = table.shape[0]
    width = groups * PAIR
    per_side = SOURCES * 2 * SLOT
    steps = HALF // TILE
    band_rows = 2 * count * TILE
    block = pl.BlockSpec((count, TILE, SEG), lambda i, h: (0, i, 0))
    src = pl.BlockSpec((SOURCES, 2 * SLOT, SEG), lambda i, h: (0, 0, 0))
    result = pl.BlockSpec((SOURCES, TILE, width), lambda i, h: (0, i, 0))
    spectra = pl.BlockSpec((groups, per_side, LANES), lambda i, h: (0, 0, 0))
    returned = jax.ShapeDtypeStruct((SOURCES, HALF, width), jnp.bfloat16)
    own = jax.ShapeDtypeStruct((groups, per_side, LANES), jnp.float32)
    return pl.pallas_call(
        outer_kernel,
        grid_spec=pltpu.PrefetchScalarGridSpec(
            num_scalar_prefetch=1,
            grid=(steps,),
            in_specs=[block, block, src, src, src, pl.BlockSpec((groups, SEG, PAIR), lambda i, h: (0, 0, 0))],
            out_specs=[
                result,
                result,
                pl.BlockSpec((2 * groups, band_rows, LANES), lambda i, h: (0, i, 0)),
                spectra,
                spectra,
                spectra,
            ],
            scratch_shapes=[pltpu.VMEM((groups, 2 * per_side, LANES), jnp.float32)] * 3,
        ),
        out_shape=[
            returned,
            returned,
            jax.ShapeDtypeStruct((2 * groups, steps * band_rows, LANES), jnp.float32),
            own,
            own,
            own,
        ],
        name="outer",
    )(limits, near, far, own_src, above_src, below_src, table)


def own_chunk(ordered, place, band, src, plus, minus, from_below, from_above):
    groups, per_side, _ = src.shape
    steps = HALF // TILE
    width = groups * PAIR
    spectra = pl.BlockSpec((groups, per_side, LANES), lambda i, o, p: (0, 0, 0))
    rows = pl.BlockSpec((SOURCES, TILE, width), lambda i, o, p: (0, i, 0))
    return pl.pallas_call(
        own_kernel,
        grid_spec=pltpu.PrefetchScalarGridSpec(
            num_scalar_prefetch=2,
            grid=(steps,),
            in_specs=[
                pl.BlockSpec((2 * groups, band.shape[1] // steps, LANES), lambda i, o, p: (0, i, 0)),
                spectra,
                spectra,
                spectra,
                rows,
                rows,
            ],
            out_specs=[rows, rows],
        ),
        out_shape=[
            jax.ShapeDtypeStruct((SOURCES, HALF, width), jnp.float32),
            jax.ShapeDtypeStruct((SOURCES, HALF, width), jnp.bfloat16),
        ],
        name="own",
    )(ordered, place, band, src, plus, minus, from_below, from_above)


def turned(ordered_ref, mine_ref, mate_ref, top_ref, halve):
    source_row = lax.broadcasted_iota(jnp.int32, (HALF, 2 * HALF), 1)
    target_row = lax.broadcasted_iota(jnp.int32, (HALF, 2 * HALF), 0)
    for j in range(SOURCES):
        wanted = target_row + ordered_ref[j]
        wanted = jnp.where(wanted >= 2 * HALF, wanted - 2 * HALF, wanted)
        turn = jnp.where(source_row == wanted, 1.0, 0.0).astype(jnp.bfloat16)
        rows = jnp.concatenate([mine_ref[j], mate_ref[j]], axis=0)
        top_ref[pl.ds(j * HALF, HALF), :] = jnp.dot(turn, rows, preferred_element_type=jnp.float32).astype(
            jnp.bfloat16
        )
    if halve:
        lane = lax.broadcasted_iota(jnp.int32, (SOURCES * HALF, LANES), 1)
        first = top_ref[:, :LANES].astype(jnp.float32)
        top_ref[:, :LANES] = jnp.where(lane == 0, 0.5 * first, first).astype(jnp.bfloat16)


def folded(top_ref, hi_ref, lo_ref, first, sums):
    for g in range(hi_ref.shape[0]):
        rows = top_ref[:, g * PAIR:(g + 1) * PAIR]
        for table in (hi_ref[g], lo_ref[g]):
            part = lax.dot_general(rows, table, (((1,), (1,)), ((), ())), preferred_element_type=jnp.float32)
            parity = (first + g) % 2
            sums[parity] = part if sums[parity] is None else sums[parity] + part


def early_kernel(ordered_ref, *refs, firsts):
    count = len(firsts)
    even_ref, odd_ref = refs[4 * count:4 * count + 2]
    tops = refs[4 * count + 2:]

    @pl.when(pl.program_id(0) == 0)
    def _():
        for c, first in enumerate(firsts):
            turned(ordered_ref, refs[4 * c], refs[4 * c + 1], tops[c], first == 0)

    sums = [None, None]
    for c, first in enumerate(firsts):
        folded(tops[c], refs[4 * c + 2], refs[4 * c + 3], first, sums)
    even_ref[...] = sums[0]
    odd_ref[...] = sums[1]


def chunk_specs(groups):
    rows = pl.BlockSpec((SOURCES, HALF, groups * PAIR), lambda m, h: (0, 0, 0))
    table = pl.BlockSpec((groups, COLS, PAIR), lambda m, h: (0, m, 0))
    return [rows, rows, table, table]


def early_inverse(ordered, parts, firsts):
    specs, operands, tops = [], [], []
    for part in parts:
        groups = part[2].shape[0]
        specs += chunk_specs(groups)
        operands += list(part)
        tops.append(pltpu.VMEM((SOURCES * HALF, groups * PAIR), jnp.bfloat16))
    block = pl.BlockSpec((SOURCES * HALF, COLS), lambda m, h: (0, m))
    shape = jax.ShapeDtypeStruct((SOURCES * HALF, SEG), jnp.float32)
    return pl.pallas_call(
        functools.partial(early_kernel, firsts=firsts),
        grid_spec=pltpu.PrefetchScalarGridSpec(
            num_scalar_prefetch=1,
            grid=(SEG // COLS,),
            in_specs=specs,
            out_specs=[block, block],
            scratch_shapes=tops,
        ),
        out_shape=[shape, shape],
        name="early",
    )(ordered, *operands)


def last_kernel(ordered_ref, mine_ref, mate_ref, hi_ref, lo_ref, even_ref, odd_ref, out_ref, top_ref, stage_ref, sem,
                *, first, scale):
    m = pl.program_id(0)

    @pl.when(m == 0)
    def _():
        turned(ordered_ref, mine_ref, mate_ref, top_ref, first == 0)

    sums = [even_ref[...], odd_ref[...]]
    folded(top_ref, hi_ref, lo_ref, first, sums)
    stage_ref[m, 0] = (sums[0] - sums[1]) * scale
    stage_ref[m, 1] = (sums[0] + sums[1]) * scale

    def copy(step, side, j):
        lane = pl.multiple_of(side * SEG + step * COLS, COLS)
        return pltpu.make_async_copy(
            stage_ref.at[step, side, pl.ds(j * HALF, HALF), :],
            out_ref.at[ordered_ref[SOURCES + j], :, pl.ds(lane, COLS)],
            sem.at[step, side, j],
        )

    for side in range(2):
        for j in range(SOURCES):
            copy(m, side, j).start()

    @pl.when(m == pl.num_programs(0) - 1)
    def _():
        for step in range(SEG // COLS):
            for side in range(2):
                for j in range(SOURCES):
                    copy(step, side, j).wait()


def last_inverse(ordered, part, even, odd, first, scale):
    groups = part[2].shape[0]
    block = pl.BlockSpec((SOURCES * HALF, COLS), lambda m, h: (0, m))
    return pl.pallas_call(
        functools.partial(last_kernel, first=first, scale=scale),
        grid_spec=pltpu.PrefetchScalarGridSpec(
            num_scalar_prefetch=1,
            grid=(SEG // COLS,),
            in_specs=chunk_specs(groups) + [block, block],
            out_specs=pl.BlockSpec(memory_space=pl.ANY),
            scratch_shapes=[
                pltpu.VMEM((SOURCES * HALF, groups * PAIR), jnp.bfloat16),
                pltpu.VMEM((SEG // COLS, 2, SOURCES * HALF, COLS), jnp.float32),
                pltpu.SemaphoreType.DMA((SEG // COLS, 2, SOURCES)),
            ],
        ),
        out_shape=jax.ShapeDtypeStruct((SOURCES, HALF, 2 * SEG), jnp.float32),
        name="last",
    )(ordered, *part, even, odd)


def block_scale(exponents):
    levels = jnp.arange(5, dtype=jnp.int32)
    powers = jnp.exp2(levels.astype(jnp.float32))
    return jnp.sum(jnp.where(exponents[..., None] == levels, powers, 0.0), axis=-1)


def passed_along(block, axis, distance):
    devices = range(lax.axis_size(axis))
    route = [(i - distance, i) for i in devices if i - distance in devices]
    return lax.ppermute(block, axis, route)


def partner(block, bit):
    return lax.ppermute(block, "win", [(i, i ^ bit) for i in range(lax.axis_size("win"))])


def pipeline(samples, exponents, alive, offsets):
    channels, windows, length = samples.shape
    seg_count = length // SEG
    place = lax.axis_index("win")
    core = place & 1
    upper_half = place >> 1

    samples_rows = samples.reshape(channels, windows, length // LANES, LANES)
    samples_rows = samples_rows.transpose(0, 2, 1, 3).reshape(channels, windows * (length // LANES), LANES)
    scales = block_scale(exponents).reshape(channels, -1)
    scales = jnp.concatenate([scales, alive.astype(jnp.float32).reshape(channels, 1)], axis=1)

    own_src, ordered = source_rows(offsets, samples_rows, scales, seg_count, windows)
    mate_src = partner(own_src, 1)
    own_src = jnp.concatenate([own_src, mate_src], axis=1)
    above_src = passed_along(own_src, "chan", -1)
    below_src = passed_along(own_src, "chan", 1)

    sent = normalize_half((1 - core).reshape(1), samples_rows, scales, seg_count, windows)
    far = partner(sent, 1)
    near = normalize_half(core.reshape(1), samples_rows, scales, seg_count, windows)
    coarse, fine = (jnp.asarray(t) for t in small_tables())

    flag = windows * seg_count
    above_off = above_src[:, flag, 0].astype(jnp.int32)
    below_off = below_src[:, flag, 0].astype(jnp.int32)
    limits = jnp.concatenate(
        [(core * HALF).reshape(1), jnp.where(above_off == 0, channels, above_off - 1), below_off - 1]
    ).astype(jnp.int32)
    where_am_i = jnp.stack([core * HALF, upper_half]).astype(jnp.int32)
    scale = 2.0 / float(2 * SEG * windows * lax.axis_size("win") * seg_count * SEG)

    tables = []
    for first, count in CHUNKS:
        tables.append(make_tables(first, count, coarse, fine))
    returned, selected = [], []

    kept_spectra = []
    for c in range(len(CHUNKS)):
        to_above, to_below, *spectra = outer_chunk(limits, near, far, own_src, above_src, below_src, tables[c][0])
        kept_spectra.append(spectra)
        from_below = passed_along(to_above, "chan", 1)
        from_above = passed_along(to_below, "chan", -1)
        returned.append((from_below, from_above))
    for c in range(len(CHUNKS)):
        kept, moved = own_chunk(ordered, where_am_i, *kept_spectra[c], *returned[c])
        selected.append((kept, partner(moved, 2)))
    parts = []
    for c in range(len(CHUNKS)):
        kept, moved = selected[c]
        if c:
            kept = lax.optimization_barrier((kept, parts[c - 1][0]))[0]
        total = (kept + moved.astype(jnp.float32)).astype(jnp.bfloat16)
        mate = partner(total, 1)
        parts.append((total, mate) + tuple(tables[c]))
    firsts = tuple(first for first, _ in CHUNKS)
    even, odd = early_inverse(ordered, parts[:-1], firsts[:-1])
    return last_inverse(ordered, parts[-1], even, odd, firsts[-1], scale)


def solution(mesh):
    placed = (P("chan", "win", None), P("chan", "win", None), P("chan"), P("chan"))
    return jax.shard_map(pipeline, mesh=mesh, in_specs=placed, out_specs=P("chan", "win", None), check_vma=False)
```

```python
import functools
import math

import jax
import jax.numpy as jnp
import numpy as np
from jax import lax
from jax.experimental import pallas as pl
from jax.experimental.pallas import tpu as pltpu
from jax.sharding import PartitionSpec as P


SEG = 1024
HALF = 96
LANES = 128
GROUPS = SEG // LANES
PAIR = 2 * LANES
CHUNKS = ((0, 5), (5, 3))
FOLD = 32
UNROLL = 4
TILE = 32
SUB = 16
PITCH = 104
SOURCES = 4
SLOT = 16
SEGMENTS = 12
COLS = 256


def small_tables():
    k = GROUPS * np.arange(LANES)[None, :] + np.arange(GROUPS)[:, None]
    step = np.arange(FOLD)

    def waves(stride):
        phase = (stride * step[None, :, None] * k[:, None, :]) % (2 * SEG)
        angle = phase * (2.0 * math.pi / (2 * SEG))
        return np.stack([np.cos(angle), np.sin(angle)], axis=1).astype(np.float32)

    return waves(FOLD), waves(1)


def table_kernel(coarse_ref, fine_ref, out_ref, *, rest):
    fine_cos = fine_ref[0, 0]
    fine_sin = fine_ref[0, 1]

    def row_block(step, carry):
        for inner in range(UNROLL):
            a = step * UNROLL + inner
            base_cos = coarse_ref[0, 0, pl.ds(a, 8, stride=0), :]
            base_sin = coarse_ref[0, 1, pl.ds(a, 8, stride=0), :]
            base_cos = jnp.concatenate([base_cos] * (FOLD // 8), axis=0)
            base_sin = jnp.concatenate([base_sin] * (FOLD // 8), axis=0)
            real = base_cos * fine_cos - base_sin * fine_sin
            imag = -(base_sin * fine_cos + base_cos * fine_sin)
            rows = pl.ds(pl.multiple_of(a * FOLD, FOLD), FOLD)
            for part, lane in ((real, 0), (imag, LANES)):
                top = part.astype(jnp.bfloat16)
                if rest:
                    top = (part - top.astype(jnp.float32)).astype(jnp.bfloat16)
                out_ref[0, rows, lane:lane + LANES] = top
        return carry

    lax.fori_loop(0, FOLD // UNROLL, row_block, 0)


def make_tables(first, count, coarse, fine, rest=False):
    shape = jax.ShapeDtypeStruct((count, SEG, PAIR), jnp.bfloat16)
    small = pl.BlockSpec((1, 2, FOLD, LANES), lambda p: (first + p, 0, 0, 0))
    large = pl.BlockSpec((1, SEG, PAIR), lambda p: (p, 0, 0))
    return pl.pallas_call(
        functools.partial(table_kernel, rest=rest),
        grid=(count,),
        in_specs=[small, small],
        out_specs=large,
        out_shape=shape,
        name="tables",
    )(coarse, fine)


def normalize_kernel(half_ref, samples_ref, scale_ref, out_ref, buffer_ref, spread_ref, wide_ref, sems, *,
                     seg_count, windows):
    step = pl.program_id(0)
    steps = pl.num_programs(0)
    per_channel = samples_ref.shape[1]
    pieces = SEG // LANES
    pairs = pieces // 2
    blocks = seg_count * pairs
    slot = step % 2

    def copy(at, into):
        first = half_ref[0] * HALF + at * TILE
        return pltpu.make_async_copy(
            samples_ref.at[pl.ds(first, TILE)],
            buffer_ref.at[into, :, pl.ds(0, per_channel), :],
            sems.at[into],
        )

    @pl.when(step == 0)
    def _():
        copy(0, 0).start()

    @pl.when(step + 1 < steps)
    def _():
        copy(step + 1, 1 - slot).start()

    columns = wide_ref.shape[0]

    @pl.when(step == 0)
    def _():
        for column in range(columns):
            row = lax.broadcasted_iota(jnp.int32, (columns, LANES), 0)
            spread_ref[:, column * LANES:(column + 1) * LANES] = jnp.where(row == column, 1.0, 0.0).astype(jnp.bfloat16)

    scale = scale_ref[...]
    narrow = scale[:, :columns].astype(jnp.bfloat16)
    for column in range(0, columns, 2):
        both = jnp.dot(
            narrow, spread_ref[:, column * LANES:(column + 2) * LANES], preferred_element_type=jnp.float32
        )
        wide_ref[column] = both[:, :LANES]
        wide_ref[column + 1] = both[:, LANES:]

    copy(step, slot).wait()
    flat = buffer_ref.reshape(2 * TILE * PITCH, LANES)
    base = slot * (TILE * PITCH)

    def rows(w, n, piece):
        start = base + (n * pieces + piece) * windows + w
        return flat[pl.ds(start, TILE, stride=PITCH), :].astype(jnp.float32)

    live = scale[:, windows * blocks:windows * blocks + 1]
    for w in range(windows):
        total = jnp.zeros((TILE, LANES), jnp.float32)
        for n in range(seg_count):
            for pair in range(pairs):
                column = w * blocks + n * pairs + pair
                one = rows(w, n, 2 * pair)
                two = rows(w, n, 2 * pair + 1)
                weight = wide_ref[column]
                total = total + (one * one + two * two) * (weight * weight)
        energy = jnp.sum(total, axis=1, keepdims=True) * (1.0 / (seg_count * SEG))
        factor = jnp.broadcast_to(live * lax.rsqrt(energy + 1e-06), (TILE, LANES))
        for n in range(seg_count):
            for pair in range(pairs):
                column = w * blocks + n * pairs + pair
                weight = wide_ref[column] * factor
                for piece in (2 * pair, 2 * pair + 1):
                    value = rows(w, n, piece) * weight
                    out_ref[w * seg_count + n, :, piece * LANES:(piece + 1) * LANES] = value.astype(jnp.bfloat16)


def normalize_half(half, samples_rows, scales, seg_count, windows):
    steps = HALF // TILE
    return pl.pallas_call(
        functools.partial(normalize_kernel, seg_count=seg_count, windows=windows),
        grid_spec=pltpu.PrefetchScalarGridSpec(
            num_scalar_prefetch=1,
            grid=(steps,),
            in_specs=[
                pl.BlockSpec(memory_space=pl.ANY),
                pl.BlockSpec((TILE, scales.shape[1]), lambda i, h: (h[0] * steps + i, 0)),
            ],
            out_specs=pl.BlockSpec((windows * seg_count, TILE, SEG), lambda i, h: (0, i, 0)),
            scratch_shapes=[
                pltpu.VMEM((2, TILE, PITCH, LANES), jnp.int32),
                pltpu.VMEM((scales.shape[1] - 1, (scales.shape[1] - 1) * LANES), jnp.bfloat16),
                pltpu.VMEM((scales.shape[1] - 1, TILE, LANES), jnp.float32),
                pltpu.SemaphoreType.DMA((2,)),
            ],
        ),
        out_shape=jax.ShapeDtypeStruct((windows * seg_count, HALF, SEG), jnp.bfloat16),
        name="normalize",
    )(half, samples_rows, scales)


def source_kernel(offsets_ref, samples_ref, scale_ref, out_ref, sorted_ref, buffer_ref, rows_ref, sems, *,
                  seg_count, windows):
    pieces = SEG // LANES
    pairs = pieces // 2
    blocks = seg_count * pairs
    per_channel = samples_ref.shape[1]
    given = [offsets_ref[j] for j in range(SOURCES)]
    ranks = []
    for j in range(SOURCES):
        rank = jnp.int32(0)
        for i in range(SOURCES):
            if i != j:
                ahead = given[i] <= given[j] if i < j else given[i] < given[j]
                rank = rank + jnp.where(ahead, 1, 0)
        ranks.append(rank)
    order = []
    for r in range(SOURCES):
        offset = jnp.int32(0)
        origin = jnp.int32(0)
        for j in range(SOURCES):
            hit = ranks[j] == r
            offset = jnp.where(hit, given[j], offset)
            origin = jnp.where(hit, j, origin)
        sorted_ref[r] = offset
        sorted_ref[SOURCES + r] = origin
        order.append(offset)
    copies = []
    for r in range(SOURCES):
        copy = pltpu.make_async_copy(
            samples_ref.at[order[r]], buffer_ref.at[r, pl.ds(0, per_channel), :], sems.at[r]
        )
        copy.start()
        copies.append(copy)
    channel = lax.broadcasted_iota(jnp.int32, scale_ref.shape, 0)
    lane = lax.broadcasted_iota(jnp.int32, (8, scale_ref.shape[1]), 1)
    segment = lax.broadcasted_iota(jnp.int32, (8, scale_ref.shape[1]), 0)
    valid = lax.broadcasted_iota(jnp.int32, (8, LANES), 0) < seg_count
    rows_ref[...] = jnp.zeros(rows_ref.shape, jnp.float32)
    for r in range(SOURCES):
        picked = jnp.sum(jnp.where(channel == order[r], scale_ref[...], 0.0), axis=0, keepdims=True)
        picked = jnp.broadcast_to(picked, (8, scale_ref.shape[1]))
        live = jnp.sum(jnp.where(lane == windows * blocks, picked, 0.0), axis=1, keepdims=True)
        copies[r].wait()
        for w in range(windows):
            parts = []
            total = jnp.zeros((8, LANES), jnp.float32)
            for pair in range(pairs):
                column = w * blocks + segment * pairs + pair
                weight = jnp.sum(jnp.where(lane == column, picked, 0.0), axis=1, keepdims=True)
                for piece in (2 * pair, 2 * pair + 1):
                    raw = buffer_ref[r, pl.ds(piece * windows + w, 8, stride=pieces * windows), :]
                    part = jnp.where(valid, raw.astype(jnp.float32), 0.0) * weight
                    total = total + part * part
                    parts.append(part)
            energy = jnp.sum(jnp.sum(total, axis=1, keepdims=True), axis=0, keepdims=True)
            factor = live * lax.rsqrt(energy * (1.0 / (seg_count * SEG)) + 1e-06)
            for piece in range(pieces):
                rows_ref[r, pl.ds(w * seg_count, seg_count), piece * LANES:(piece + 1) * LANES] = (
                    parts[piece] * factor
                )[:seg_count]
        rows_ref[r, pl.ds(windows * seg_count, 1), :] = jnp.full((1, SEG), 1, jnp.float32) * (
            order[r] + 1
        ).astype(jnp.float32)
        out_ref[r] = rows_ref[r].astype(jnp.bfloat16)


def source_rows(offsets, samples_rows, scales, seg_count, windows):
    return pl.pallas_call(
        functools.partial(source_kernel, seg_count=seg_count, windows=windows),
        grid_spec=pltpu.PrefetchScalarGridSpec(
            num_scalar_prefetch=1,
            grid=(1,),
            in_specs=[
                pl.BlockSpec(memory_space=pl.ANY),
                pl.BlockSpec(scales.shape, lambda i, h: (0, 0)),
            ],
            out_specs=[
                pl.BlockSpec((SOURCES, SLOT, SEG), lambda i, h: (0, 0, 0)),
                pl.BlockSpec(memory_space=pltpu.SMEM),
            ],
            scratch_shapes=[
                pltpu.VMEM((SOURCES, 128, LANES), jnp.int32),
                pltpu.VMEM((SOURCES, SLOT, SEG), jnp.float32),
                pltpu.SemaphoreType.DMA((SOURCES,)),
            ],
        ),
        out_shape=[
            jax.ShapeDtypeStruct((SOURCES, SLOT, SEG), jnp.bfloat16),
            jax.ShapeDtypeStruct((2 * SOURCES,), jnp.int32),
        ],
        name="sources",
    )(offsets, samples_rows, scales)


def products(band_ref, sources, base, members, emit, g, row):
    src_ref, plus_ref, minus_ref = sources
    count = SEGMENTS
    lane = pl.multiple_of(g * PAIR, PAIR)
    real_lanes = pl.ds(lane, LANES)
    imag_lanes = pl.ds(pl.multiple_of(lane + LANES, LANES), LANES)
    zero = jnp.zeros((8, LANES), jnp.float32)
    acc = {(t, j): [zero, zero, zero] for t in range(SUB // 8) for j in members}
    for q in range(2 * count):
        band = []
        for t in range(SUB // 8):
            at = pl.ds(q * TILE + row + 8 * t, 8)
            g_re = band_ref[2 * g, at, :]
            g_im = band_ref[2 * g + 1, at, :]
            band.append((g_re, g_im, g_re + g_im))
        spot = q if q < count else SLOT + q - count
        for j in members:
            at = pl.ds(base + j * 2 * SLOT + spot, 8, stride=0)
            s_re = src_ref[g, at, :]
            s_plus = plus_ref[g, at, :]
            s_minus = minus_ref[g, at, :]
            for t in range(SUB // 8):
                g_re, g_im, g_sum = band[t]
                a = acc[t, j]
                a[0] = a[0] + s_re * g_sum
                a[1] = a[1] + s_minus * g_im
                a[2] = a[2] + s_plus * g_re
    for j in members:
        real = jnp.concatenate([acc[t, j][0] + acc[t, j][1] for t in range(SUB // 8)], axis=0)
        imag = jnp.concatenate([acc[t, j][0] - acc[t, j][2] for t in range(SUB // 8)], axis=0)
        emit(j, pl.ds(row, SUB), real_lanes, real)
        emit(j, pl.ds(row, SUB), imag_lanes, imag)


def outer_kernel(limits_ref, near_ref, far_ref, own_src_ref, above_src_ref, below_src_ref, table_ref,
                 up_ref, down_ref, band_ref, own_re_ref, own_plus_ref, own_minus_ref, src_ref, plus_ref, minus_ref):
    step = pl.program_id(0)
    count = near_ref.shape[0]
    groups = table_ref.shape[0]
    src_rows = 2 * SLOT
    per_side = SOURCES * src_rows

    @pl.when(step == 0)
    def _():
        scratch = (src_ref, plus_ref, minus_ref)
        for ref, base, into in (
            (own_src_ref, 0, (own_re_ref, own_plus_ref, own_minus_ref)),
            (above_src_ref, 0, scratch),
            (below_src_ref, per_side, scratch),
        ):
            rows = ref[...].reshape(per_side, SEG)
            at = pl.ds(base, per_side)
            for g in range(groups):
                spec = jnp.dot(rows, table_ref[g], preferred_element_type=jnp.float32)
                spec = spec.astype(jnp.bfloat16).astype(jnp.float32)
                real = spec[:, :LANES]
                imag = spec[:, LANES:]
                into[0][g, at, :] = real
                into[1][g, at, :] = real + imag
                into[2][g, at, :] = imag - real

    for part, ref in ((0, near_ref), (1, far_ref)):
        rows = ref[...].reshape(count * TILE, SEG)
        at = pl.ds(part * count * TILE, count * TILE)
        for g in range(groups):
            spec = jnp.dot(rows, table_ref[g], preferred_element_type=jnp.float32)
            spec = spec.astype(jnp.bfloat16).astype(jnp.float32)
            band_ref[2 * g, at, :] = spec[:, :LANES]
            band_ref[2 * g + 1, at, :] = spec[:, LANES:]

    def to_up(j, rows, lanes, value):
        up_ref[j, rows, lanes] = value.astype(up_ref.dtype)

    def to_down(j, rows, lanes, value):
        down_ref[j, rows, lanes] = value.astype(down_ref.dtype)

    def tile(index, carry):
        g = index // (TILE // SUB)
        row = pl.multiple_of((index % (TILE // SUB)) * SUB, SUB)
        channel = limits_ref[0] + step * TILE + row
        sources = (src_ref, plus_ref, minus_ref)
        for first in (0, 2):
            pair = (first, first + 1)

            @pl.when(channel + SUB > limits_ref[1 + first])
            def _():
                products(band_ref, sources, 0, pair, to_up, g, row)

            @pl.when(channel < limits_ref[1 + SOURCES + first + 1])
            def _():
                products(band_ref, sources, per_side, pair, to_down, g, row)

        return carry

    lax.fori_loop(0, groups * (TILE // SUB), tile, 0)


def own_kernel(ordered_ref, place_ref, band_ref, src_ref, plus_ref, minus_ref, below_ref, above_ref,
               kept_ref, passed_ref):
    groups = src_ref.shape[0]
    lower = place_ref[1] == 0
    base = place_ref[0] + pl.program_id(0) * TILE

    def tile(index, carry):
        g = index // (TILE // SUB)
        row = pl.multiple_of((index % (TILE // SUB)) * SUB, SUB)
        channel = base + row + lax.broadcasted_iota(jnp.int32, (SUB, LANES), 0)

        def emit(j, rows, lanes, value):
            below_source = channel < ordered_ref[j]
            above = above_ref[j, rows, lanes].astype(jnp.float32)
            other = jnp.where(below_source, above, below_ref[j, rows, lanes].astype(jnp.float32))
            keep = jnp.where(below_source, 1, 0) == jnp.where(lower, 1, 0)
            kept_ref[j, rows, lanes] = jnp.where(keep, value, other)
            passed_ref[j, rows, lanes] = jnp.where(keep, other, value).astype(jnp.bfloat16)

        for first in (0, 2):
            products(band_ref, (src_ref, plus_ref, minus_ref), 0, (first, first + 1), emit, g, row)
        return carry

    lax.fori_loop(0, groups * (TILE // SUB), tile, 0)


def outer_chunk(limits, near, far, own_src, above_src, below_src, table):
    count = near.shape[0]
    groups = table.shape[0]
    width = groups * PAIR
    per_side = SOURCES * 2 * SLOT
    steps = HALF // TILE
    band_rows = 2 * count * TILE
    block = pl.BlockSpec((count, TILE, SEG), lambda i, h: (0, i, 0))
    src = pl.BlockSpec((SOURCES, 2 * SLOT, SEG), lambda i, h: (0, 0, 0))
    result = pl.BlockSpec((SOURCES, TILE, width), lambda i, h: (0, i, 0))
    spectra = pl.BlockSpec((groups, per_side, LANES), lambda i, h: (0, 0, 0))
    returned = jax.ShapeDtypeStruct((SOURCES, HALF, width), jnp.bfloat16)
    own = jax.ShapeDtypeStruct((groups, per_side, LANES), jnp.float32)
    return pl.pallas_call(
        outer_kernel,
        grid_spec=pltpu.PrefetchScalarGridSpec(
            num_scalar_prefetch=1,
            grid=(steps,),
            in_specs=[block, block, src, src, src, pl.BlockSpec((groups, SEG, PAIR), lambda i, h: (0, 0, 0))],
            out_specs=[
                result,
                result,
                pl.BlockSpec((2 * groups, band_rows, LANES), lambda i, h: (0, i, 0)),
                spectra,
                spectra,
                spectra,
            ],
            scratch_shapes=[pltpu.VMEM((groups, 2 * per_side, LANES), jnp.float32)] * 3,
        ),
        out_shape=[
            returned,
            returned,
            jax.ShapeDtypeStruct((2 * groups, steps * band_rows, LANES), jnp.float32),
            own,
            own,
            own,
        ],
        name="outer",
    )(limits, near, far, own_src, above_src, below_src, table)


def own_chunk(ordered, place, band, src, plus, minus, from_below, from_above):
    groups, per_side, _ = src.shape
    steps = HALF // TILE
    width = groups * PAIR
    spectra = pl.BlockSpec((groups, per_side, LANES), lambda i, o, p: (0, 0, 0))
    rows = pl.BlockSpec((SOURCES, TILE, width), lambda i, o, p: (0, i, 0))
    return pl.pallas_call(
        own_kernel,
        grid_spec=pltpu.PrefetchScalarGridSpec(
            num_scalar_prefetch=2,
            grid=(steps,),
            in_specs=[
                pl.BlockSpec((2 * groups, band.shape[1] // steps, LANES), lambda i, o, p: (0, i, 0)),
                spectra,
                spectra,
                spectra,
                rows,
                rows,
            ],
            out_specs=[rows, rows],
        ),
        out_shape=[
            jax.ShapeDtypeStruct((SOURCES, HALF, width), jnp.float32),
            jax.ShapeDtypeStruct((SOURCES, HALF, width), jnp.bfloat16),
        ],
        name="own",
    )(ordered, place, band, src, plus, minus, from_below, from_above)


def turned(ordered_ref, mine_ref, mate_ref, top_ref, halve):
    source_row = lax.broadcasted_iota(jnp.int32, (HALF, 2 * HALF), 1)
    target_row = lax.broadcasted_iota(jnp.int32, (HALF, 2 * HALF), 0)
    for j in range(SOURCES):
        wanted = target_row + ordered_ref[j]
        wanted = jnp.where(wanted >= 2 * HALF, wanted - 2 * HALF, wanted)
        turn = jnp.where(source_row == wanted, 1.0, 0.0).astype(jnp.bfloat16)
        rows = jnp.concatenate([mine_ref[j], mate_ref[j]], axis=0)
        top_ref[pl.ds(j * HALF, HALF), :] = jnp.dot(turn, rows, preferred_element_type=jnp.float32).astype(
            jnp.bfloat16
        )
    if halve:
        lane = lax.broadcasted_iota(jnp.int32, (SOURCES * HALF, LANES), 1)
        first = top_ref[:, :LANES].astype(jnp.float32)
        top_ref[:, :LANES] = jnp.where(lane == 0, 0.5 * first, first).astype(jnp.bfloat16)


def folded(top_ref, hi_ref, lo_ref, first, sums):
    for g in range(hi_ref.shape[0]):
        rows = top_ref[:, g * PAIR:(g + 1) * PAIR]
        for table in (hi_ref[g], lo_ref[g]):
            part = lax.dot_general(rows, table, (((1,), (1,)), ((), ())), preferred_element_type=jnp.float32)
            parity = (first + g) % 2
            sums[parity] = part if sums[parity] is None else sums[parity] + part


def early_kernel(ordered_ref, *refs, firsts):
    count = len(firsts)
    even_ref, odd_ref = refs[4 * count:4 * count + 2]
    tops = refs[4 * count + 2:]

    @pl.when(pl.program_id(0) == 0)
    def _():
        for c, first in enumerate(firsts):
            turned(ordered_ref, refs[4 * c], refs[4 * c + 1], tops[c], first == 0)

    sums = [None, None]
    for c, first in enumerate(firsts):
        folded(tops[c], refs[4 * c + 2], refs[4 * c + 3], first, sums)
    even_ref[...] = sums[0]
    odd_ref[...] = sums[1]


def chunk_specs(groups):
    rows = pl.BlockSpec((SOURCES, HALF, groups * PAIR), lambda m, h: (0, 0, 0))
    table = pl.BlockSpec((groups, COLS, PAIR), lambda m, h: (0, m, 0))
    return [rows, rows, table, table]


def early_inverse(ordered, parts, firsts):
    specs, operands, tops = [], [], []
    for part in parts:
        groups = part[2].shape[0]
        specs += chunk_specs(groups)
        operands += list(part)
        tops.append(pltpu.VMEM((SOURCES * HALF, groups * PAIR), jnp.bfloat16))
    block = pl.BlockSpec((SOURCES * HALF, COLS), lambda m, h: (0, m))
    shape = jax.ShapeDtypeStruct((SOURCES * HALF, SEG), jnp.float32)
    return pl.pallas_call(
        functools.partial(early_kernel, firsts=firsts),
        grid_spec=pltpu.PrefetchScalarGridSpec(
            num_scalar_prefetch=1,
            grid=(SEG // COLS,),
            in_specs=specs,
            out_specs=[block, block],
            scratch_shapes=tops,
        ),
        out_shape=[shape, shape],
        name="early",
    )(ordered, *operands)


def last_kernel(ordered_ref, mine_ref, mate_ref, hi_ref, lo_ref, even_ref, odd_ref, out_ref, top_ref, stage_ref, sem,
                *, first, scale):
    m = pl.program_id(0)

    @pl.when(m == 0)
    def _():
        turned(ordered_ref, mine_ref, mate_ref, top_ref, first == 0)

    sums = [even_ref[...], odd_ref[...]]
    folded(top_ref, hi_ref, lo_ref, first, sums)
    stage_ref[m, 0] = (sums[0] - sums[1]) * scale
    stage_ref[m, 1] = (sums[0] + sums[1]) * scale

    def copy(step, side, j):
        lane = pl.multiple_of(side * SEG + step * COLS, COLS)
        return pltpu.make_async_copy(
            stage_ref.at[step, side, pl.ds(j * HALF, HALF), :],
            out_ref.at[ordered_ref[SOURCES + j], :, pl.ds(lane, COLS)],
            sem.at[step, side, j],
        )

    for side in range(2):
        for j in range(SOURCES):
            copy(m, side, j).start()

    @pl.when(m == pl.num_programs(0) - 1)
    def _():
        for step in range(SEG // COLS):
            for side in range(2):
                for j in range(SOURCES):
                    copy(step, side, j).wait()


def last_inverse(ordered, part, even, odd, first, scale):
    groups = part[2].shape[0]
    block = pl.BlockSpec((SOURCES * HALF, COLS), lambda m, h: (0, m))
    return pl.pallas_call(
        functools.partial(last_kernel, first=first, scale=scale),
        grid_spec=pltpu.PrefetchScalarGridSpec(
            num_scalar_prefetch=1,
            grid=(SEG // COLS,),
            in_specs=chunk_specs(groups) + [block, block],
            out_specs=pl.BlockSpec(memory_space=pl.ANY),
            scratch_shapes=[
                pltpu.VMEM((SOURCES * HALF, groups * PAIR), jnp.bfloat16),
                pltpu.VMEM((SEG // COLS, 2, SOURCES * HALF, COLS), jnp.float32),
                pltpu.SemaphoreType.DMA((SEG // COLS, 2, SOURCES)),
            ],
        ),
        out_shape=jax.ShapeDtypeStruct((SOURCES, HALF, 2 * SEG), jnp.float32),
        name="last",
    )(ordered, *part, even, odd)


def block_scale(exponents):
    levels = jnp.arange(5, dtype=jnp.int32)
    powers = jnp.exp2(levels.astype(jnp.float32))
    return jnp.sum(jnp.where(exponents[..., None] == levels, powers, 0.0), axis=-1)


def passed_along(block, axis, distance):
    devices = range(lax.axis_size(axis))
    route = [(i - distance, i) for i in devices if i - distance in devices]
    return lax.ppermute(block, axis, route)


def partner(block, bit):
    return lax.ppermute(block, "win", [(i, i ^ bit) for i in range(lax.axis_size("win"))])


def pipeline(samples, exponents, alive, offsets):
    channels, windows, length = samples.shape
    seg_count = length // SEG
    place = lax.axis_index("win")
    core = place & 1
    upper_half = place >> 1

    samples_rows = samples.reshape(channels, windows, length // LANES, LANES)
    samples_rows = samples_rows.transpose(0, 2, 1, 3).reshape(channels, windows * (length // LANES), LANES)
    scales = block_scale(exponents).reshape(channels, -1)
    scales = jnp.concatenate([scales, alive.astype(jnp.float32).reshape(channels, 1)], axis=1)

    own_src, ordered = source_rows(offsets, samples_rows, scales, seg_count, windows)
    mate_src = partner(own_src, 1)
    own_src = jnp.concatenate([own_src, mate_src], axis=1)
    above_src = passed_along(own_src, "chan", -1)
    below_src = passed_along(own_src, "chan", 1)

    sent = normalize_half((1 - core).reshape(1), samples_rows, scales, seg_count, windows)
    far = partner(sent, 1)
    near = normalize_half(core.reshape(1), samples_rows, scales, seg_count, windows)
    coarse, fine = (jnp.asarray(t) for t in small_tables())

    flag = windows * seg_count
    above_off = above_src[:, flag, 0].astype(jnp.int32)
    below_off = below_src[:, flag, 0].astype(jnp.int32)
    limits = jnp.concatenate(
        [(core * HALF).reshape(1), jnp.where(above_off == 0, channels, above_off - 1), below_off - 1]
    ).astype(jnp.int32)
    where_am_i = jnp.stack([core * HALF, upper_half]).astype(jnp.int32)
    scale = 2.0 / float(2 * SEG * windows * lax.axis_size("win") * seg_count * SEG)

    tables = []
    for first, count in CHUNKS:
        tables.append(make_tables(first, count, coarse, fine))
    returned, selected = [], []

    kept_spectra = []
    for c in range(len(CHUNKS)):
        to_above, to_below, *spectra = outer_chunk(limits, near, far, own_src, above_src, below_src, tables[c])
        kept_spectra.append(spectra)
        from_below = passed_along(to_above, "chan", 1)
        from_above = passed_along(to_below, "chan", -1)
        returned.append((from_below, from_above))
    for c in range(len(CHUNKS)):
        kept, moved = own_chunk(ordered, where_am_i, *kept_spectra[c], *returned[c])
        selected.append((kept, partner(moved, 2), moved))
    rests = []
    for first, count in CHUNKS:
        later = lax.optimization_barrier((fine, selected[-1][2]))[0]
        rests.append(make_tables(first, count, coarse, later, True))
    parts = []
    for c in range(len(CHUNKS)):
        kept, moved, _ = selected[c]
        if c:
            kept = lax.optimization_barrier((kept, parts[c - 1][0]))[0]
        total = (kept + moved.astype(jnp.float32)).astype(jnp.bfloat16)
        mate = partner(total, 1)
        parts.append((total, mate, tables[c], rests[c]))
    firsts = tuple(first for first, _ in CHUNKS)
    even, odd = early_inverse(ordered, parts[:-1], firsts[:-1])
    return last_inverse(ordered, parts[-1], even, odd, firsts[-1], scale)


def solution(mesh):
    placed = (P("chan", "win", None), P("chan", "win", None), P("chan"), P("chan"))
    return jax.shard_map(pipeline, mesh=mesh, in_specs=placed, out_specs=P("chan", "win", None), check_vma=False)
```

```python
import functools
import math

import jax
import jax.numpy as jnp
import numpy as np
from jax import lax
from jax.experimental import pallas as pl
from jax.experimental.pallas import tpu as pltpu
from jax.sharding import PartitionSpec as P


SEG = 1024
HALF = 96
LANES = 128
GROUPS = SEG // LANES
PAIR = 2 * LANES
CHUNKS = ((0, 4), (4, 4))
FOLD = 32
UNROLL = 4
TILE = 32
SUB = 16
PITCH = 104
SOURCES = 4
SLOT = 16
SEGMENTS = 12
COLS = 256


def small_tables():
    k = GROUPS * np.arange(LANES)[None, :] + np.arange(GROUPS)[:, None]
    step = np.arange(FOLD)

    def waves(stride):
        phase = (stride * step[None, :, None] * k[:, None, :]) % (2 * SEG)
        angle = phase * (2.0 * math.pi / (2 * SEG))
        return np.stack([np.cos(angle), np.sin(angle)], axis=1).astype(np.float32)

    return waves(FOLD), waves(1)


def table_kernel(coarse_ref, fine_ref, out_ref, *, rest):
    fine_cos = fine_ref[0, 0]
    fine_sin = fine_ref[0, 1]

    def row_block(step, carry):
        for inner in range(UNROLL):
            a = step * UNROLL + inner
            base_cos = coarse_ref[0, 0, pl.ds(a, 8, stride=0), :]
            base_sin = coarse_ref[0, 1, pl.ds(a, 8, stride=0), :]
            base_cos = jnp.concatenate([base_cos] * (FOLD // 8), axis=0)
            base_sin = jnp.concatenate([base_sin] * (FOLD // 8), axis=0)
            real = base_cos * fine_cos - base_sin * fine_sin
            imag = -(base_sin * fine_cos + base_cos * fine_sin)
            rows = pl.ds(pl.multiple_of(a * FOLD, FOLD), FOLD)
            for part, lane in ((real, 0), (imag, LANES)):
                top = part.astype(jnp.bfloat16)
                if rest:
                    top = (part - top.astype(jnp.float32)).astype(jnp.bfloat16)
                out_ref[0, rows, lane:lane + LANES] = top
        return carry

    lax.fori_loop(0, FOLD // UNROLL, row_block, 0)


def make_tables(first, count, coarse, fine, rest=False):
    shape = jax.ShapeDtypeStruct((count, SEG, PAIR), jnp.bfloat16)
    small = pl.BlockSpec((1, 2, FOLD, LANES), lambda p: (first + p, 0, 0, 0))
    large = pl.BlockSpec((1, SEG, PAIR), lambda p: (p, 0, 0))
    return pl.pallas_call(
        functools.partial(table_kernel, rest=rest),
        grid=(count,),
        in_specs=[small, small],
        out_specs=large,
        out_shape=shape,
        name="tables",
    )(coarse, fine)


def normalize_kernel(half_ref, samples_ref, scale_ref, out_ref, buffer_ref, spread_ref, wide_ref, sems, *,
                     seg_count, windows):
    step = pl.program_id(0)
    steps = pl.num_programs(0)
    per_channel = samples_ref.shape[1]
    pieces = SEG // LANES
    pairs = pieces // 2
    blocks = seg_count * pairs
    slot = step % 2

    def copy(at, into):
        first = half_ref[0] * HALF + at * TILE
        return pltpu.make_async_copy(
            samples_ref.at[pl.ds(first, TILE)],
            buffer_ref.at[into, :, pl.ds(0, per_channel), :],
            sems.at[into],
        )

    @pl.when(step == 0)
    def _():
        copy(0, 0).start()

    @pl.when(step + 1 < steps)
    def _():
        copy(step + 1, 1 - slot).start()

    columns = wide_ref.shape[0]

    @pl.when(step == 0)
    def _():
        for column in range(columns):
            row = lax.broadcasted_iota(jnp.int32, (columns, LANES), 0)
            spread_ref[:, column * LANES:(column + 1) * LANES] = jnp.where(row == column, 1.0, 0.0).astype(jnp.bfloat16)

    scale = scale_ref[...]
    narrow = scale.astype(jnp.bfloat16)
    for column in range(0, columns, 2):
        both = jnp.dot(
            narrow, spread_ref[:, column * LANES:(column + 2) * LANES], preferred_element_type=jnp.float32
        )
        wide_ref[column] = both[:, :LANES]
        wide_ref[column + 1] = both[:, LANES:]

    copy(step, slot).wait()
    flat = buffer_ref.reshape(2 * TILE * PITCH, LANES)
    base = slot * (TILE * PITCH)

    def rows(w, n, piece):
        start = base + (n * pieces + piece) * windows + w
        return flat[pl.ds(start, TILE, stride=PITCH), :].astype(jnp.float32)

    for w in range(windows):
        total = jnp.zeros((TILE, LANES), jnp.float32)
        for n in range(seg_count):
            for pair in range(pairs):
                column = w * blocks + n * pairs + pair
                one = rows(w, n, 2 * pair)
                two = rows(w, n, 2 * pair + 1)
                weight = wide_ref[column]
                total = total + (one * one + two * two) * (weight * weight)
        energy = jnp.sum(total, axis=1, keepdims=True) * (1.0 / (seg_count * SEG))
        factor = jnp.broadcast_to(lax.rsqrt(energy + 1e-06), (TILE, LANES))
        for n in range(seg_count):
            for pair in range(pairs):
                column = w * blocks + n * pairs + pair
                weight = wide_ref[column] * factor
                for piece in (2 * pair, 2 * pair + 1):
                    value = rows(w, n, piece) * weight
                    out_ref[w * seg_count + n, :, piece * LANES:(piece + 1) * LANES] = value.astype(jnp.bfloat16)


def normalize_half(half, samples_rows, scales, seg_count, windows):
    steps = HALF // TILE
    return pl.pallas_call(
        functools.partial(normalize_kernel, seg_count=seg_count, windows=windows),
        grid_spec=pltpu.PrefetchScalarGridSpec(
            num_scalar_prefetch=1,
            grid=(steps,),
            in_specs=[
                pl.BlockSpec(memory_space=pl.ANY),
                pl.BlockSpec((TILE, scales.shape[1]), lambda i, h: (h[0] * steps + i, 0)),
            ],
            out_specs=pl.BlockSpec((windows * seg_count, TILE, SEG), lambda i, h: (0, i, 0)),
            scratch_shapes=[
                pltpu.VMEM((2, TILE, PITCH, LANES), jnp.int32),
                pltpu.VMEM((scales.shape[1], scales.shape[1] * LANES), jnp.bfloat16),
                pltpu.VMEM((scales.shape[1], TILE, LANES), jnp.float32),
                pltpu.SemaphoreType.DMA((2,)),
            ],
        ),
        out_shape=jax.ShapeDtypeStruct((windows * seg_count, HALF, SEG), jnp.bfloat16),
        name="normalize",
    )(half, samples_rows, scales)


def source_kernel(offsets_ref, samples_ref, scale_ref, out_ref, sorted_ref, buffer_ref, rows_ref, sems, *,
                  seg_count, windows):
    pieces = SEG // LANES
    pairs = pieces // 2
    blocks = seg_count * pairs
    per_channel = samples_ref.shape[1]
    given = [offsets_ref[j] for j in range(SOURCES)]
    ranks = []
    for j in range(SOURCES):
        rank = jnp.int32(0)
        for i in range(SOURCES):
            if i != j:
                ahead = given[i] <= given[j] if i < j else given[i] < given[j]
                rank = rank + jnp.where(ahead, 1, 0)
        ranks.append(rank)
    order = []
    for r in range(SOURCES):
        offset = jnp.int32(0)
        origin = jnp.int32(0)
        for j in range(SOURCES):
            hit = ranks[j] == r
            offset = jnp.where(hit, given[j], offset)
            origin = jnp.where(hit, j, origin)
        sorted_ref[r] = offset
        sorted_ref[SOURCES + r] = origin
        order.append(offset)
    copies = []
    for r in range(SOURCES):
        copy = pltpu.make_async_copy(
            samples_ref.at[order[r]], buffer_ref.at[r, pl.ds(0, per_channel), :], sems.at[r]
        )
        copy.start()
        copies.append(copy)
    channel = lax.broadcasted_iota(jnp.int32, scale_ref.shape, 0)
    lane = lax.broadcasted_iota(jnp.int32, (8, scale_ref.shape[1]), 1)
    segment = lax.broadcasted_iota(jnp.int32, (8, scale_ref.shape[1]), 0)
    valid = lax.broadcasted_iota(jnp.int32, (8, LANES), 0) < seg_count
    rows_ref[...] = jnp.zeros(rows_ref.shape, jnp.float32)
    for r in range(SOURCES):
        picked = jnp.sum(jnp.where(channel == order[r], scale_ref[...], 0.0), axis=0, keepdims=True)
        picked = jnp.broadcast_to(picked, (8, scale_ref.shape[1]))
        copies[r].wait()
        for w in range(windows):
            parts = []
            total = jnp.zeros((8, LANES), jnp.float32)
            for pair in range(pairs):
                column = w * blocks + segment * pairs + pair
                weight = jnp.sum(jnp.where(lane == column, picked, 0.0), axis=1, keepdims=True)
                for piece in (2 * pair, 2 * pair + 1):
                    raw = buffer_ref[r, pl.ds(piece * windows + w, 8, stride=pieces * windows), :]
                    part = jnp.where(valid, raw.astype(jnp.float32), 0.0) * weight
                    total = total + part * part
                    parts.append(part)
            energy = jnp.sum(jnp.sum(total, axis=1, keepdims=True), axis=0, keepdims=True)
            factor = lax.rsqrt(energy * (1.0 / (seg_count * SEG)) + 1e-06)
            for piece in range(pieces):
                rows_ref[r, pl.ds(w * seg_count, seg_count), piece * LANES:(piece + 1) * LANES] = (
                    parts[piece] * factor
                )[:seg_count]
        rows_ref[r, pl.ds(windows * seg_count, 1), :] = jnp.full((1, SEG), 1, jnp.float32) * (
            order[r] + 1
        ).astype(jnp.float32)
        out_ref[r] = rows_ref[r].astype(jnp.bfloat16)


def source_rows(offsets, samples_rows, scales, seg_count, windows):
    return pl.pallas_call(
        functools.partial(source_kernel, seg_count=seg_count, windows=windows),
        grid_spec=pltpu.PrefetchScalarGridSpec(
            num_scalar_prefetch=1,
            grid=(1,),
            in_specs=[
                pl.BlockSpec(memory_space=pl.ANY),
                pl.BlockSpec(scales.shape, lambda i, h: (0, 0)),
            ],
            out_specs=[
                pl.BlockSpec((SOURCES, SLOT, SEG), lambda i, h: (0, 0, 0)),
                pl.BlockSpec(memory_space=pltpu.SMEM),
            ],
            scratch_shapes=[
                pltpu.VMEM((SOURCES, 128, LANES), jnp.int32),
                pltpu.VMEM((SOURCES, SLOT, SEG), jnp.float32),
                pltpu.SemaphoreType.DMA((SOURCES,)),
            ],
        ),
        out_shape=[
            jax.ShapeDtypeStruct((SOURCES, SLOT, SEG), jnp.bfloat16),
            jax.ShapeDtypeStruct((2 * SOURCES,), jnp.int32),
        ],
        name="sources",
    )(offsets, samples_rows, scales)


def products(band_ref, sources, base, members, emit, g, row):
    src_ref, plus_ref, minus_ref = sources
    count = SEGMENTS
    lane = pl.multiple_of(g * PAIR, PAIR)
    real_lanes = pl.ds(lane, LANES)
    imag_lanes = pl.ds(pl.multiple_of(lane + LANES, LANES), LANES)
    zero = jnp.zeros((8, LANES), jnp.float32)
    acc = {(t, j): [zero, zero, zero] for t in range(SUB // 8) for j in members}
    for q in range(2 * count):
        band = []
        for t in range(SUB // 8):
            at = pl.ds(q * TILE + row + 8 * t, 8)
            g_re = band_ref[2 * g, at, :]
            g_im = band_ref[2 * g + 1, at, :]
            band.append((g_re, g_im, g_re + g_im))
        spot = q if q < count else SLOT + q - count
        for j in members:
            at = pl.ds(base + j * 2 * SLOT + spot, 8, stride=0)
            s_re = src_ref[g, at, :]
            s_plus = plus_ref[g, at, :]
            s_minus = minus_ref[g, at, :]
            for t in range(SUB // 8):
                g_re, g_im, g_sum = band[t]
                a = acc[t, j]
                a[0] = a[0] + s_re * g_sum
                a[1] = a[1] + s_minus * g_im
                a[2] = a[2] + s_plus * g_re
    for j in members:
        real = jnp.concatenate([acc[t, j][0] + acc[t, j][1] for t in range(SUB // 8)], axis=0)
        imag = jnp.concatenate([acc[t, j][0] - acc[t, j][2] for t in range(SUB // 8)], axis=0)
        emit(j, pl.ds(row, SUB), real_lanes, real)
        emit(j, pl.ds(row, SUB), imag_lanes, imag)


def outer_kernel(limits_ref, near_ref, far_ref, own_src_ref, above_src_ref, below_src_ref, table_ref,
                 up_ref, down_ref, band_ref, own_re_ref, own_plus_ref, own_minus_ref, src_ref, plus_ref, minus_ref):
    step = pl.program_id(0)
    count = near_ref.shape[0]
    groups = table_ref.shape[0]
    src_rows = 2 * SLOT
    per_side = SOURCES * src_rows

    @pl.when(step == 0)
    def _():
        scratch = (src_ref, plus_ref, minus_ref)
        for ref, base, into in (
            (own_src_ref, 0, (own_re_ref, own_plus_ref, own_minus_ref)),
            (above_src_ref, 0, scratch),
            (below_src_ref, per_side, scratch),
        ):
            rows = ref[...].reshape(per_side, SEG)
            at = pl.ds(base, per_side)
            for g in range(groups):
                spec = jnp.dot(rows, table_ref[g], preferred_element_type=jnp.float32)
                spec = spec.astype(jnp.bfloat16).astype(jnp.float32)
                real = spec[:, :LANES]
                imag = spec[:, LANES:]
                into[0][g, at, :] = real
                into[1][g, at, :] = real + imag
                into[2][g, at, :] = imag - real

    for part, ref in ((0, near_ref), (1, far_ref)):
        rows = ref[...].reshape(count * TILE, SEG)
        at = pl.ds(part * count * TILE, count * TILE)
        for g in range(groups):
            spec = jnp.dot(rows, table_ref[g], preferred_element_type=jnp.float32)
            spec = spec.astype(jnp.bfloat16).astype(jnp.float32)
            band_ref[2 * g, at, :] = spec[:, :LANES]
            band_ref[2 * g + 1, at, :] = spec[:, LANES:]

    def to_up(j, rows, lanes, value):
        up_ref[j, rows, lanes] = value.astype(up_ref.dtype)

    def to_down(j, rows, lanes, value):
        down_ref[j, rows, lanes] = value.astype(down_ref.dtype)

    def tile(index, carry):
        g = index // (TILE // SUB)
        row = pl.multiple_of((index % (TILE // SUB)) * SUB, SUB)
        channel = limits_ref[0] + step * TILE + row
        sources = (src_ref, plus_ref, minus_ref)
        for first in (0, 2):
            pair = (first, first + 1)

            @pl.when(channel + SUB > limits_ref[1 + first])
            def _():
                products(band_ref, sources, 0, pair, to_up, g, row)

            @pl.when(channel < limits_ref[1 + SOURCES + first + 1])
            def _():
                products(band_ref, sources, per_side, pair, to_down, g, row)

        return carry

    lax.fori_loop(0, groups * (TILE // SUB), tile, 0)


def own_kernel(ordered_ref, place_ref, band_ref, src_ref, plus_ref, minus_ref, below_ref, above_ref,
               kept_ref, passed_ref):
    groups = src_ref.shape[0]
    lower = place_ref[1] == 0
    base = place_ref[0] + pl.program_id(0) * TILE

    def tile(index, carry):
        g = index // (TILE // SUB)
        row = pl.multiple_of((index % (TILE // SUB)) * SUB, SUB)
        channel = base + row + lax.broadcasted_iota(jnp.int32, (SUB, LANES), 0)

        def emit(j, rows, lanes, value):
            below_source = channel < ordered_ref[j]
            above = above_ref[j, rows, lanes].astype(jnp.float32)
            other = jnp.where(below_source, above, below_ref[j, rows, lanes].astype(jnp.float32))
            keep = jnp.where(below_source, 1, 0) == jnp.where(lower, 1, 0)
            kept_ref[j, rows, lanes] = jnp.where(keep, value, other)
            passed_ref[j, rows, lanes] = jnp.where(keep, other, value).astype(jnp.bfloat16)

        for first in (0, 2):
            products(band_ref, (src_ref, plus_ref, minus_ref), 0, (first, first + 1), emit, g, row)
        return carry

    lax.fori_loop(0, groups * (TILE // SUB), tile, 0)


def outer_chunk(limits, near, far, own_src, above_src, below_src, table):
    count = near.shape[0]
    groups = table.shape[0]
    width = groups * PAIR
    per_side = SOURCES * 2 * SLOT
    steps = HALF // TILE
    band_rows = 2 * count * TILE
    block = pl.BlockSpec((count, TILE, SEG), lambda i, h: (0, i, 0))
    src = pl.BlockSpec((SOURCES, 2 * SLOT, SEG), lambda i, h: (0, 0, 0))
    result = pl.BlockSpec((SOURCES, TILE, width), lambda i, h: (0, i, 0))
    spectra = pl.BlockSpec((groups, per_side, LANES), lambda i, h: (0, 0, 0))
    returned = jax.ShapeDtypeStruct((SOURCES, HALF, width), jnp.bfloat16)
    own = jax.ShapeDtypeStruct((groups, per_side, LANES), jnp.float32)
    return pl.pallas_call(
        outer_kernel,
        grid_spec=pltpu.PrefetchScalarGridSpec(
            num_scalar_prefetch=1,
            grid=(steps,),
            in_specs=[block, block, src, src, src, pl.BlockSpec((groups, SEG, PAIR), lambda i, h: (0, 0, 0))],
            out_specs=[
                result,
                result,
                pl.BlockSpec((2 * groups, band_rows, LANES), lambda i, h: (0, i, 0)),
                spectra,
                spectra,
                spectra,
            ],
            scratch_shapes=[pltpu.VMEM((groups, 2 * per_side, LANES), jnp.float32)] * 3,
        ),
        out_shape=[
            returned,
            returned,
            jax.ShapeDtypeStruct((2 * groups, steps * band_rows, LANES), jnp.float32),
            own,
            own,
            own,
        ],
        name="outer",
    )(limits, near, far, own_src, above_src, below_src, table)


def own_chunk(ordered, place, band, src, plus, minus, from_below, from_above):
    groups, per_side, _ = src.shape
    steps = HALF // TILE
    width = groups * PAIR
    spectra = pl.BlockSpec((groups, per_side, LANES), lambda i, o, p: (0, 0, 0))
    rows = pl.BlockSpec((SOURCES, TILE, width), lambda i, o, p: (0, i, 0))
    return pl.pallas_call(
        own_kernel,
        grid_spec=pltpu.PrefetchScalarGridSpec(
            num_scalar_prefetch=2,
            grid=(steps,),
            in_specs=[
                pl.BlockSpec((2 * groups, band.shape[1] // steps, LANES), lambda i, o, p: (0, i, 0)),
                spectra,
                spectra,
                spectra,
                rows,
                rows,
            ],
            out_specs=[rows, rows],
        ),
        out_shape=[
            jax.ShapeDtypeStruct((SOURCES, HALF, width), jnp.float32),
            jax.ShapeDtypeStruct((SOURCES, HALF, width), jnp.bfloat16),
        ],
        name="own",
    )(ordered, place, band, src, plus, minus, from_below, from_above)


def turned(ordered_ref, mine_ref, mate_ref, top_ref, halve):
    source_row = lax.broadcasted_iota(jnp.int32, (HALF, 2 * HALF), 1)
    target_row = lax.broadcasted_iota(jnp.int32, (HALF, 2 * HALF), 0)
    for j in range(SOURCES):
        wanted = target_row + ordered_ref[j]
        wanted = jnp.where(wanted >= 2 * HALF, wanted - 2 * HALF, wanted)
        turn = jnp.where(source_row == wanted, 1.0, 0.0).astype(jnp.bfloat16)
        rows = jnp.concatenate([mine_ref[j], mate_ref[j]], axis=0)
        top_ref[pl.ds(j * HALF, HALF), :] = jnp.dot(turn, rows, preferred_element_type=jnp.float32).astype(
            jnp.bfloat16
        )
    if halve:
        lane = lax.broadcasted_iota(jnp.int32, (SOURCES * HALF, LANES), 1)
        first = top_ref[:, :LANES].astype(jnp.float32)
        top_ref[:, :LANES] = jnp.where(lane == 0, 0.5 * first, first).astype(jnp.bfloat16)


def folded(top_ref, hi_ref, lo_ref, first, sums):
    for g in range(hi_ref.shape[0]):
        rows = top_ref[:, g * PAIR:(g + 1) * PAIR]
        for table in (hi_ref[g], lo_ref[g]):
            part = lax.dot_general(rows, table, (((1,), (1,)), ((), ())), preferred_element_type=jnp.float32)
            parity = (first + g) % 2
            sums[parity] = part if sums[parity] is None else sums[parity] + part


def early_kernel(ordered_ref, *refs, firsts):
    count = len(firsts)
    even_ref, odd_ref = refs[4 * count:4 * count + 2]
    tops = refs[4 * count + 2:]

    @pl.when(pl.program_id(0) == 0)
    def _():
        for c, first in enumerate(firsts):
            turned(ordered_ref, refs[4 * c], refs[4 * c + 1], tops[c], first == 0)

    sums = [None, None]
    for c, first in enumerate(firsts):
        folded(tops[c], refs[4 * c + 2], refs[4 * c + 3], first, sums)
    even_ref[...] = sums[0]
    odd_ref[...] = sums[1]


def chunk_specs(groups):
    rows = pl.BlockSpec((SOURCES, HALF, groups * PAIR), lambda m, h: (0, 0, 0))
    table = pl.BlockSpec((groups, COLS, PAIR), lambda m, h: (0, m, 0))
    return [rows, rows, table, table]


def early_inverse(ordered, parts, firsts):
    specs, operands, tops = [], [], []
    for part in parts:
        groups = part[2].shape[0]
        specs += chunk_specs(groups)
        operands += list(part)
        tops.append(pltpu.VMEM((SOURCES * HALF, groups * PAIR), jnp.bfloat16))
    block = pl.BlockSpec((SOURCES * HALF, COLS), lambda m, h: (0, m))
    shape = jax.ShapeDtypeStruct((SOURCES * HALF, SEG), jnp.float32)
    return pl.pallas_call(
        functools.partial(early_kernel, firsts=firsts),
        grid_spec=pltpu.PrefetchScalarGridSpec(
            num_scalar_prefetch=1,
            grid=(SEG // COLS,),
            in_specs=specs,
            out_specs=[block, block],
            scratch_shapes=tops,
        ),
        out_shape=[shape, shape],
        name="early",
    )(ordered, *operands)


def last_kernel(ordered_ref, mine_ref, mate_ref, hi_ref, lo_ref, even_ref, odd_ref, out_ref, top_ref, stage_ref, sem,
                *, first, scale):
    m = pl.program_id(0)

    @pl.when(m == 0)
    def _():
        turned(ordered_ref, mine_ref, mate_ref, top_ref, first == 0)

    sums = [even_ref[...], odd_ref[...]]
    folded(top_ref, hi_ref, lo_ref, first, sums)
    stage_ref[m, 0] = (sums[0] - sums[1]) * scale
    stage_ref[m, 1] = (sums[0] + sums[1]) * scale

    def copy(step, side, j):
        lane = pl.multiple_of(side * SEG + step * COLS, COLS)
        return pltpu.make_async_copy(
            stage_ref.at[step, side, pl.ds(j * HALF, HALF), :],
            out_ref.at[ordered_ref[SOURCES + j], :, pl.ds(lane, COLS)],
            sem.at[step, side, j],
        )

    for side in range(2):
        for j in range(SOURCES):
            copy(m, side, j).start()

    @pl.when(m == pl.num_programs(0) - 1)
    def _():
        for step in range(SEG // COLS):
            for side in range(2):
                for j in range(SOURCES):
                    copy(step, side, j).wait()


def last_inverse(ordered, part, even, odd, first, scale):
    groups = part[2].shape[0]
    block = pl.BlockSpec((SOURCES * HALF, COLS), lambda m, h: (0, m))
    return pl.pallas_call(
        functools.partial(last_kernel, first=first, scale=scale),
        grid_spec=pltpu.PrefetchScalarGridSpec(
            num_scalar_prefetch=1,
            grid=(SEG // COLS,),
            in_specs=chunk_specs(groups) + [block, block],
            out_specs=pl.BlockSpec(memory_space=pl.ANY),
            scratch_shapes=[
                pltpu.VMEM((SOURCES * HALF, groups * PAIR), jnp.bfloat16),
                pltpu.VMEM((SEG // COLS, 2, SOURCES * HALF, COLS), jnp.float32),
                pltpu.SemaphoreType.DMA((SEG // COLS, 2, SOURCES)),
            ],
        ),
        out_shape=jax.ShapeDtypeStruct((SOURCES, HALF, 2 * SEG), jnp.float32),
        name="last",
    )(ordered, *part, even, odd)


def block_scale(exponents, alive):
    scale = jnp.zeros(exponents.shape, jnp.float32)
    for level in range(5):
        hit = (exponents == level) & (alive != 0)[:, None, None]
        scale = jnp.where(hit, float(2 ** level), scale)
    return scale


def passed_along(block, axis, distance):
    devices = range(lax.axis_size(axis))
    route = [(i - distance, i) for i in devices if i - distance in devices]
    return lax.ppermute(block, axis, route)


def partner(block, bit):
    return lax.ppermute(block, "win", [(i, i ^ bit) for i in range(lax.axis_size("win"))])


def pipeline(samples, exponents, alive, offsets):
    channels, windows, length = samples.shape
    seg_count = length // SEG
    place = lax.axis_index("win")
    core = place & 1
    upper_half = place >> 1

    samples_rows = samples.reshape(channels, windows, length // LANES, LANES)
    samples_rows = samples_rows.transpose(0, 2, 1, 3).reshape(channels, windows * (length // LANES), LANES)
    scales = block_scale(exponents, alive).reshape(channels, -1)

    own_src, ordered = source_rows(offsets, samples_rows, scales, seg_count, windows)
    mate_src = partner(own_src, 1)
    own_src = jnp.concatenate([own_src, mate_src], axis=1)
    above_src = passed_along(own_src, "chan", -1)
    below_src = passed_along(own_src, "chan", 1)

    sent = normalize_half((1 - core).reshape(1), samples_rows, scales, seg_count, windows)
    far = partner(sent, 1)
    near = normalize_half(core.reshape(1), samples_rows, scales, seg_count, windows)
    coarse, fine = (jnp.asarray(t) for t in small_tables())

    flag = windows * seg_count
    above_off = above_src[:, flag, 0].astype(jnp.int32)
    below_off = below_src[:, flag, 0].astype(jnp.int32)
    limits = jnp.concatenate(
        [(core * HALF).reshape(1), jnp.where(above_off == 0, channels, above_off - 1), below_off - 1]
    ).astype(jnp.int32)
    where_am_i = jnp.stack([core * HALF, upper_half]).astype(jnp.int32)
    scale = 2.0 / float(2 * SEG * windows * lax.axis_size("win") * seg_count * SEG)

    tables = []
    for first, count in CHUNKS:
        tables.append(make_tables(first, count, coarse, fine))
    returned, selected = [], []

    kept_spectra = []
    for c in range(len(CHUNKS)):
        to_above, to_below, *spectra = outer_chunk(limits, near, far, own_src, above_src, below_src, tables[c])
        kept_spectra.append(spectra)
        from_below = passed_along(to_above, "chan", 1)
        from_above = passed_along(to_below, "chan", -1)
        returned.append((from_below, from_above))
    for c in range(len(CHUNKS)):
        kept, moved = own_chunk(ordered, where_am_i, *kept_spectra[c], *returned[c])
        selected.append((kept, partner(moved, 2), moved))
    rests = []
    for first, count in CHUNKS:
        later = lax.optimization_barrier((fine, selected[0][2]))[0]
        rests.append(make_tables(first, count, coarse, later, True))
    parts = []
    for c in range(len(CHUNKS)):
        kept, moved, _ = selected[c]
        if c:
            kept = lax.optimization_barrier((kept, parts[c - 1][0]))[0]
        total = (kept + moved.astype(jnp.float32)).astype(jnp.bfloat16)
        mate = partner(total, 1)
        parts.append((total, mate, tables[c], rests[c]))
    firsts = tuple(first for first, _ in CHUNKS)
    even, odd = early_inverse(ordered, parts[:-1], firsts[:-1])
    return last_inverse(ordered, parts[-1], even, odd, firsts[-1], scale)


def solution(mesh):
    placed = (P("chan", "win", None), P("chan", "win", None), P("chan"), P("chan"))
    return jax.shard_map(pipeline, mesh=mesh, in_specs=placed, out_specs=P("chan", "win", None), check_vma=False)
```

```python
import functools
import math

import jax
import jax.numpy as jnp
import numpy as np
from jax import lax
from jax.experimental import pallas as pl
from jax.experimental.pallas import tpu as pltpu
from jax.sharding import PartitionSpec as P


SEG = 1024
HALF = 96
LANES = 128
GROUPS = SEG // LANES
PAIR = 2 * LANES
CHUNKS = ((0, 4), (4, 4))
FOLD = 32
UNROLL = 4
TILE = 32
SUB = 16
PITCH = 104
SOURCES = 4
SLOT = 16
SEGMENTS = 12
COLS = 256


def small_tables():
    k = GROUPS * np.arange(LANES)[None, :] + np.arange(GROUPS)[:, None]
    step = np.arange(FOLD)

    def waves(stride):
        phase = (stride * step[None, :, None] * k[:, None, :]) % (2 * SEG)
        angle = phase * (2.0 * math.pi / (2 * SEG))
        return np.stack([np.cos(angle), np.sin(angle)], axis=1).astype(np.float32)

    return waves(FOLD), waves(1)


def table_kernel(coarse_ref, fine_ref, out_ref, *, rest):
    fine_cos = fine_ref[0, 0]
    fine_sin = fine_ref[0, 1]

    def row_block(step, carry):
        for inner in range(UNROLL):
            a = step * UNROLL + inner
            base_cos = coarse_ref[0, 0, pl.ds(a, 8, stride=0), :]
            base_sin = coarse_ref[0, 1, pl.ds(a, 8, stride=0), :]
            base_cos = jnp.concatenate([base_cos] * (FOLD // 8), axis=0)
            base_sin = jnp.concatenate([base_sin] * (FOLD // 8), axis=0)
            real = base_cos * fine_cos - base_sin * fine_sin
            imag = -(base_sin * fine_cos + base_cos * fine_sin)
            rows = pl.ds(pl.multiple_of(a * FOLD, FOLD), FOLD)
            for part, lane in ((real, 0), (imag, LANES)):
                top = part.astype(jnp.bfloat16)
                if rest:
                    top = (part - top.astype(jnp.float32)).astype(jnp.bfloat16)
                out_ref[0, rows, lane:lane + LANES] = top
        return carry

    lax.fori_loop(0, FOLD // UNROLL, row_block, 0)


def make_tables(first, count, coarse, fine, rest=False):
    shape = jax.ShapeDtypeStruct((count, SEG, PAIR), jnp.bfloat16)
    small = pl.BlockSpec((1, 2, FOLD, LANES), lambda p: (first + p, 0, 0, 0))
    large = pl.BlockSpec((1, SEG, PAIR), lambda p: (p, 0, 0))
    return pl.pallas_call(
        functools.partial(table_kernel, rest=rest),
        grid=(count,),
        in_specs=[small, small],
        out_specs=large,
        out_shape=shape,
        name="tables",
    )(coarse, fine)


def normalize_kernel(half_ref, samples_ref, scale_ref, out_ref, buffer_ref, spread_ref, wide_ref, sems, *,
                     seg_count, windows):
    step = pl.program_id(0)
    steps = pl.num_programs(0)
    per_channel = samples_ref.shape[1]
    pieces = SEG // LANES
    pairs = pieces // 2
    blocks = seg_count * pairs
    slot = step % 2

    def copy(at, into):
        first = half_ref[0] * HALF + at * TILE
        return pltpu.make_async_copy(
            samples_ref.at[pl.ds(first, TILE)],
            buffer_ref.at[into, :, pl.ds(0, per_channel), :],
            sems.at[into],
        )

    @pl.when(step == 0)
    def _():
        copy(0, 0).start()

    @pl.when(step + 1 < steps)
    def _():
        copy(step + 1, 1 - slot).start()

    columns = wide_ref.shape[0]

    @pl.when(step == 0)
    def _():
        for column in range(columns):
            row = lax.broadcasted_iota(jnp.int32, (columns, LANES), 0)
            spread_ref[:, column * LANES:(column + 1) * LANES] = jnp.where(row == column, 1.0, 0.0).astype(jnp.bfloat16)

    scale = scale_ref[...]
    narrow = scale.astype(jnp.bfloat16)
    for column in range(0, columns, 2):
        both = jnp.dot(
            narrow, spread_ref[:, column * LANES:(column + 2) * LANES], preferred_element_type=jnp.float32
        )
        wide_ref[column] = both[:, :LANES]
        wide_ref[column + 1] = both[:, LANES:]

    copy(step, slot).wait()
    flat = buffer_ref.reshape(2 * TILE * PITCH, LANES)
    base = slot * (TILE * PITCH)

    def rows(w, n, piece):
        start = base + (n * pieces + piece) * windows + w
        return flat[pl.ds(start, TILE, stride=PITCH), :].astype(jnp.float32)

    for w in range(windows):
        total = jnp.zeros((TILE, LANES), jnp.float32)
        for n in range(seg_count):
            for pair in range(pairs):
                column = w * blocks + n * pairs + pair
                one = rows(w, n, 2 * pair)
                two = rows(w, n, 2 * pair + 1)
                weight = wide_ref[column]
                total = total + (one * one + two * two) * (weight * weight)
        energy = jnp.sum(total, axis=1, keepdims=True) * (1.0 / (seg_count * SEG))
        factor = jnp.broadcast_to(lax.rsqrt(energy + 1e-06), (TILE, LANES))
        for n in range(seg_count):
            for pair in range(pairs):
                column = w * blocks + n * pairs + pair
                weight = wide_ref[column] * factor
                for piece in (2 * pair, 2 * pair + 1):
                    value = rows(w, n, piece) * weight
                    out_ref[w * seg_count + n, :, piece * LANES:(piece + 1) * LANES] = value.astype(jnp.bfloat16)


def normalize_half(half, samples_rows, scales, seg_count, windows):
    steps = HALF // TILE
    return pl.pallas_call(
        functools.partial(normalize_kernel, seg_count=seg_count, windows=windows),
        grid_spec=pltpu.PrefetchScalarGridSpec(
            num_scalar_prefetch=1,
            grid=(steps,),
            in_specs=[
                pl.BlockSpec(memory_space=pl.ANY),
                pl.BlockSpec((TILE, scales.shape[1]), lambda i, h: (h[0] * steps + i, 0)),
            ],
            out_specs=pl.BlockSpec((windows * seg_count, TILE, SEG), lambda i, h: (0, i, 0)),
            scratch_shapes=[
                pltpu.VMEM((2, TILE, PITCH, LANES), jnp.int32),
                pltpu.VMEM((scales.shape[1], scales.shape[1] * LANES), jnp.bfloat16),
                pltpu.VMEM((scales.shape[1], TILE, LANES), jnp.float32),
                pltpu.SemaphoreType.DMA((2,)),
            ],
        ),
        out_shape=jax.ShapeDtypeStruct((windows * seg_count, HALF, SEG), jnp.bfloat16),
        name="normalize",
    )(half, samples_rows, scales)


def source_kernel(offsets_ref, samples_ref, scale_ref, out_ref, sorted_ref, buffer_ref, rows_ref, sems, *,
                  seg_count, windows):
    pieces = SEG // LANES
    pairs = pieces // 2
    blocks = seg_count * pairs
    per_channel = samples_ref.shape[1]
    given = [offsets_ref[j] for j in range(SOURCES)]
    ranks = []
    for j in range(SOURCES):
        rank = jnp.int32(0)
        for i in range(SOURCES):
            if i != j:
                ahead = given[i] <= given[j] if i < j else given[i] < given[j]
                rank = rank + jnp.where(ahead, 1, 0)
        ranks.append(rank)
    order = []
    for r in range(SOURCES):
        offset = jnp.int32(0)
        origin = jnp.int32(0)
        for j in range(SOURCES):
            hit = ranks[j] == r
            offset = jnp.where(hit, given[j], offset)
            origin = jnp.where(hit, j, origin)
        sorted_ref[r] = offset
        sorted_ref[SOURCES + r] = origin
        order.append(offset)
    copies = []
    for r in range(SOURCES):
        copy = pltpu.make_async_copy(
            samples_ref.at[order[r]], buffer_ref.at[r, pl.ds(0, per_channel), :], sems.at[r]
        )
        copy.start()
        copies.append(copy)
    channel = lax.broadcasted_iota(jnp.int32, scale_ref.shape, 0)
    lane = lax.broadcasted_iota(jnp.int32, (8, scale_ref.shape[1]), 1)
    segment = lax.broadcasted_iota(jnp.int32, (8, scale_ref.shape[1]), 0)
    valid = lax.broadcasted_iota(jnp.int32, (8, LANES), 0) < seg_count
    rows_ref[...] = jnp.zeros(rows_ref.shape, jnp.float32)
    for r in range(SOURCES):
        picked = jnp.sum(jnp.where(channel == order[r], scale_ref[...], 0.0), axis=0, keepdims=True)
        picked = jnp.broadcast_to(picked, (8, scale_ref.shape[1]))
        copies[r].wait()
        for w in range(windows):
            parts = []
            total = jnp.zeros((8, LANES), jnp.float32)
            for pair in range(pairs):
                column = w * blocks + segment * pairs + pair
                weight = jnp.sum(jnp.where(lane == column, picked, 0.0), axis=1, keepdims=True)
                for piece in (2 * pair, 2 * pair + 1):
                    raw = buffer_ref[r, pl.ds(piece * windows + w, 8, stride=pieces * windows), :]
                    part = jnp.where(valid, raw.astype(jnp.float32), 0.0) * weight
                    total = total + part * part
                    parts.append(part)
            energy = jnp.sum(jnp.sum(total, axis=1, keepdims=True), axis=0, keepdims=True)
            factor = lax.rsqrt(energy * (1.0 / (seg_count * SEG)) + 1e-06)
            for piece in range(pieces):
                rows_ref[r, pl.ds(w * seg_count, seg_count), piece * LANES:(piece + 1) * LANES] = (
                    parts[piece] * factor
                )[:seg_count]
        rows_ref[r, pl.ds(windows * seg_count, 1), :] = jnp.full((1, SEG), 1, jnp.float32) * (
            order[r] + 1
        ).astype(jnp.float32)
        out_ref[r] = rows_ref[r].astype(jnp.bfloat16)


def source_rows(offsets, samples_rows, scales, seg_count, windows):
    return pl.pallas_call(
        functools.partial(source_kernel, seg_count=seg_count, windows=windows),
        grid_spec=pltpu.PrefetchScalarGridSpec(
            num_scalar_prefetch=1,
            grid=(1,),
            in_specs=[
                pl.BlockSpec(memory_space=pl.ANY),
                pl.BlockSpec(scales.shape, lambda i, h: (0, 0)),
            ],
            out_specs=[
                pl.BlockSpec((SOURCES, SLOT, SEG), lambda i, h: (0, 0, 0)),
                pl.BlockSpec(memory_space=pltpu.SMEM),
            ],
            scratch_shapes=[
                pltpu.VMEM((SOURCES, 128, LANES), jnp.int32),
                pltpu.VMEM((SOURCES, SLOT, SEG), jnp.float32),
                pltpu.SemaphoreType.DMA((SOURCES,)),
            ],
        ),
        out_shape=[
            jax.ShapeDtypeStruct((SOURCES, SLOT, SEG), jnp.bfloat16),
            jax.ShapeDtypeStruct((2 * SOURCES,), jnp.int32),
        ],
        name="sources",
    )(offsets, samples_rows, scales)


def products(band_ref, sources, base, members, emit, g, row):
    src_ref, plus_ref, minus_ref = sources
    count = SEGMENTS
    lane = pl.multiple_of(g * PAIR, PAIR)
    real_lanes = pl.ds(lane, LANES)
    imag_lanes = pl.ds(pl.multiple_of(lane + LANES, LANES), LANES)
    zero = jnp.zeros((8, LANES), jnp.float32)
    acc = {(t, j): [zero, zero, zero] for t in range(SUB // 8) for j in members}
    for q in range(2 * count):
        band = []
        for t in range(SUB // 8):
            at = pl.ds(q * TILE + row + 8 * t, 8)
            g_re = band_ref[2 * g, at, :]
            g_im = band_ref[2 * g + 1, at, :]
            band.append((g_re, g_im, g_re + g_im))
        spot = q if q < count else SLOT + q - count
        for j in members:
            at = pl.ds(base + j * 2 * SLOT + spot, 8, stride=0)
            s_re = src_ref[g, at, :]
            s_plus = plus_ref[g, at, :]
            s_minus = minus_ref[g, at, :]
            for t in range(SUB // 8):
                g_re, g_im, g_sum = band[t]
                a = acc[t, j]
                a[0] = a[0] + s_re * g_sum
                a[1] = a[1] + s_minus * g_im
                a[2] = a[2] + s_plus * g_re
    for j in members:
        real = jnp.concatenate([acc[t, j][0] + acc[t, j][1] for t in range(SUB // 8)], axis=0)
        imag = jnp.concatenate([acc[t, j][0] - acc[t, j][2] for t in range(SUB // 8)], axis=0)
        emit(j, pl.ds(row, SUB), real_lanes, real)
        emit(j, pl.ds(row, SUB), imag_lanes, imag)


def outer_kernel(limits_ref, near_ref, far_ref, own_src_ref, above_src_ref, below_src_ref, table_ref,
                 up_ref, down_ref, band_ref, own_re_ref, own_plus_ref, own_minus_ref, src_ref, plus_ref, minus_ref):
    step = pl.program_id(0)
    count = near_ref.shape[0]
    groups = table_ref.shape[0]
    src_rows = 2 * SLOT
    per_side = SOURCES * src_rows

    @pl.when(step == 0)
    def _():
        scratch = (src_ref, plus_ref, minus_ref)
        for ref, base, into in (
            (own_src_ref, 0, (own_re_ref, own_plus_ref, own_minus_ref)),
            (above_src_ref, 0, scratch),
            (below_src_ref, per_side, scratch),
        ):
            rows = ref[...].reshape(per_side, SEG)
            at = pl.ds(base, per_side)
            for g in range(groups):
                spec = jnp.dot(rows, table_ref[g], preferred_element_type=jnp.float32)
                spec = spec.astype(jnp.bfloat16).astype(jnp.float32)
                real = spec[:, :LANES]
                imag = spec[:, LANES:]
                into[0][g, at, :] = real
                into[1][g, at, :] = real + imag
                into[2][g, at, :] = imag - real

    for part, ref in ((0, near_ref), (1, far_ref)):
        rows = ref[...].reshape(count * TILE, SEG)
        at = pl.ds(part * count * TILE, count * TILE)
        for g in range(groups):
            spec = jnp.dot(rows, table_ref[g], preferred_element_type=jnp.float32)
            spec = spec.astype(jnp.bfloat16).astype(jnp.float32)
            band_ref[2 * g, at, :] = spec[:, :LANES]
            band_ref[2 * g + 1, at, :] = spec[:, LANES:]

    def to_up(j, rows, lanes, value):
        up_ref[j, rows, lanes] = value.astype(up_ref.dtype)

    def to_down(j, rows, lanes, value):
        down_ref[j, rows, lanes] = value.astype(down_ref.dtype)

    def tile(index, carry):
        g = index // (TILE // SUB)
        row = pl.multiple_of((index % (TILE // SUB)) * SUB, SUB)
        channel = limits_ref[0] + step * TILE + row
        sources = (src_ref, plus_ref, minus_ref)
        for first in (0, 2):
            pair = (first, first + 1)
            at = 1 + first // 2

            @pl.when((channel + SUB > limits_ref[at]) & (channel < limits_ref[at + 2]))
            def _():
                products(band_ref, sources, 0, pair, to_up, g, row)

            @pl.when((channel + SUB > limits_ref[at + 4]) & (channel < limits_ref[at + 6]))
            def _():
                products(band_ref, sources, per_side, pair, to_down, g, row)

        return carry

    lax.fori_loop(0, groups * (TILE // SUB), tile, 0)


def own_kernel(ordered_ref, place_ref, band_ref, src_ref, plus_ref, minus_ref, first_ref, second_ref,
               kept_ref, passed_ref):
    groups = src_ref.shape[0]
    lower = place_ref[1] == 0
    base = place_ref[0] + pl.program_id(0) * TILE

    def tile(index, carry):
        g = index // (TILE // SUB)
        row = pl.multiple_of((index % (TILE // SUB)) * SUB, SUB)
        channel = base + row + lax.broadcasted_iota(jnp.int32, (SUB, LANES), 0)

        def emit(j, rows, lanes, value):
            below_source = jnp.where(channel < ordered_ref[j], 1, 0)
            first = first_ref[j, rows, lanes].astype(jnp.float32)
            second = second_ref[j, rows, lanes].astype(jnp.float32)
            other = jnp.where(below_source == place_ref[2], first, second)
            keep = below_source == jnp.where(lower, 1, 0)
            kept_ref[j, rows, lanes] = jnp.where(keep, value, other)
            passed_ref[j, rows, lanes] = jnp.where(keep, other, value).astype(jnp.bfloat16)

        for first in (0, 2):
            products(band_ref, (src_ref, plus_ref, minus_ref), 0, (first, first + 1), emit, g, row)
        return carry

    lax.fori_loop(0, groups * (TILE // SUB), tile, 0)


def outer_chunk(limits, near, far, own_src, above_src, below_src, table):
    count = near.shape[0]
    groups = table.shape[0]
    width = groups * PAIR
    per_side = SOURCES * 2 * SLOT
    steps = HALF // TILE
    band_rows = 2 * count * TILE
    block = pl.BlockSpec((count, TILE, SEG), lambda i, h: (0, i, 0))
    src = pl.BlockSpec((SOURCES, 2 * SLOT, SEG), lambda i, h: (0, 0, 0))
    result = pl.BlockSpec((SOURCES, TILE, width), lambda i, h: (0, i, 0))
    spectra = pl.BlockSpec((groups, per_side, LANES), lambda i, h: (0, 0, 0))
    returned = jax.ShapeDtypeStruct((SOURCES, HALF, width), jnp.bfloat16)
    own = jax.ShapeDtypeStruct((groups, per_side, LANES), jnp.float32)
    return pl.pallas_call(
        outer_kernel,
        grid_spec=pltpu.PrefetchScalarGridSpec(
            num_scalar_prefetch=1,
            grid=(steps,),
            in_specs=[block, block, src, src, src, pl.BlockSpec((groups, SEG, PAIR), lambda i, h: (0, 0, 0))],
            out_specs=[
                result,
                result,
                pl.BlockSpec((2 * groups, band_rows, LANES), lambda i, h: (0, i, 0)),
                spectra,
                spectra,
                spectra,
            ],
            scratch_shapes=[pltpu.VMEM((groups, 2 * per_side, LANES), jnp.float32)] * 3,
        ),
        out_shape=[
            returned,
            returned,
            jax.ShapeDtypeStruct((2 * groups, steps * band_rows, LANES), jnp.float32),
            own,
            own,
            own,
        ],
        name="outer",
    )(limits, near, far, own_src, above_src, below_src, table)


def own_chunk(ordered, place, band, src, plus, minus, from_first, from_second):
    groups, per_side, _ = src.shape
    steps = HALF // TILE
    width = groups * PAIR
    spectra = pl.BlockSpec((groups, per_side, LANES), lambda i, o, p: (0, 0, 0))
    rows = pl.BlockSpec((SOURCES, TILE, width), lambda i, o, p: (0, i, 0))
    return pl.pallas_call(
        own_kernel,
        grid_spec=pltpu.PrefetchScalarGridSpec(
            num_scalar_prefetch=2,
            grid=(steps,),
            in_specs=[
                pl.BlockSpec((2 * groups, band.shape[1] // steps, LANES), lambda i, o, p: (0, i, 0)),
                spectra,
                spectra,
                spectra,
                rows,
                rows,
            ],
            out_specs=[rows, rows],
        ),
        out_shape=[
            jax.ShapeDtypeStruct((SOURCES, HALF, width), jnp.float32),
            jax.ShapeDtypeStruct((SOURCES, HALF, width), jnp.bfloat16),
        ],
        name="own",
    )(ordered, place, band, src, plus, minus, from_first, from_second)


def turned(ordered_ref, mine_ref, mate_ref, top_ref, halve):
    source_row = lax.broadcasted_iota(jnp.int32, (HALF, 2 * HALF), 1)
    target_row = lax.broadcasted_iota(jnp.int32, (HALF, 2 * HALF), 0)
    for j in range(SOURCES):
        wanted = target_row + ordered_ref[j]
        wanted = jnp.where(wanted >= 2 * HALF, wanted - 2 * HALF, wanted)
        turn = jnp.where(source_row == wanted, 1.0, 0.0).astype(jnp.bfloat16)
        rows = jnp.concatenate([mine_ref[j], mate_ref[j]], axis=0)
        top_ref[pl.ds(j * HALF, HALF), :] = jnp.dot(turn, rows, preferred_element_type=jnp.float32).astype(
            jnp.bfloat16
        )
    if halve:
        lane = lax.broadcasted_iota(jnp.int32, (SOURCES * HALF, LANES), 1)
        first = top_ref[:, :LANES].astype(jnp.float32)
        top_ref[:, :LANES] = jnp.where(lane == 0, 0.5 * first, first).astype(jnp.bfloat16)


def folded(top_ref, hi_ref, lo_ref, first, sums):
    for g in range(hi_ref.shape[0]):
        rows = top_ref[:, g * PAIR:(g + 1) * PAIR]
        for table in (hi_ref[g], lo_ref[g]):
            part = lax.dot_general(rows, table, (((1,), (1,)), ((), ())), preferred_element_type=jnp.float32)
            parity = (first + g) % 2
            sums[parity] = part if sums[parity] is None else sums[parity] + part


def early_kernel(ordered_ref, *refs, firsts):
    count = len(firsts)
    even_ref, odd_ref = refs[4 * count:4 * count + 2]
    tops = refs[4 * count + 2:]

    @pl.when(pl.program_id(0) == 0)
    def _():
        for c, first in enumerate(firsts):
            turned(ordered_ref, refs[4 * c], refs[4 * c + 1], tops[c], first == 0)

    sums = [None, None]
    for c, first in enumerate(firsts):
        folded(tops[c], refs[4 * c + 2], refs[4 * c + 3], first, sums)
    even_ref[...] = sums[0]
    odd_ref[...] = sums[1]


def chunk_specs(groups):
    rows = pl.BlockSpec((SOURCES, HALF, groups * PAIR), lambda m, h: (0, 0, 0))
    table = pl.BlockSpec((groups, COLS, PAIR), lambda m, h: (0, m, 0))
    return [rows, rows, table, table]


def early_inverse(ordered, parts, firsts):
    specs, operands, tops = [], [], []
    for part in parts:
        groups = part[2].shape[0]
        specs += chunk_specs(groups)
        operands += list(part)
        tops.append(pltpu.VMEM((SOURCES * HALF, groups * PAIR), jnp.bfloat16))
    block = pl.BlockSpec((SOURCES * HALF, COLS), lambda m, h: (0, m))
    shape = jax.ShapeDtypeStruct((SOURCES * HALF, SEG), jnp.float32)
    return pl.pallas_call(
        functools.partial(early_kernel, firsts=firsts),
        grid_spec=pltpu.PrefetchScalarGridSpec(
            num_scalar_prefetch=1,
            grid=(SEG // COLS,),
            in_specs=specs,
            out_specs=[block, block],
            scratch_shapes=tops,
        ),
        out_shape=[shape, shape],
        name="early",
    )(ordered, *operands)


def last_kernel(ordered_ref, mine_ref, mate_ref, hi_ref, lo_ref, even_ref, odd_ref, out_ref, top_ref, stage_ref, sem,
                *, first, scale):
    m = pl.program_id(0)

    @pl.when(m == 0)
    def _():
        turned(ordered_ref, mine_ref, mate_ref, top_ref, first == 0)

    sums = [even_ref[...], odd_ref[...]]
    folded(top_ref, hi_ref, lo_ref, first, sums)
    stage_ref[m, 0] = (sums[0] - sums[1]) * scale
    stage_ref[m, 1] = (sums[0] + sums[1]) * scale

    def copy(step, side, j):
        lane = pl.multiple_of(side * SEG + step * COLS, COLS)
        return pltpu.make_async_copy(
            stage_ref.at[step, side, pl.ds(j * HALF, HALF), :],
            out_ref.at[ordered_ref[SOURCES + j], :, pl.ds(lane, COLS)],
            sem.at[step, side, j],
        )

    for side in range(2):
        for j in range(SOURCES):
            copy(m, side, j).start()

    @pl.when(m == pl.num_programs(0) - 1)
    def _():
        for step in range(SEG // COLS):
            for side in range(2):
                for j in range(SOURCES):
                    copy(step, side, j).wait()


def last_inverse(ordered, part, even, odd, first, scale):
    groups = part[2].shape[0]
    block = pl.BlockSpec((SOURCES * HALF, COLS), lambda m, h: (0, m))
    return pl.pallas_call(
        functools.partial(last_kernel, first=first, scale=scale),
        grid_spec=pltpu.PrefetchScalarGridSpec(
            num_scalar_prefetch=1,
            grid=(SEG // COLS,),
            in_specs=chunk_specs(groups) + [block, block],
            out_specs=pl.BlockSpec(memory_space=pl.ANY),
            scratch_shapes=[
                pltpu.VMEM((SOURCES * HALF, groups * PAIR), jnp.bfloat16),
                pltpu.VMEM((SEG // COLS, 2, SOURCES * HALF, COLS), jnp.float32),
                pltpu.SemaphoreType.DMA((SEG // COLS, 2, SOURCES)),
            ],
        ),
        out_shape=jax.ShapeDtypeStruct((SOURCES, HALF, 2 * SEG), jnp.float32),
        name="last",
    )(ordered, *part, even, odd)


def block_scale(exponents, alive):
    scale = jnp.zeros(exponents.shape, jnp.float32)
    for level in range(5):
        hit = (exponents == level) & (alive != 0)[:, None, None]
        scale = jnp.where(hit, float(2 ** level), scale)
    return scale


def swapped(block, first):
    route = []
    for low in range(first, lax.axis_size("chan") - 1, 2):
        route += [(low, low + 1), (low + 1, low)]
    return lax.ppermute(block, "chan", route)


def partner(block, bit):
    return lax.ppermute(block, "win", [(i, i ^ bit) for i in range(lax.axis_size("win"))])


def pipeline(samples, exponents, alive, offsets):
    channels, windows, length = samples.shape
    seg_count = length // SEG
    place = lax.axis_index("win")
    core = place & 1
    upper_half = place >> 1

    samples_rows = samples.reshape(channels, windows, length // LANES, LANES)
    samples_rows = samples_rows.transpose(0, 2, 1, 3).reshape(channels, windows * (length // LANES), LANES)
    scales = block_scale(exponents, alive).reshape(channels, -1)

    own_src, ordered = source_rows(offsets, samples_rows, scales, seg_count, windows)
    mate_src = partner(own_src, 1)
    own_src = jnp.concatenate([own_src, mate_src], axis=1)
    first_src = swapped(own_src, 0)
    second_src = swapped(own_src, 1)

    sent = normalize_half((1 - core).reshape(1), samples_rows, scales, seg_count, windows)
    far = partner(sent, 1)
    near = normalize_half(core.reshape(1), samples_rows, scales, seg_count, windows)
    coarse, fine = (jnp.asarray(t) for t in small_tables())

    flag = windows * seg_count
    even = lax.axis_index("chan") % 2 == 0
    bounds = []
    for src, is_above in ((first_src, even), (second_src, jnp.logical_not(even))):
        marks = src[:, flag, 0].astype(jnp.int32)
        near_pair = marks.reshape(SOURCES // 2, 2)
        present = near_pair[:, 0] > 0
        low = jnp.where(is_above, jnp.where(present, near_pair[:, 0] - 1, channels), 0)
        high = jnp.where(is_above, channels, near_pair[:, 1] - 1)
        bounds += [low, high]
    limits = jnp.concatenate([(core * HALF).reshape(1)] + bounds).astype(jnp.int32)
    where_am_i = jnp.stack([core * HALF, upper_half, even.astype(jnp.int32)]).astype(jnp.int32)
    scale = 2.0 / float(2 * SEG * windows * lax.axis_size("win") * seg_count * SEG)

    tables = []
    for first, count in CHUNKS:
        tables.append(make_tables(first, count, coarse, fine))
    returned, selected = [], []

    kept_spectra = []
    for c in range(len(CHUNKS)):
        to_first, to_second, *spectra = outer_chunk(limits, near, far, own_src, first_src, second_src, tables[c])
        kept_spectra.append(spectra)
        from_first = swapped(to_first, 0)
        from_second = swapped(to_second, 1)
        returned.append((from_first, from_second))
    for c in range(len(CHUNKS)):
        kept, moved = own_chunk(ordered, where_am_i, *kept_spectra[c], *returned[c])
        selected.append((kept, partner(moved, 2), moved))
    rests = []
    for c, (first, count) in enumerate(CHUNKS):
        later = lax.optimization_barrier((fine, selected[c][2]))[0]
        rests.append(make_tables(first, count, coarse, later, True))
    parts = []
    for c in range(len(CHUNKS)):
        kept, moved, _ = selected[c]
        if c:
            kept = lax.optimization_barrier((kept, parts[c - 1][0]))[0]
        total = (kept + moved.astype(jnp.float32)).astype(jnp.bfloat16)
        mate = partner(total, 1)
        parts.append((total, mate, tables[c], rests[c]))
    firsts = tuple(first for first, _ in CHUNKS)
    even, odd = early_inverse(ordered, parts[:-1], firsts[:-1])
    return last_inverse(ordered, parts[-1], even, odd, firsts[-1], scale)


def solution(mesh):
    placed = (P("chan", "win", None), P("chan", "win", None), P("chan"), P("chan"))
    return jax.shard_map(pipeline, mesh=mesh, in_specs=placed, out_specs=P("chan", "win", None), check_vma=False)
```

```python
import functools
import math

import jax
import jax.numpy as jnp
import numpy as np
from jax import lax
from jax.experimental import pallas as pl
from jax.experimental.pallas import tpu as pltpu
from jax.sharding import PartitionSpec as P


SEG = 1024
HALF = 96
LANES = 128
GROUPS = SEG // LANES
PAIR = 2 * LANES
CHUNKS = ((0, 5), (5, 3))
FOLD = 32
UNROLL = 4
TILE = 32
SUB = 16
PITCH = 104
SOURCES = 4
SLOT = 16
SEGMENTS = 12
COLS = 256


def small_tables():
    k = GROUPS * np.arange(LANES)[None, :] + np.arange(GROUPS)[:, None]
    step = np.arange(FOLD)

    def waves(stride):
        phase = (stride * step[None, :, None] * k[:, None, :]) % (2 * SEG)
        angle = phase * (2.0 * math.pi / (2 * SEG))
        return np.stack([np.cos(angle), np.sin(angle)], axis=1).astype(np.float32)

    return waves(FOLD), waves(1)


def table_kernel(coarse_ref, fine_ref, out_ref, *, rest):
    fine_cos = fine_ref[0, 0]
    fine_sin = fine_ref[0, 1]

    def row_block(step, carry):
        for inner in range(UNROLL):
            a = step * UNROLL + inner
            base_cos = coarse_ref[0, 0, pl.ds(a, 8, stride=0), :]
            base_sin = coarse_ref[0, 1, pl.ds(a, 8, stride=0), :]
            base_cos = jnp.concatenate([base_cos] * (FOLD // 8), axis=0)
            base_sin = jnp.concatenate([base_sin] * (FOLD // 8), axis=0)
            real = base_cos * fine_cos - base_sin * fine_sin
            imag = -(base_sin * fine_cos + base_cos * fine_sin)
            rows = pl.ds(pl.multiple_of(a * FOLD, FOLD), FOLD)
            for part, lane in ((real, 0), (imag, LANES)):
                top = part.astype(jnp.bfloat16)
                if rest:
                    top = (part - top.astype(jnp.float32)).astype(jnp.bfloat16)
                out_ref[0, rows, lane:lane + LANES] = top
        return carry

    lax.fori_loop(0, FOLD // UNROLL, row_block, 0)


def make_tables(first, count, coarse, fine, rest=False):
    shape = jax.ShapeDtypeStruct((count, SEG, PAIR), jnp.bfloat16)
    small = pl.BlockSpec((1, 2, FOLD, LANES), lambda p: (first + p, 0, 0, 0))
    large = pl.BlockSpec((1, SEG, PAIR), lambda p: (p, 0, 0))
    return pl.pallas_call(
        functools.partial(table_kernel, rest=rest),
        grid=(count,),
        in_specs=[small, small],
        out_specs=large,
        out_shape=shape,
        name="tables",
    )(coarse, fine)


def normalize_kernel(half_ref, samples_ref, scale_ref, out_ref, buffer_ref, spread_ref, wide_ref, sems, *,
                     seg_count, windows):
    step = pl.program_id(0)
    steps = pl.num_programs(0)
    per_channel = samples_ref.shape[1]
    pieces = SEG // LANES
    pairs = pieces // 2
    blocks = seg_count * pairs
    slot = step % 2

    def copy(at, into):
        first = half_ref[0] * HALF + at * TILE
        return pltpu.make_async_copy(
            samples_ref.at[pl.ds(first, TILE)],
            buffer_ref.at[into, :, pl.ds(0, per_channel), :],
            sems.at[into],
        )

    @pl.when(step == 0)
    def _():
        copy(0, 0).start()

    @pl.when(step + 1 < steps)
    def _():
        copy(step + 1, 1 - slot).start()

    columns = wide_ref.shape[0]

    @pl.when(step == 0)
    def _():
        for column in range(columns):
            row = lax.broadcasted_iota(jnp.int32, (columns, LANES), 0)
            spread_ref[:, column * LANES:(column + 1) * LANES] = jnp.where(row == column, 1.0, 0.0).astype(jnp.bfloat16)

    scale = scale_ref[...]
    narrow = scale.astype(jnp.bfloat16)
    for column in range(0, columns, 2):
        both = jnp.dot(
            narrow, spread_ref[:, column * LANES:(column + 2) * LANES], preferred_element_type=jnp.float32
        )
        wide_ref[column] = both[:, :LANES]
        wide_ref[column + 1] = both[:, LANES:]

    copy(step, slot).wait()
    flat = buffer_ref.reshape(2 * TILE * PITCH, LANES)
    base = slot * (TILE * PITCH)

    def rows(w, n, piece):
        start = base + (n * pieces + piece) * windows + w
        return flat[pl.ds(start, TILE, stride=PITCH), :].astype(jnp.float32)

    for w in range(windows):
        total = jnp.zeros((TILE, LANES), jnp.float32)
        for n in range(seg_count):
            for pair in range(pairs):
                column = w * blocks + n * pairs + pair
                one = rows(w, n, 2 * pair)
                two = rows(w, n, 2 * pair + 1)
                weight = wide_ref[column]
                total = total + (one * one + two * two) * (weight * weight)
        energy = jnp.sum(total, axis=1, keepdims=True) * (1.0 / (seg_count * SEG))
        factor = jnp.broadcast_to(lax.rsqrt(energy + 1e-06), (TILE, LANES))
        for n in range(seg_count):
            for pair in range(pairs):
                column = w * blocks + n * pairs + pair
                weight = wide_ref[column] * factor
                for piece in (2 * pair, 2 * pair + 1):
                    value = rows(w, n, piece) * weight
                    out_ref[w * seg_count + n, :, piece * LANES:(piece + 1) * LANES] = value.astype(jnp.bfloat16)


def normalize_half(half, samples_rows, scales, seg_count, windows):
    steps = HALF // TILE
    return pl.pallas_call(
        functools.partial(normalize_kernel, seg_count=seg_count, windows=windows),
        grid_spec=pltpu.PrefetchScalarGridSpec(
            num_scalar_prefetch=1,
            grid=(steps,),
            in_specs=[
                pl.BlockSpec(memory_space=pl.ANY),
                pl.BlockSpec((TILE, scales.shape[1]), lambda i, h: (h[0] * steps + i, 0)),
            ],
            out_specs=pl.BlockSpec((windows * seg_count, TILE, SEG), lambda i, h: (0, i, 0)),
            scratch_shapes=[
                pltpu.VMEM((2, TILE, PITCH, LANES), jnp.int32),
                pltpu.VMEM((scales.shape[1], scales.shape[1] * LANES), jnp.bfloat16),
                pltpu.VMEM((scales.shape[1], TILE, LANES), jnp.float32),
                pltpu.SemaphoreType.DMA((2,)),
            ],
        ),
        out_shape=jax.ShapeDtypeStruct((windows * seg_count, HALF, SEG), jnp.bfloat16),
        name="normalize",
    )(half, samples_rows, scales)


def source_kernel(offsets_ref, samples_ref, scale_ref, out_ref, sorted_ref, buffer_ref, rows_ref, sems, *,
                  seg_count, windows):
    pieces = SEG // LANES
    pairs = pieces // 2
    blocks = seg_count * pairs
    per_channel = samples_ref.shape[1]
    given = [offsets_ref[j] for j in range(SOURCES)]
    ranks = []
    for j in range(SOURCES):
        rank = jnp.int32(0)
        for i in range(SOURCES):
            if i != j:
                ahead = given[i] <= given[j] if i < j else given[i] < given[j]
                rank = rank + jnp.where(ahead, 1, 0)
        ranks.append(rank)
    order = []
    for r in range(SOURCES):
        offset = jnp.int32(0)
        origin = jnp.int32(0)
        for j in range(SOURCES):
            hit = ranks[j] == r
            offset = jnp.where(hit, given[j], offset)
            origin = jnp.where(hit, j, origin)
        sorted_ref[r] = offset
        sorted_ref[SOURCES + r] = origin
        order.append(offset)
    copies = []
    for r in range(SOURCES):
        copy = pltpu.make_async_copy(
            samples_ref.at[order[r]], buffer_ref.at[r, pl.ds(0, per_channel), :], sems.at[r]
        )
        copy.start()
        copies.append(copy)
    channel = lax.broadcasted_iota(jnp.int32, scale_ref.shape, 0)
    lane = lax.broadcasted_iota(jnp.int32, (8, scale_ref.shape[1]), 1)
    segment = lax.broadcasted_iota(jnp.int32, (8, scale_ref.shape[1]), 0)
    valid = lax.broadcasted_iota(jnp.int32, (8, LANES), 0) < seg_count
    rows_ref[...] = jnp.zeros(rows_ref.shape, jnp.float32)
    for r in range(SOURCES):
        picked = jnp.sum(jnp.where(channel == order[r], scale_ref[...], 0.0), axis=0, keepdims=True)
        picked = jnp.broadcast_to(picked, (8, scale_ref.shape[1]))
        copies[r].wait()
        for w in range(windows):
            parts = []
            total = jnp.zeros((8, LANES), jnp.float32)
            for pair in range(pairs):
                column = w * blocks + segment * pairs + pair
                weight = jnp.sum(jnp.where(lane == column, picked, 0.0), axis=1, keepdims=True)
                for piece in (2 * pair, 2 * pair + 1):
                    raw = buffer_ref[r, pl.ds(piece * windows + w, 8, stride=pieces * windows), :]
                    part = jnp.where(valid, raw.astype(jnp.float32), 0.0) * weight
                    total = total + part * part
                    parts.append(part)
            energy = jnp.sum(jnp.sum(total, axis=1, keepdims=True), axis=0, keepdims=True)
            factor = lax.rsqrt(energy * (1.0 / (seg_count * SEG)) + 1e-06)
            for piece in range(pieces):
                rows_ref[r, pl.ds(w * seg_count, seg_count), piece * LANES:(piece + 1) * LANES] = (
                    parts[piece] * factor
                )[:seg_count]
        rows_ref[r, pl.ds(windows * seg_count, 1), :] = jnp.full((1, SEG), 1, jnp.float32) * (
            order[r] + 1
        ).astype(jnp.float32)
        out_ref[r] = rows_ref[r].astype(jnp.bfloat16)


def source_rows(offsets, samples_rows, scales, seg_count, windows):
    return pl.pallas_call(
        functools.partial(source_kernel, seg_count=seg_count, windows=windows),
        grid_spec=pltpu.PrefetchScalarGridSpec(
            num_scalar_prefetch=1,
            grid=(1,),
            in_specs=[
                pl.BlockSpec(memory_space=pl.ANY),
                pl.BlockSpec(scales.shape, lambda i, h: (0, 0)),
            ],
            out_specs=[
                pl.BlockSpec((SOURCES, SLOT, SEG), lambda i, h: (0, 0, 0)),
                pl.BlockSpec(memory_space=pltpu.SMEM),
            ],
            scratch_shapes=[
                pltpu.VMEM((SOURCES, 128, LANES), jnp.int32),
                pltpu.VMEM((SOURCES, SLOT, SEG), jnp.float32),
                pltpu.SemaphoreType.DMA((SOURCES,)),
            ],
        ),
        out_shape=[
            jax.ShapeDtypeStruct((SOURCES, SLOT, SEG), jnp.bfloat16),
            jax.ShapeDtypeStruct((2 * SOURCES,), jnp.int32),
        ],
        name="sources",
    )(offsets, samples_rows, scales)


def products(band_ref, sources, base, members, emit, g, row):
    src_ref, plus_ref, minus_ref = sources
    count = SEGMENTS
    lane = pl.multiple_of(g * PAIR, PAIR)
    real_lanes = pl.ds(lane, LANES)
    imag_lanes = pl.ds(pl.multiple_of(lane + LANES, LANES), LANES)
    zero = jnp.zeros((8, LANES), jnp.float32)
    acc = {(t, j): [zero, zero, zero] for t in range(SUB // 8) for j in members}
    for q in range(2 * count):
        band = []
        for t in range(SUB // 8):
            at = pl.ds(q * TILE + row + 8 * t, 8)
            g_re = band_ref[2 * g, at, :]
            g_im = band_ref[2 * g + 1, at, :]
            band.append((g_re, g_im, g_re + g_im))
        spot = q if q < count else SLOT + q - count
        for j in members:
            at = pl.ds(base + j * 2 * SLOT + spot, 8, stride=0)
            s_re = src_ref[g, at, :]
            s_plus = plus_ref[g, at, :]
            s_minus = minus_ref[g, at, :]
            for t in range(SUB // 8):
                g_re, g_im, g_sum = band[t]
                a = acc[t, j]
                a[0] = a[0] + s_re * g_sum
                a[1] = a[1] + s_minus * g_im
                a[2] = a[2] + s_plus * g_re
    for j in members:
        real = jnp.concatenate([acc[t, j][0] + acc[t, j][1] for t in range(SUB // 8)], axis=0)
        imag = jnp.concatenate([acc[t, j][0] - acc[t, j][2] for t in range(SUB // 8)], axis=0)
        emit(j, pl.ds(row, SUB), real_lanes, real)
        emit(j, pl.ds(row, SUB), imag_lanes, imag)


def outer_kernel(limits_ref, near_ref, far_ref, own_src_ref, above_src_ref, below_src_ref, table_ref,
                 up_ref, down_ref, band_ref, own_re_ref, own_plus_ref, own_minus_ref, src_ref, plus_ref, minus_ref):
    step = pl.program_id(0)
    count = near_ref.shape[0]
    groups = table_ref.shape[0]
    src_rows = 2 * SLOT
    per_side = SOURCES * src_rows

    @pl.when(step == 0)
    def _():
        scratch = (src_ref, plus_ref, minus_ref)
        for ref, base, into in (
            (own_src_ref, 0, (own_re_ref, own_plus_ref, own_minus_ref)),
            (above_src_ref, 0, scratch),
            (below_src_ref, per_side, scratch),
        ):
            rows = ref[...].reshape(per_side, SEG)
            at = pl.ds(base, per_side)
            for g in range(groups):
                spec = jnp.dot(rows, table_ref[g], preferred_element_type=jnp.float32)
                spec = spec.astype(jnp.bfloat16).astype(jnp.float32)
                real = spec[:, :LANES]
                imag = spec[:, LANES:]
                into[0][g, at, :] = real
                into[1][g, at, :] = real + imag
                into[2][g, at, :] = imag - real

    for part, ref in ((0, near_ref), (1, far_ref)):
        rows = ref[...].reshape(count * TILE, SEG)
        at = pl.ds(part * count * TILE, count * TILE)
        for g in range(groups):
            spec = jnp.dot(rows, table_ref[g], preferred_element_type=jnp.float32)
            spec = spec.astype(jnp.bfloat16).astype(jnp.float32)
            band_ref[2 * g, at, :] = spec[:, :LANES]
            band_ref[2 * g + 1, at, :] = spec[:, LANES:]

    def to_up(j, rows, lanes, value):
        up_ref[j, rows, lanes] = value.astype(up_ref.dtype)

    def to_down(j, rows, lanes, value):
        down_ref[j, rows, lanes] = value.astype(down_ref.dtype)

    def tile(index, carry):
        g = index // (TILE // SUB)
        row = pl.multiple_of((index % (TILE // SUB)) * SUB, SUB)
        channel = limits_ref[0] + step * TILE + row
        sources = (src_ref, plus_ref, minus_ref)
        for first in (0, 2):
            pair = (first, first + 1)
            at = 1 + first // 2

            @pl.when((channel + SUB > limits_ref[at]) & (channel < limits_ref[at + 2]))
            def _():
                products(band_ref, sources, 0, pair, to_up, g, row)

            @pl.when((channel + SUB > limits_ref[at + 4]) & (channel < limits_ref[at + 6]))
            def _():
                products(band_ref, sources, per_side, pair, to_down, g, row)

        return carry

    lax.fori_loop(0, groups * (TILE // SUB), tile, 0)


def own_kernel(ordered_ref, place_ref, band_ref, src_ref, plus_ref, minus_ref, first_ref, second_ref,
               kept_ref, passed_ref):
    groups = src_ref.shape[0]
    lower = place_ref[1] == 0
    base = place_ref[0] + pl.program_id(0) * TILE

    def tile(index, carry):
        g = index // (TILE // SUB)
        row = pl.multiple_of((index % (TILE // SUB)) * SUB, SUB)
        channel = base + row + lax.broadcasted_iota(jnp.int32, (SUB, LANES), 0)

        def emit(j, rows, lanes, value):
            below_source = jnp.where(channel < ordered_ref[j], 1, 0)
            first = first_ref[j, rows, lanes].astype(jnp.float32)
            second = second_ref[j, rows, lanes].astype(jnp.float32)
            other = jnp.where(below_source == place_ref[2], first, second)
            keep = below_source == jnp.where(lower, 1, 0)
            kept_ref[j, rows, lanes] = jnp.where(keep, value, other)
            passed_ref[j, rows, lanes] = jnp.where(keep, other, value).astype(jnp.bfloat16)

        for first in (0, 2):
            products(band_ref, (src_ref, plus_ref, minus_ref), 0, (first, first + 1), emit, g, row)
        return carry

    lax.fori_loop(0, groups * (TILE // SUB), tile, 0)


def outer_chunk(limits, near, far, own_src, above_src, below_src, table):
    count = near.shape[0]
    groups = table.shape[0]
    width = groups * PAIR
    per_side = SOURCES * 2 * SLOT
    steps = HALF // TILE
    band_rows = 2 * count * TILE
    block = pl.BlockSpec((count, TILE, SEG), lambda i, h: (0, i, 0))
    src = pl.BlockSpec((SOURCES, 2 * SLOT, SEG), lambda i, h: (0, 0, 0))
    result = pl.BlockSpec((SOURCES, TILE, width), lambda i, h: (0, i, 0))
    spectra = pl.BlockSpec((groups, per_side, LANES), lambda i, h: (0, 0, 0))
    returned = jax.ShapeDtypeStruct((SOURCES, HALF, width), jnp.bfloat16)
    own = jax.ShapeDtypeStruct((groups, per_side, LANES), jnp.float32)
    return pl.pallas_call(
        outer_kernel,
        grid_spec=pltpu.PrefetchScalarGridSpec(
            num_scalar_prefetch=1,
            grid=(steps,),
            in_specs=[block, block, src, src, src, pl.BlockSpec((groups, SEG, PAIR), lambda i, h: (0, 0, 0))],
            out_specs=[
                result,
                result,
                pl.BlockSpec((2 * groups, band_rows, LANES), lambda i, h: (0, i, 0)),
                spectra,
                spectra,
                spectra,
            ],
            scratch_shapes=[pltpu.VMEM((groups, 2 * per_side, LANES), jnp.float32)] * 3,
        ),
        out_shape=[
            returned,
            returned,
            jax.ShapeDtypeStruct((2 * groups, steps * band_rows, LANES), jnp.float32),
            own,
            own,
            own,
        ],
        name="outer",
    )(limits, near, far, own_src, above_src, below_src, table)


def own_chunk(ordered, place, band, src, plus, minus, from_first, from_second):
    groups, per_side, _ = src.shape
    steps = HALF // TILE
    width = groups * PAIR
    spectra = pl.BlockSpec((groups, per_side, LANES), lambda i, o, p: (0, 0, 0))
    rows = pl.BlockSpec((SOURCES, TILE, width), lambda i, o, p: (0, i, 0))
    return pl.pallas_call(
        own_kernel,
        grid_spec=pltpu.PrefetchScalarGridSpec(
            num_scalar_prefetch=2,
            grid=(steps,),
            in_specs=[
                pl.BlockSpec((2 * groups, band.shape[1] // steps, LANES), lambda i, o, p: (0, i, 0)),
                spectra,
                spectra,
                spectra,
                rows,
                rows,
            ],
            out_specs=[rows, rows],
        ),
        out_shape=[
            jax.ShapeDtypeStruct((SOURCES, HALF, width), jnp.float32),
            jax.ShapeDtypeStruct((SOURCES, HALF, width), jnp.bfloat16),
        ],
        name="own",
    )(ordered, place, band, src, plus, minus, from_first, from_second)


def turned(ordered_ref, mine_ref, mate_ref, top_ref, halve):
    source_row = lax.broadcasted_iota(jnp.int32, (HALF, 2 * HALF), 1)
    target_row = lax.broadcasted_iota(jnp.int32, (HALF, 2 * HALF), 0)
    for j in range(SOURCES):
        wanted = target_row + ordered_ref[j]
        wanted = jnp.where(wanted >= 2 * HALF, wanted - 2 * HALF, wanted)
        turn = jnp.where(source_row == wanted, 1.0, 0.0).astype(jnp.bfloat16)
        rows = jnp.concatenate([mine_ref[j], mate_ref[j]], axis=0)
        top_ref[pl.ds(j * HALF, HALF), :] = jnp.dot(turn, rows, preferred_element_type=jnp.float32).astype(
            jnp.bfloat16
        )
    if halve:
        lane = lax.broadcasted_iota(jnp.int32, (SOURCES * HALF, LANES), 1)
        first = top_ref[:, :LANES].astype(jnp.float32)
        top_ref[:, :LANES] = jnp.where(lane == 0, 0.5 * first, first).astype(jnp.bfloat16)


def folded(top_ref, hi_ref, lo_ref, first, sums):
    for g in range(hi_ref.shape[0]):
        rows = top_ref[:, g * PAIR:(g + 1) * PAIR]
        for table in (hi_ref[g], lo_ref[g]):
            part = lax.dot_general(rows, table, (((1,), (1,)), ((), ())), preferred_element_type=jnp.float32)
            parity = (first + g) % 2
            sums[parity] = part if sums[parity] is None else sums[parity] + part


def early_kernel(ordered_ref, *refs, firsts):
    count = len(firsts)
    even_ref, odd_ref = refs[4 * count:4 * count + 2]
    tops = refs[4 * count + 2:]

    @pl.when(pl.program_id(0) == 0)
    def _():
        for c, first in enumerate(firsts):
            turned(ordered_ref, refs[4 * c], refs[4 * c + 1], tops[c], first == 0)

    sums = [None, None]
    for c, first in enumerate(firsts):
        folded(tops[c], refs[4 * c + 2], refs[4 * c + 3], first, sums)
    even_ref[...] = sums[0]
    odd_ref[...] = sums[1]


def chunk_specs(groups):
    rows = pl.BlockSpec((SOURCES, HALF, groups * PAIR), lambda m, h: (0, 0, 0))
    table = pl.BlockSpec((groups, COLS, PAIR), lambda m, h: (0, m, 0))
    return [rows, rows, table, table]


def early_inverse(ordered, parts, firsts):
    specs, operands, tops = [], [], []
    for part in parts:
        groups = part[2].shape[0]
        specs += chunk_specs(groups)
        operands += list(part)
        tops.append(pltpu.VMEM((SOURCES * HALF, groups * PAIR), jnp.bfloat16))
    block = pl.BlockSpec((SOURCES * HALF, COLS), lambda m, h: (0, m))
    shape = jax.ShapeDtypeStruct((SOURCES * HALF, SEG), jnp.float32)
    return pl.pallas_call(
        functools.partial(early_kernel, firsts=firsts),
        grid_spec=pltpu.PrefetchScalarGridSpec(
            num_scalar_prefetch=1,
            grid=(SEG // COLS,),
            in_specs=specs,
            out_specs=[block, block],
            scratch_shapes=tops,
        ),
        out_shape=[shape, shape],
        name="early",
    )(ordered, *operands)


def last_kernel(ordered_ref, mine_ref, mate_ref, hi_ref, lo_ref, even_ref, odd_ref, out_ref, top_ref, stage_ref, sem,
                *, first, scale):
    m = pl.program_id(0)

    @pl.when(m == 0)
    def _():
        turned(ordered_ref, mine_ref, mate_ref, top_ref, first == 0)

    sums = [even_ref[...], odd_ref[...]]
    folded(top_ref, hi_ref, lo_ref, first, sums)
    stage_ref[m, 0] = (sums[0] - sums[1]) * scale
    stage_ref[m, 1] = (sums[0] + sums[1]) * scale

    def copy(step, side, j):
        lane = pl.multiple_of(side * SEG + step * COLS, COLS)
        return pltpu.make_async_copy(
            stage_ref.at[step, side, pl.ds(j * HALF, HALF), :],
            out_ref.at[ordered_ref[SOURCES + j], :, pl.ds(lane, COLS)],
            sem.at[step, side, j],
        )

    for side in range(2):
        for j in range(SOURCES):
            copy(m, side, j).start()

    @pl.when(m == pl.num_programs(0) - 1)
    def _():
        for step in range(SEG // COLS):
            for side in range(2):
                for j in range(SOURCES):
                    copy(step, side, j).wait()


def last_inverse(ordered, part, even, odd, first, scale):
    groups = part[2].shape[0]
    block = pl.BlockSpec((SOURCES * HALF, COLS), lambda m, h: (0, m))
    return pl.pallas_call(
        functools.partial(last_kernel, first=first, scale=scale),
        grid_spec=pltpu.PrefetchScalarGridSpec(
            num_scalar_prefetch=1,
            grid=(SEG // COLS,),
            in_specs=chunk_specs(groups) + [block, block],
            out_specs=pl.BlockSpec(memory_space=pl.ANY),
            scratch_shapes=[
                pltpu.VMEM((SOURCES * HALF, groups * PAIR), jnp.bfloat16),
                pltpu.VMEM((SEG // COLS, 2, SOURCES * HALF, COLS), jnp.float32),
                pltpu.SemaphoreType.DMA((SEG // COLS, 2, SOURCES)),
            ],
        ),
        out_shape=jax.ShapeDtypeStruct((SOURCES, HALF, 2 * SEG), jnp.float32),
        name="last",
    )(ordered, *part, even, odd)


def block_scale(exponents, alive):
    scale = jnp.zeros(exponents.shape, jnp.float32)
    for level in range(5):
        hit = (exponents == level) & (alive != 0)[:, None, None]
        scale = jnp.where(hit, float(2 ** level), scale)
    return scale


def swapped(block, first):
    route = []
    for low in range(first, lax.axis_size("chan") - 1, 2):
        route += [(low, low + 1), (low + 1, low)]
    return lax.ppermute(block, "chan", route)


def partner(block, bit):
    return lax.ppermute(block, "win", [(i, i ^ bit) for i in range(lax.axis_size("win"))])


def pipeline(samples, exponents, alive, offsets):
    channels, windows, length = samples.shape
    seg_count = length // SEG
    place = lax.axis_index("win")
    core = place & 1
    upper_half = place >> 1

    samples_rows = samples.reshape(channels, windows, length // LANES, LANES)
    samples_rows = samples_rows.transpose(0, 2, 1, 3).reshape(channels, windows * (length // LANES), LANES)
    scales = block_scale(exponents, alive).reshape(channels, -1)

    own_src, ordered = source_rows(offsets, samples_rows, scales, seg_count, windows)
    mate_src = partner(own_src, 1)
    own_src = jnp.concatenate([own_src, mate_src], axis=1)
    first_src = swapped(own_src, 0)
    second_src = swapped(own_src, 1)

    sent = normalize_half((1 - core).reshape(1), samples_rows, scales, seg_count, windows)
    far = partner(sent, 1)
    near = normalize_half(core.reshape(1), samples_rows, scales, seg_count, windows)
    coarse, fine = (jnp.asarray(t) for t in small_tables())

    flag = windows * seg_count
    even = lax.axis_index("chan") % 2 == 0
    bounds = []
    for src, is_above in ((first_src, even), (second_src, jnp.logical_not(even))):
        marks = src[:, flag, 0].astype(jnp.int32)
        near_pair = marks.reshape(SOURCES // 2, 2)
        present = near_pair[:, 0] > 0
        low = jnp.where(is_above, jnp.where(present, near_pair[:, 0] - 1, channels), 0)
        high = jnp.where(is_above, channels, near_pair[:, 1] - 1)
        bounds += [low, high]
    limits = jnp.concatenate([(core * HALF).reshape(1)] + bounds).astype(jnp.int32)
    where_am_i = jnp.stack([core * HALF, upper_half, even.astype(jnp.int32)]).astype(jnp.int32)
    scale = 2.0 / float(2 * SEG * windows * lax.axis_size("win") * seg_count * SEG)

    tables = []
    for first, count in CHUNKS:
        tables.append(make_tables(first, count, coarse, fine))
    returned, selected = [], []

    kept_spectra = []
    for c in range(len(CHUNKS)):
        to_first, to_second, *spectra = outer_chunk(limits, near, far, own_src, first_src, second_src, tables[c])
        kept_spectra.append(spectra)
        from_first = swapped(to_first, 0)
        from_second = swapped(to_second, 1)
        returned.append((from_first, from_second))
    for c in range(len(CHUNKS)):
        kept, moved = own_chunk(ordered, where_am_i, *kept_spectra[c], *returned[c])
        selected.append((kept, partner(moved, 2), moved))
    rests = []
    for first, count in CHUNKS:
        later = lax.optimization_barrier((fine, selected[-1][2]))[0]
        rests.append(make_tables(first, count, coarse, later, True))
    parts = []
    for c in range(len(CHUNKS)):
        kept, moved, _ = selected[c]
        if c:
            kept = lax.optimization_barrier((kept, parts[c - 1][0]))[0]
        total = (kept + moved.astype(jnp.float32)).astype(jnp.bfloat16)
        mate = partner(total, 1)
        parts.append((total, mate, tables[c], rests[c]))
    firsts = tuple(first for first, _ in CHUNKS)
    even, odd = early_inverse(ordered, parts[:-1], firsts[:-1])
    return last_inverse(ordered, parts[-1], even, odd, firsts[-1], scale)


def solution(mesh):
    placed = (P("chan", "win", None), P("chan", "win", None), P("chan"), P("chan"))
    return jax.shard_map(pipeline, mesh=mesh, in_specs=placed, out_specs=P("chan", "win", None), check_vma=False)
```
